256 devices in a mesh: cols: 32 (over y, z), mem: 8 (over x, core).
Axes of the slice: x: 4, y: 4, z: 8, core: 2. Of those that a mesh axis runs over, the one named last changes fastest.
Arguments:
- state: float32 [80, 1048576], P('mem', 'cols'), may hold values from -6 to 6
- obs_value: float32 [4, 1024], P(None, 'cols'), may hold values from -6 to 6
- obs_var: float32 [4, 1024], P(None, 'cols'), may hold values from 0.2 to 2
- owner: int32 [4, 1024, 1], P(None, 'cols'), may hold values from 0 to 31; in each aligned block of 32 rows (0 to 31, 32 to 63, ..., all dimensions but the last counted through in order) at most 2 rows name the same one
- tile_of: int32 [4, 1024], P(None, 'cols'), may hold values from 0 to 63
- offsets: int32 [4, 1024, 4], P(None, 'cols'), may hold values from 0 to 511
- accept: int32 [4, 1024], P(None, 'cols'), may hold values 0 or 1
- loc_mask: int32 [2048, 4, 8], P(('cols', 'mem')), may hold values 0 or 1
Outputs:
- posterior: float32 [80, 1048576], P(None, ('cols', 'mem'))
The draws below stay inside these ranges and needn't reach their ends.
Inputs may be any that keep to these rules, and one draw needn't show every extreme that they name: Within the 32 observations of one batch held by one index of cols, no owner is named more than 2 times, and that many is reached.
All inputs are finite; a program needn't handle non-finite values. No bound on the sum of `accept` or of `loc_mask` on one device may be relied on, other than what follows from the above.
Results may differ from the reference program's by a relative error of at most 0.0002.
Values sent between devices are 32-bit elements; how exact they have to be, the bound alone decides.
A program may use at most 64 MiB of HBM per device.

```python
import math
import jax
import jax.numpy as jnp
import numpy as np
from jax import lax

M = 80
NS_DEV = 32768
NB = 4
KB = 1024
P_SIZE = 4
TILE = 512
OBLK = 128
NS = 1048576
KS = 32
SCAP = 2
TPS = 64
NTILES = 2048
NBLK = 8
N_COLS = 32


def set_ends(entries, rng, low, top_value):
    longest = entries.shape.index(max(entries.shape))
    spots = []
    for shift in (0, 1):
        where = [jax.random.randint(jax.random.fold_in(rng, axis), (), 0, length) for axis, length in enumerate(entries.shape)]
        where[longest] = (where[longest] + shift) % entries.shape[longest]
        spots.append(tuple(where))
    return entries.at[spots[0]].set(low).at[spots[1]].set(top_value)


def level_of(stream_key, dims, cuts, smallest, high):
    def one(dim, parts):
        steps = jax.random.uniform(jax.random.fold_in(jax.random.fold_in(stream_key, 6), dim), (parts,), jnp.float32, smallest / len(cuts), high / len(cuts))
        return jnp.repeat(jnp.exp(steps), dims[dim] // parts).reshape((-1,) + (1,) * (len(dims) - dim - 1))

    loudness = one(*cuts[0])
    for cut in cuts[1:]:
        loudness = loudness * one(*cut)
    return loudness


def shared_out(stream_key, own, number, rows, amount, top, bound, slope):
    sequence = jax.random.permutation(stream_key, amount)
    crowded, common = portions_of(amount, rows * top, bound, slope, True), portions_of(amount, rows * top, bound, slope, False)
    places = jnp.arange(amount)

    def named(lengths, offset_by):
        used = int((lengths > 0).sum())
        fixed = max(1, used // 4)
        moved = fixed + (places - fixed + offset_by * (used - fixed)) % max(1, amount - fixed)
        return jnp.zeros((amount,), jnp.int32).at[sequence[jnp.where(places < fixed, places, moved)]].set(jnp.asarray(lengths, jnp.int32))

    lengths = jnp.where(number % 4 == 0, named(crowded, number // 4), named(common, number - number // 4 - 1))
    mixed = jax.random.permutation(jax.random.fold_in(own, 3), amount)
    donor, sink = mixed[0:amount // 2 * 2:2], mixed[1:amount // 2 * 2:2]
    room = jnp.minimum(lengths[donor] - 1, bound - lengths[sink]) // 2
    room = jnp.where((donor == sequence[0]) | (sink == sequence[0]) | (lengths[sink] == 0), 0, jnp.maximum(room, 0))
    moved = jax.random.randint(jax.random.fold_in(own, 4), (amount // 2,), 0, 1 << 20) % (room + 1)
    lengths = lengths.at[donor].add(-moved).at[sink].add(moved)
    items = jnp.searchsorted(jnp.cumsum(lengths), jnp.arange(rows * top), side="right").astype(jnp.int32)
    listing = items.reshape(top, rows).T
    listing = listing[jax.random.permutation(jax.random.fold_in(own, 1), rows)]
    offset_by = jax.random.randint(jax.random.fold_in(own, 2), (rows, 1), 0, top)
    return jnp.take_along_axis(listing, (jnp.arange(top)[None, :] + offset_by) % top, axis=1)


def portions_of(count, total, limit, lean, full):
    portions = [(1 << 20) // math.isqrt(standing ** lean) + 1 for standing in range(1, count + 1)]
    largest = limit if full else min(limit, max(-(-total // count), total * portions[0] // sum(portions)))
    least = 1 if total - largest >= count - 1 else 0
    given, rest = [largest] + [least] * (count - 1), total - largest - least * (count - 1)
    while rest > 0:
        candidates = [i for i in range(1, count) if given[i] < largest] or [i for i in range(1, count) if given[i] < limit]
        mass, budget = sum([portions[i] for i in candidates]), rest
        for i in candidates:
            more = min(limit - given[i], max(1, budget * portions[i] // mass), rest)
            given[i] = given[i] + more
            rest = rest - more
    return np.array(given)


def scatter_about(own_key, shape, width, limit, shards=(), kind=jnp.bfloat16):
    result = jax.random.normal(own_key, shape, jnp.float32) * width
    if len(shards) > 0:
        result = level_of(own_key, shape, shards, -0.22, 0.18) * result
    return jnp.clip(result, min=-limit, max=limit).astype(kind)


def setup_inputs(seed: int = 0) -> dict:
    arg_keys = jax.random.split(jax.random.key(seed), 9)
    state = scatter_about(arg_keys[0], (M, NS), 1.0, 6.0, ((0, 8), (1, 32)), jnp.float32)
    obs_value = scatter_about(arg_keys[1], (NB, KB), 1.0, 6.0, ((1, 32),), jnp.float32)
    obs_var = jnp.clip(jnp.exp(math.log(2.0) - 2.3025851 * jax.random.uniform(arg_keys[2], (NB, KB), jnp.float32) ** level_of(arg_keys[2], (NB, KB), ((1, 32),), -0.2, 0.2)), 0.2, 2.0)
    owner_keys = jax.random.split(jax.random.fold_in(arg_keys[3], 1), NB * KB // KS)
    owner_turns = jax.random.permutation(jax.random.fold_in(arg_keys[3], 3), NB * KB // KS)
    owner = jax.vmap(lambda own, number: shared_out(jax.random.fold_in(arg_keys[3], 2), own, number, KS, N_COLS, 1, SCAP, 2))(owner_keys, owner_turns).reshape((NB, KB, 1))
    tile_of = set_ends(jax.random.randint(arg_keys[4], (NB, KB), 0, TPS), jax.random.fold_in(arg_keys[4], 1), 0, TPS - 1).astype(jnp.int32)
    offsets = set_ends(jax.random.randint(arg_keys[5], (NB, KB, P_SIZE), 0, TILE), jax.random.fold_in(arg_keys[5], 1), 0, TILE - 1).astype(jnp.int32)
    accept = set_ends((jax.random.randint(arg_keys[6], (NB, KB), 0, 10) < 9).astype(jnp.int32), jax.random.fold_in(arg_keys[6], 1), 0, 1)
    loc_mask = set_ends((jax.random.randint(arg_keys[7], (NTILES, NB, NBLK), 0, 4) < 1).astype(jnp.int32), jax.random.fold_in(arg_keys[7], 1), 0, 1)
    return {"state": state, "obs_value": obs_value, "obs_var": obs_var, "owner": owner, "tile_of": tile_of, "offsets": offsets, "accept": accept, "loc_mask": loc_mask}


epsilon = 1e-05
EXACT = lax.Precision.HIGHEST

def innovations(prior_obs, observed, obs_noise, accepted):
    members = prior_obs.shape[0]
    mean_prior = lax.optimization_barrier(jnp.mean(prior_obs, axis=0))
    spread = prior_obs - mean_prior
    spread_var = lax.optimization_barrier(jnp.sum(spread * spread, axis=0)) / (members - 1) + epsilon
    denominator = spread_var + obs_noise
    mean_shift = spread_var / denominator * (observed - mean_prior)
    factor = jnp.sqrt(obs_noise / denominator) - 1.0
    increment = accepted * (mean_shift + factor * spread)
    scaled = spread / ((members - 1) * spread_var)
    return (increment, scaled)

def reference(state, obs_value, obs_var, owner, tile_of, offsets, accept, loc_mask):
    ensemble = state
    for batch_no in range(NB):
        cells_of = (owner[batch_no, :, 0] * NS_DEV + tile_of[batch_no] * TILE).astype(jnp.int32)[:, None] + offsets[batch_no]
        picked = jnp.take(ensemble, cells_of.reshape(-1).astype(jnp.int32), axis=1).reshape(M, KB, P_SIZE)
        prior_obs = lax.optimization_barrier(jnp.sum(picked, axis=2)) / P_SIZE
        increment, scaled = innovations(prior_obs, obs_value[batch_no], obs_var[batch_no], accept[batch_no].astype(jnp.float32))
        per_block = jnp.einsum('nbk,mbk->bnm', scaled.reshape(M, NBLK, OBLK), increment.reshape(M, NBLK, OBLK), precision=EXACT)
        mixing = jnp.einsum('tb,bnm->tnm', loc_mask[:, batch_no, :].astype(jnp.float32), per_block, precision=EXACT)
        mean_state = lax.optimization_barrier(jnp.mean(ensemble, axis=0))
        deviation = (ensemble - mean_state).reshape(M, NTILES, TILE)
        change = jnp.einsum('tnm,nti->mti', mixing, deviation, precision=EXACT)
        ensemble = ensemble + change.reshape(M, NS)
    return ensemble
```

```python
import jax
import jax.numpy as jnp
from jax import lax
from jax.experimental import pallas as pl
from jax.experimental.pallas import tpu as pltpu
from jax.sharding import PartitionSpec as P

epsilon = 1e-05
MESH = pl.DeviceIdType.MESH
F32 = jnp.float32
BF = jnp.bfloat16
I32 = jnp.int32

NB = 4
NC = 32
NK = 8
MLOC = 10
M = 80
NY = 4
NZ = 8
TILE = 512
NT = 8
CELLS = 4096
RA = 40
RB = 24


def vm():
    return pl.BlockSpec(memory_space=pltpu.VMEM)


def sm():
    return pl.BlockSpec(memory_space=pltpu.SMEM)


def hbm():
    return pl.BlockSpec(memory_space=pl.ANY)


def iota(shape, axis):
    return lax.broadcasted_iota(I32, shape, axis)


def greet(c, k):
    bar = pltpu.get_barrier_semaphore()
    for d in range(1, NC):
        pl.semaphore_signal(bar, inc=1, device_id=(lax.rem(c + d, NC), k), device_id_type=MESH)
    for d in range(1, NK):
        pl.semaphore_signal(bar, inc=1, device_id=(c, lax.rem(k + d, NK)), device_id_type=MESH)
    pl.semaphore_wait(bar, NC - 1 + NK - 1)


def send(src, dst, ssem, rsem, dev):
    cp = pltpu.make_async_remote_copy(
        src_ref=src, dst_ref=dst, send_sem=ssem, recv_sem=rsem, device_id=dev, device_id_type=MESH
    )
    cp.start()
    return cp


def slots_kernel(m_ref, mk_ref, r_ref, mko_ref, ss, rs, ks, kr):
    c = lax.axis_index("cols")
    k = lax.axis_index("mem")
    greet(c, k)
    cps = []
    for d in range(1, NC):
        p = lax.rem(c + d, NC)
        cps.append(send(m_ref.at[p], r_ref.at[c], ss.at[d], rs.at[d], (p, k)))
    for d in range(1, NK):
        cps.append(send(mk_ref, mko_ref.at[k], ks.at[d], kr.at[d], (c, lax.rem(k + d, NK))))
    r_ref[c] = m_ref[c]
    mko_ref[k] = mk_ref[...]
    for cp in cps:
        cp.wait()


def slots_call(m, mk):
    return pl.pallas_call(
        slots_kernel,
        out_shape=(
            jax.ShapeDtypeStruct((NC, 1, 128), I32),
            jax.ShapeDtypeStruct((NK, 8, 128), I32),
        ),
        in_specs=[vm(), vm()],
        out_specs=(vm(), vm()),
        scratch_shapes=[
            pltpu.SemaphoreType.DMA((NC,)),
            pltpu.SemaphoreType.DMA((NC,)),
            pltpu.SemaphoreType.DMA((NK,)),
            pltpu.SemaphoreType.DMA((NK,)),
        ],
        compiler_params=pltpu.CompilerParams(collective_id=0, has_side_effects=True),
        name="slots",
    )(m, mk)


def prior_kernel(r_ref, mk_ref, st_ref, out_ref, xs):
    k = lax.axis_index("mem")
    lane = iota((MLOC, 128), 1)
    lane1 = iota((1, 128), 1)
    xs[...] = jnp.zeros_like(xs)
    for q in range(8):

        def body(s, acc):
            a, e0, e1, e2 = acc
            v = jnp.zeros((MLOC, 128), F32)
            for p in range(4):
                cell = r_ref[s, q * 4 + p]
                base = pl.multiple_of((cell >> 7) * 128, 128)
                hit = lane == (cell & 127)
                v = v + jnp.where(hit, st_ref[:, pl.ds(base, 128)], 0.0)
            tile = r_ref[s, q * 4] >> 9
            col = jnp.sum(v, axis=1, keepdims=True) * 0.25
            here = lane1 == s
            a = jnp.where(lane == s, col, a)
            e0 = jnp.where(here, mk_ref[tile, 3 * k], e0)
            e1 = jnp.where(here, mk_ref[tile, 3 * k + 1], e1)
            e2 = jnp.where(here, mk_ref[tile, 3 * k + 2], e2)
            return a, e0, e1, e2

        z = jnp.zeros((1, 128), I32)
        a, e0, e1, e2 = lax.fori_loop(
            0, NC, body, (jnp.zeros((MLOC, 128), F32), z, z, z), unroll=4
        )
        xs[16 * q : 16 * q + 10, :] = a
        xs[16 * q + 10 : 16 * q + 11, :] = e0.astype(F32)
        xs[16 * q + 11 : 16 * q + 12, :] = e1.astype(F32)
        xs[16 * q + 12 : 16 * q + 13, :] = e2.astype(F32)
    xt = jnp.transpose(xs[...])
    out_ref[...] = xt[:NC].reshape(NC, 1, 128)


def prior_call(r, mk, state):
    return pl.pallas_call(
        prior_kernel,
        out_shape=jax.ShapeDtypeStruct((NC, 1, 128), F32),
        in_specs=[sm(), sm(), vm()],
        out_specs=vm(),
        scratch_shapes=[pltpu.VMEM((128, 128), F32)],
        name="prior",
    )(r, mk, state)


def gather_kernel(
    z_ref, meta_ref, st_ref, g_ref, s_ref, rz,
    ss, rs, xs, xr, a1s, a1r, b1s, b1r, a2s, a2r, b2s, b2r, ps, pr, ts, tr, own,
):
    c = lax.axis_index("cols")
    k = lax.axis_index("mem")
    y = c // NZ
    z = lax.rem(c, NZ)
    x = k // 2
    core = lax.rem(k, 2)
    greet(c, k)
    rows = []
    for d in range(1, NC):
        p = lax.rem(c + d, NC)
        rows.append(send(z_ref.at[p], rz.at[c], ss.at[d], rs.at[d], (p, k)))
    rz[c] = z_ref[c]
    for cp in rows:
        cp.wait()
    got = rz[...].reshape(NC, 128)
    owner = meta_ref[0:1, :]
    slot = meta_ref[1:2, :]
    hot = jnp.where(iota((NC, 128), 0).astype(F32) == owner, 1.0, 0.0)
    full = lax.dot_general(
        got, hot, (((0,), (0,)), ((), ())),
        precision=lax.Precision.HIGHEST, preferred_element_type=F32,
    )
    blk = jnp.zeros((16, 128), F32)
    for q in range(8):
        blk = blk + jnp.where(slot == float(q), full[16 * q : 16 * q + 16, :], 0.0)
    first = blk[0:8]
    second = blk[8:16]
    row8 = iota((8, 128), 0)
    second = jnp.where(row8 == 5, meta_ref[2:3, :], second)
    second = jnp.where(row8 == 6, meta_ref[3:4, :], second)
    second = jnp.where(row8 == 7, meta_ref[4:5, :], second)
    quad = lax.rem(k, 4)
    turned = second
    for j in range(1, 4):
        turned = jnp.where(quad == j, pltpu.roll(second, 2 * j, 0), turned)
    r0 = pl.multiple_of(16 * k, 16)
    g_ref[y, z, pl.ds(r0, 8), :] = first
    g_ref[y, z, pl.ds(pl.multiple_of(r0 + 8, 8), 8), :] = turned
    mine = g_ref.at[y, z, pl.ds(r0, 16), :]
    step = []
    for d in range(1, NK):
        step.append(send(mine, mine, xs.at[d], xr.at[d], (c, lax.rem(k + d, NK))))
    for cp in step:
        cp.wait()
    moves = []
    for d in range(1, NK):
        p = lax.rem(k + d, NK)
        moves.append(
            send(
                st_ref.at[:, pl.ds(pl.multiple_of(p * CELLS, CELLS), CELLS)],
                s_ref.at[k], ts.at[d], tr.at[d], (c, p),
            )
        )
    keep = pltpu.make_async_copy(
        st_ref.at[:, pl.ds(pl.multiple_of(k * CELLS, CELLS), CELLS)], s_ref.at[k], own
    )
    keep.start()
    ra = pl.multiple_of(64 * core, 8)
    rb = pl.multiple_of(64 * core + RA, 8)
    a1 = g_ref.at[y, z, pl.ds(ra, RA), :]
    b1 = g_ref.at[y, z, pl.ds(rb, RB), :]
    first_a = []
    first_b = []
    for d in range(1, NZ):
        first_a.append(send(a1, a1, a1s.at[d], a1r.at[d], (y * NZ + lax.rem(z + d, NZ), k)))
    for d in range(1, NY):
        first_b.append(send(b1, b1, b1s.at[d], b1r.at[d], (lax.rem(y + d, NY) * NZ + z, k)))
    for cp in first_b:
        cp.wait()
    b2 = g_ref.at[:, z, pl.ds(rb, RB), :]
    second_b = []
    for d in range(1, NZ):
        second_b.append(send(b2, b2, b2s.at[d], b2r.at[d], (y * NZ + lax.rem(z + d, NZ), k)))
    for cp in first_a:
        cp.wait()
    a2 = g_ref.at[y, :, pl.ds(ra, RA), :]
    second_a = []
    for d in range(1, NY):
        second_a.append(send(a2, a2, a2s.at[d], a2r.at[d], (lax.rem(y + d, NY) * NZ + z, k)))
    for cp in second_b:
        cp.wait()
    for cp in second_a:
        cp.wait()
    pair = []
    for d in range(1, NC):
        p = lax.rem(c + d, NC)
        half = g_ref.at[p // NZ, lax.rem(p, NZ), pl.ds(ra, 64), :]
        pair.append(send(half, half, ps.at[d], pr.at[d], (c, k + 1 - 2 * core)))
    for cp in pair:
        cp.wait()
    keep.wait()
    for cp in moves:
        cp.wait()


def gather_call(z, meta, state):
    dma = pltpu.SemaphoreType.DMA
    return pl.pallas_call(
        gather_kernel,
        out_shape=(
            jax.ShapeDtypeStruct((NY, NZ, 128, 128), F32),
            jax.ShapeDtypeStruct((NK, MLOC, CELLS), F32),
        ),
        in_specs=[vm(), vm(), hbm()],
        out_specs=(vm(), hbm()),
        scratch_shapes=[
            pltpu.VMEM((NC, 1, 128), F32),
            dma((NC,)), dma((NC,)), dma((NK,)), dma((NK,)),
            dma((NZ,)), dma((NZ,)), dma((NY,)), dma((NY,)),
            dma((NY,)), dma((NY,)), dma((NZ,)), dma((NZ,)),
            dma((NC,)), dma((NC,)), dma((NK,)), dma((NK,)), dma(()),
        ],
        compiler_params=pltpu.CompilerParams(collective_id=1, has_side_effects=True),
        name="spread_out",
    )(z, meta, state)


def split(v):
    hi = v.astype(BF)
    lo = (v - hi.astype(F32)).astype(BF)
    return hi, lo


def mm(a, b, dims):
    return lax.dot_general(a, b, (dims, ((), ())), preferred_element_type=F32)


NN = ((1,), (0,))
NT_ = ((1,), (1,))
TN = ((0,), (0,))
WIDE = NB * 1024 + NT * 128
CH = 512


def extra_row(k, x):
    return 16 * k + 8 + (2 * (k % 4) + 2 + x) % 8


def window_kernel(g_ref, s_ref, mk_ref, out_ref, zz, mask, val, pp, pt, dh, dl, sp, tp):
    lane_group = iota((128, 128), 1) // 32
    sub = iota((8, 128), 0) // 2

    def assemble(blk, _):
        parts = [g_ref[4 * blk + u] for u in range(4)]
        for b in range(NB):
            v = parts[3]
            for u in range(3):
                v = jnp.where(lane_group == (b + u) % 4, parts[u], v)
            lanes = pl.ds(pl.multiple_of(b * 1024 + blk * 128, 128), 128)
            for kk in range(NK):
                zz[8 * kk : 8 * kk + 8, lanes] = v[16 * kk : 16 * kk + 8]
            for h in range(2):
                t = v[16 * (4 * h) + 8 : 16 * (4 * h) + 16]
                for j in range(1, 4):
                    kk = 4 * h + j
                    t = jnp.where(sub == j, v[16 * kk + 8 : 16 * kk + 16], t)
                zz[64 + 8 * h : 72 + 8 * h, lanes] = t
            for e in range(8 * b):
                r = extra_row(e // 3, e % 3)
                mask[e : e + 1, lanes] = v[r : r + 1]
            for j in range(3):
                r = extra_row(0, 3 + j)
                val[j : j + 1, lanes] = v[r : r + 1]
        return 0

    lax.fori_loop(0, 8, assemble, 0)
    n = lax.rem(iota((M, NT * 128), 1), 128)
    kk = n // 16
    ii = lax.rem(n, 16)
    place = jnp.where(ii < 8, 8 * kk + ii, 64 + 2 * kk + ii - 8)
    unit = (iota((M, NT * 128), 0) == place) & (ii < MLOC)
    zz[:, NB * 1024 :] = jnp.where(unit, 1.0, 0.0)
    grow = jnp.where(iota((8, NT * 128), 0) == iota((8, NT * 128), 1) // 128, 1.0, 0.0)
    mask[:, NB * 1024 :] = mm(mk_ref[...].astype(F32), grow, TN)[:32]
    pp[...] = jnp.zeros_like(pp)

    for b in range(NB):
        lanes = slice(b * 1024, b * 1024 + 1024)
        prior = zz[:, lanes]
        accepted = val[0:1, lanes]
        observed = val[1:2, lanes]
        noise = val[2:3, lanes]
        mean = jnp.sum(prior, axis=0, keepdims=True) / M
        dev = prior - mean
        var = jnp.sum(dev * dev, axis=0, keepdims=True) / (M - 1) + epsilon
        den = var + noise
        shift = var / den * (observed - mean)
        factor = jnp.sqrt(noise / den) - 1.0
        inc = accepted * (shift + factor * dev)
        scl = dev / ((M - 1) * var)
        ih, il = split(inc)
        sh, sl = split(scl)
        for q in range(8):
            w = slice(128 * q, 128 * q + 128)
            prod = mm(sh[:, w], ih[:, w], NT_) + mm(sh[:, w], il[:, w], NT_) + mm(sl[:, w], ih[:, w], NT_)
            pp[80 * q : 80 * q + 80, 0:80] = prod
        ph, plo = split(jnp.transpose(pp[...])[:M])
        pt[0:M, :] = ph
        pt[M : 2 * M, :] = plo

        def update(i, _):
            at = pl.ds(pl.multiple_of((b + 1) * 1024 + i * CH, CH), CH)
            v = zz[:, at]
            d = v - jnp.sum(v, axis=0, keepdims=True) * (1.0 / M)
            hi, lo = split(d)
            for q in range(8):
                w = jnp.broadcast_to(mask[8 * b + q : 8 * b + q + 1, at], (16, CH)).astype(BF)
                for g in range(5):
                    rr = slice(80 * q + 16 * g, 80 * q + 16 * g + 16)
                    dh[rr, :] = hi[16 * g : 16 * g + 16] * w
                    dl[rr, :] = lo[16 * g : 16 * g + 16] * w
            both = mm(pt[...], dh[...], NN)
            rest = mm(pt[0:M, :], dl[...], NN)
            zz[:, at] = v + (both[0:M] + (both[M : 2 * M] + rest))
            return 0

        lax.fori_loop(0, (WIDE - (b + 1) * 1024) // CH, update, 0)

    true = iota((M, M), 0)
    tk = true // MLOC
    ti = lax.rem(true, MLOC)
    place = jnp.where(ti < 8, 8 * tk + ti, 64 + 2 * tk + ti - 8)
    perm = jnp.where(iota((M, M), 1) == place, 1.0, 0.0).astype(BF)
    th, tl = split(zz[:, NB * 1024 :])
    tp[0:M, :] = mm(perm, th, NN).astype(BF)
    tp[M : 2 * M, :] = mm(perm, tl, NN).astype(BF)
    sp[...] = jnp.zeros_like(sp)
    for t in range(NT):
        at = slice(TILE * t, TILE * t + TILE)
        for kk in range(NK):
            sp[16 * kk : 16 * kk + MLOC, :] = s_ref[kk, :, at]
        hi, lo = split(sp[...])
        maps = tp[:, 128 * t : 128 * t + 128]
        both = mm(maps, hi, NN)
        rest = mm(maps[0:M], lo, NN)
        out_ref[:, at] = both[0:M] + (both[M : 2 * M] + rest)


def window_call(g, s, mk):
    return pl.pallas_call(
        window_kernel,
        out_shape=jax.ShapeDtypeStruct((M, CELLS), F32),
        in_specs=[vm(), vm(), vm()],
        out_specs=vm(),
        scratch_shapes=[
            pltpu.VMEM((M, WIDE), F32),
            pltpu.VMEM((32, WIDE), F32),
            pltpu.VMEM((8, NB * 1024), F32),
            pltpu.VMEM((640, 128), F32),
            pltpu.VMEM((2 * M, 640), BF),
            pltpu.VMEM((640, CH), BF),
            pltpu.VMEM((640, CH), BF),
            pltpu.VMEM((128, TILE), F32),
            pltpu.VMEM((2 * M, NT * 128), BF),
        ],
        name="window",
    )(g, s, mk)


def prepare(obs_value, obs_var, owner, tile_of, offsets, accept, loc_mask, source):
    dest = owner[:, :, 0]
    order = jnp.arange(32, dtype=I32)
    same = (dest[:, :, None] == dest[:, None, :]) & (order[None, :] < order[:, None])[None]
    rank = jnp.sum(same.astype(I32), axis=2)
    cells = tile_of[:, :, None] * TILE + offsets
    hit = (dest[None, :, None, :] == order[:, None, None, None]) & (
        rank[None, :, None, :] == jnp.arange(2, dtype=I32)[None, None, :, None]
    )
    slots = jnp.sum(jnp.where(hit[:, :, :, :, None], cells[None, :, None, :, :], 0), axis=3)
    slots = jnp.pad(slots.reshape(NC, 32), ((0, 0), (0, 96))).reshape(NC, 1, 128)
    batch = jnp.arange(NB, dtype=I32)
    rows = jnp.stack(
        [
            dest.astype(F32),
            (batch[:, None] * 2 + rank).astype(F32),
            accept.astype(F32),
            obs_value,
            obs_var,
        ]
    )
    turn = jnp.mod(batch[:, None] - source, NB) == batch[None, :]
    meta = jnp.sum(jnp.where(turn[None, :, :, None], rows[:, None], 0.0), axis=2)
    meta = jnp.pad(meta.reshape(5, 128), ((0, 3), (0, 0)))
    mk = jnp.pad(loc_mask.reshape(8, 32), ((0, 0), (0, 96)))
    return slots, meta, mk


def local(state, obs_value, obs_var, owner, tile_of, offsets, accept, loc_mask):
    slots, meta, mk = prepare(
        obs_value, obs_var, owner, tile_of, offsets, accept, loc_mask, lax.axis_index("cols")
    )
    r, mks = slots_call(slots, mk)
    z = prior_call(r.reshape(NC, 128), mks.reshape(64, 128), state)
    g, s = gather_call(z, meta, state)
    return window_call(g.reshape(NC, 128, 128), s, mk)


def solution(mesh):
    return jax.shard_map(
        local,
        mesh=mesh,
        in_specs=(
            P("mem", "cols"),
            P(None, "cols"),
            P(None, "cols"),
            P(None, "cols", None),
            P(None, "cols"),
            P(None, "cols", None),
            P(None, "cols"),
            P(("cols", "mem"), None, None),
        ),
        out_specs=P(None, ("cols", "mem")),
        check_vma=False,
    )
```

```python
import jax
import jax.numpy as jnp
from jax import lax
from jax.experimental import pallas as pl
from jax.experimental.pallas import tpu as pltpu
from jax.sharding import PartitionSpec as P

epsilon = 1e-05
MESH = pl.DeviceIdType.MESH
F32 = jnp.float32
BF = jnp.bfloat16
I32 = jnp.int32

NB = 4
NC = 32
NK = 8
MLOC = 10
M = 80
NY = 4
NZ = 8
TILE = 512
NT = 8
CELLS = 4096
RA = 40
RB = 24


def vm():
    return pl.BlockSpec(memory_space=pltpu.VMEM)


def sm():
    return pl.BlockSpec(memory_space=pltpu.SMEM)


def hbm():
    return pl.BlockSpec(memory_space=pl.ANY)


def iota(shape, axis):
    return lax.broadcasted_iota(I32, shape, axis)


def split(v):
    hi = v.astype(BF)
    lo = (v - hi.astype(F32)).astype(BF)
    return hi, lo


def mm(a, b, dims):
    return lax.dot_general(a, b, (dims, ((), ())), preferred_element_type=F32)


NN = ((1,), (0,))
NT_ = ((1,), (1,))
TN = ((0,), (0,))
def send(src, dst, ssem, rsem, dev):
    cp = pltpu.make_async_remote_copy(
        src_ref=src, dst_ref=dst, send_sem=ssem, recv_sem=rsem, device_id=dev, device_id_type=MESH
    )
    cp.start()
    return cp


def exchange_kernel(
    ow, ti, of, ac, va, vr, lm, st, g_ref, s_ref,
    stv, tiled, fi, fl, mv, mrow, rr, rsm, mks, xs, zrow, rz,
    ls, own, cs, ms, mr, ks, kr, ss, rs, xss, xsr, a1s, a1r, b1s, b1r, a2s, a2r, b2s, b2r,
    pas, par, pbs, pbr, pcs, pcr, pds, pdr, ts, tr,
):
    c = lax.axis_index("cols")
    k = lax.axis_index("mem")
    y = c // NZ
    z = lax.rem(c, NZ)
    core = lax.rem(k, 2)
    quad = lax.rem(k, 4)
    bar = pltpu.get_barrier_semaphore()
    for d in range(1, NC):
        pl.semaphore_signal(bar, inc=1, device_id=(lax.rem(c + d, NC), k), device_id_type=MESH)
    for d in range(1, NK):
        pl.semaphore_signal(bar, inc=1, device_id=(c, lax.rem(k + d, NK)), device_id_type=MESH)
    load = pltpu.make_async_copy(st, stv, ls)
    load.start()
    mv[...] = jnp.zeros_like(mv)
    tiles = ti[...] * TILE
    cells = [tiles + of[:, p, :] for p in range(4)]
    places = [ow[...], cells[0] + (cells[1] << 15), cells[2] + (cells[3] << 15)]
    fields = [ac[...].astype(F32), va[...], vr[...]]
    for b in range(NB):
        at = slice(32 * b, 32 * b + 32)
        for f in range(3):
            fi[f : f + 1, at] = places[f][b : b + 1, :]
            fl[f : f + 1, at] = fields[f][b : b + 1, :]
        mv[:, 8 * b : 8 * b + 8] = lm[:, b, :].astype(F32)
    r128 = iota((128, 128), 0)
    c128 = iota((128, 128), 1)
    lane32 = iota((NC, 128), 1)
    within = lane32 & 31
    hoti = jnp.where(iota((NC, 128), 0) == fi[0:1, :], 1, 0)
    seen = hoti
    for h in (1, 2, 4, 8, 16):
        seen = seen + jnp.where(within >= h, pltpu.roll(seen, h, 1), 0)
    slots = jnp.zeros((NC, 128), I32)
    for r in range(2):
        for w in range(2):
            v = jnp.where((hoti == 1) & (seen == r + 1), fi[w + 1 : w + 2, :], 0)
            for h in (1, 2, 4, 8, 16):
                v = v + pltpu.roll(v, 128 - h, 1)
            for p, cell in ((2 * w, v & 32767), (2 * w + 1, (v >> 15) & 32767)):
                for f, word in ((p, cell >> 7), (p + 4, cell & 127)):
                    spot = 8 * r + f
                    word = word if spot == 0 else pltpu.roll(word, spot, 1)
                    slots = jnp.where(within == spot, word, slots)
    mrow[...] = slots.reshape(NC, 1, 128)
    hot = hoti.astype(F32)
    rank = jnp.sum((hoti * (seen - 1)).astype(F32), axis=0, keepdims=True)
    load.wait()
    for t in range(NK * CELLS // 128):
        tiled[t] = stv[:, 128 * t : 128 * t + 128]
    pl.semaphore_wait(bar, NC - 1 + NK - 1)

    ask = []
    for d in range(1, NC):
        p = lax.rem(c + d, NC)
        ask.append(send(mrow.at[p], rr.at[c], ms.at[d], mr.at[d], (p, k)))
    maps = []
    for d in range(1, NK):
        maps.append(send(mv, mks.at[k], ks.at[d], kr.at[d], (c, lax.rem(k + d, NK))))
    rr[c] = mrow[c]
    mks[k] = mv[...]
    moves = []
    for d in range(1, NK):
        p = lax.rem(k + d, NK)
        part = stv.at[:, pl.ds(pl.multiple_of(p * CELLS, CELLS), CELLS)]
        moves.append(send(part, s_ref.at[k], ts.at[d], tr.at[d], (c, p)))
    keep = pltpu.make_async_copy(
        stv.at[:, pl.ds(pl.multiple_of(k * CELLS, CELLS), CELLS)], s_ref.at[k], own
    )
    keep.start()
    for cp in ask:
        cp.wait()
    scal = pltpu.make_async_copy(rr, rsm, cs)
    scal.start()
    for cp in maps:
        cp.wait()
    pick = lax.rem(c128, 16) - 10
    chosen = jnp.where((pick >= 0) & (pick < 3) & (r128 == 3 * k + pick), 1.0, 0.0)
    table = mm(mks[...].reshape(64, 128).astype(BF), chosen.astype(BF), NN).astype(BF)
    got = rr[...].reshape(NC, 128)
    extra = jnp.zeros((NC, 128), F32)
    for q in range(8):
        word = 32 * (q // 2) + 8 * (q % 2)
        tile = got[:, word : word + 1] >> 2
        at_tile = jnp.where(iota((NC, 64), 1) == tile, 1.0, 0.0).astype(BF)
        extra = jnp.where(lane32 // 16 == q, mm(at_tile, table, NN), extra)
    scal.wait()
    lane = iota((MLOC, 128), 1)

    def priors(i, accs):
        here = lane == i
        out = []
        for q in range(8):
            v = jnp.zeros((MLOC, 128), F32)
            word = 32 * (q // 2) + 8 * (q % 2)
            for p in range(4):
                hit = lane == rsm[i, 0, word + 4 + p]
                v = v + jnp.where(hit, tiled[rsm[i, 0, word + p]], 0.0)
            out.append(jnp.where(here, jnp.sum(v, axis=1, keepdims=True), accs[q]))
        return tuple(out)

    accs = lax.fori_loop(0, NC, priors, tuple(jnp.zeros((MLOC, 128), F32) for _ in range(8)))
    xs[...] = jnp.zeros_like(xs)
    for q in range(8):
        xs[16 * q : 16 * q + MLOC, :] = accs[q] * 0.25
    zr = jnp.transpose(xs[...])[:NC] + extra
    zrow[...] = zr.reshape(NC, 1, 128)
    back = []
    for d in range(1, NC):
        p = lax.rem(c + d, NC)
        back.append(send(zrow.at[p], rz.at[c], ss.at[d], rs.at[d], (p, k)))
    rz[c] = zrow[c]
    for cp in back:
        cp.wait()
    full = lax.dot_general(
        rz[...].reshape(NC, 128), hot, (TN, ((), ())),
        precision=lax.Precision.HIGHEST, preferred_element_type=F32,
    )
    batch = iota((1, 128), 1) // 32
    blk = jnp.zeros((16, 128), F32)
    for q in range(8):
        mine = (batch == q // 2) & (rank == float(q % 2))
        blk = blk + jnp.where(mine, full[16 * q : 16 * q + 16, :], 0.0)
    row16 = iota((16, 128), 0)
    for j in range(3):
        blk = jnp.where(row16 == 13 + j, fl[j : j + 1, :], blk)
    turned = blk
    around = lax.rem(z, 4)
    for j in range(1, 4):
        turned = jnp.where(around == j, pltpu.roll(blk, 32 * j, 1), turned)
    second = turned[8:16]
    placed = second
    for j in range(1, 4):
        placed = jnp.where(quad == j, pltpu.roll(second, 2 * j, 0), placed)
    r0 = pl.multiple_of(16 * k, 16)
    g_ref[y, z, pl.ds(r0, 8), :] = turned[0:8]
    g_ref[y, z, pl.ds(pl.multiple_of(r0 + 8, 8), 8), :] = placed
    block = g_ref.at[y, z, pl.ds(r0, 16), :]
    step = []
    for d in range(1, NK):
        step.append(send(block, block, xss.at[d], xsr.at[d], (c, lax.rem(k + d, NK))))
    for cp in step:
        cp.wait()
    ra = pl.multiple_of(64 * core, 8)
    rb = pl.multiple_of(64 * core + RA, 8)
    mate = (c, k + 1 - 2 * core)
    a1 = g_ref.at[y, z, pl.ds(ra, RA), :]
    b1 = g_ref.at[y, z, pl.ds(rb, RB), :]
    first_a = []
    first_b = []
    for d in range(1, NZ):
        first_a.append(send(a1, a1, a1s.at[d], a1r.at[d], (y * NZ + lax.rem(z + d, NZ), k)))
    for d in range(1, NY):
        first_b.append(send(b1, b1, b1s.at[d], b1r.at[d], (lax.rem(y + d, NY) * NZ + z, k)))
    for cp in first_b:
        cp.wait()
    b2 = g_ref.at[:, z, pl.ds(rb, RB), :]
    second_b = []
    for d in range(1, NZ):
        second_b.append(send(b2, b2, b2s.at[d], b2r.at[d], (y * NZ + lax.rem(z + d, NZ), k)))
    for cp in first_a:
        cp.wait()
    a2 = g_ref.at[y, :, pl.ds(ra, RA), :]
    second_a = []
    for d in range(1, NY):
        second_a.append(send(a2, a2, a2s.at[d], a2r.at[d], (lax.rem(y + d, NY) * NZ + z, k)))
    pair = []
    for d in range(1, NY):
        piece = g_ref.at[lax.rem(y + d, NY), z, pl.ds(rb, RB), :]
        pair.append(send(piece, piece, pas.at[d], par.at[d], mate))
    for d in range(1, NZ):
        piece = g_ref.at[y, lax.rem(z + d, NZ), pl.ds(ra, RA), :]
        pair.append(send(piece, piece, pbs.at[d], pbr.at[d], mate))
    for d in range(1, NZ):
        second_b[d - 1].wait_recv()
        piece = g_ref.at[:, lax.rem(z + NZ - d, NZ), pl.ds(rb, RB), :]
        pair.append(send(piece, piece, pcs.at[d], pcr.at[d], mate))
    for d in range(1, NY):
        second_a[d - 1].wait_recv()
        piece = g_ref.at[lax.rem(y + NY - d, NY), :, pl.ds(ra, RA), :]
        pair.append(send(piece, piece, pds.at[d], pdr.at[d], mate))
    for cp in second_b + second_a:
        cp.wait_send()
    keep.wait()
    for cp in moves + pair:
        cp.wait()


def exchange_call(ow, ti, of, ac, va, vr, lm, st):
    dma = pltpu.SemaphoreType.DMA
    row = pltpu.VMEM((NC, 1, 128), F32)
    irow = pltpu.VMEM((NC, 1, 128), I32)
    return pl.pallas_call(
        exchange_kernel,
        out_shape=(
            jax.ShapeDtypeStruct((NY, NZ, 128, 128), F32),
            jax.ShapeDtypeStruct((NK, MLOC, CELLS), F32),
        ),
        in_specs=[vm()] * 7 + [hbm()],
        out_specs=(vm(), hbm()),
        scratch_shapes=[
            pltpu.VMEM((MLOC, NK * CELLS), F32),
            pltpu.VMEM((NK * CELLS // 128, MLOC, 128), F32),
            pltpu.VMEM((8, 128), I32),
            pltpu.VMEM((8, 128), F32),
            pltpu.VMEM((8, 128), F32),
            irow, irow,
            pltpu.SMEM((NC, 1, 128), I32),
            pltpu.VMEM((NK, 8, 128), F32),
            pltpu.VMEM((128, 128), F32),
            row, row,
            dma(()), dma(()), dma(()),
            dma((NC,)), dma((NC,)), dma((NK,)), dma((NK,)),
            dma((NC,)), dma((NC,)), dma((NK,)), dma((NK,)),
            dma((NZ,)), dma((NZ,)), dma((NY,)), dma((NY,)),
            dma((NY,)), dma((NY,)), dma((NZ,)), dma((NZ,)),
            dma((NY,)), dma((NY,)), dma((NZ,)), dma((NZ,)),
            dma((NZ,)), dma((NZ,)), dma((NY,)), dma((NY,)),
            dma((NK,)), dma((NK,)),
        ],
        compiler_params=pltpu.CompilerParams(collective_id=0, has_side_effects=True),
        name="exchange",
    )(ow, ti, of, ac, va, vr, lm, st)


WIDE = NB * 1024 + NT * 128
CH = 512


def extra_row(k, x):
    return 16 * k + 8 + (2 * (k % 4) + 2 + x) % 8


def window_kernel(g_ref, s_ref, mk_ref, out_ref, zz, mask, val, pp, pt, dh, dl, sp, tp):
    lane_group = iota((128, 128), 1) // 32
    sub = iota((8, 128), 0) // 2

    def assemble(blk, _):
        parts = [g_ref[4 * blk + u] for u in range(4)]
        for b in range(NB):
            v = parts[3]
            for u in range(3):
                v = jnp.where(lane_group == (b + u) % 4, parts[u], v)
            lanes = pl.ds(pl.multiple_of(b * 1024 + blk * 128, 128), 128)
            for kk in range(NK):
                zz[8 * kk : 8 * kk + 8, lanes] = v[16 * kk : 16 * kk + 8]
            for h in range(2):
                t = v[16 * (4 * h) + 8 : 16 * (4 * h) + 16]
                for j in range(1, 4):
                    kk = 4 * h + j
                    t = jnp.where(sub == j, v[16 * kk + 8 : 16 * kk + 16], t)
                zz[64 + 8 * h : 72 + 8 * h, lanes] = t
            for e in range(8 * b):
                r = extra_row(e // 3, e % 3)
                mask[e : e + 1, lanes] = v[r : r + 1]
            for j in range(3):
                r = extra_row(0, 3 + j)
                val[j : j + 1, lanes] = v[r : r + 1]
        return 0

    lax.fori_loop(0, 8, assemble, 0)
    n = lax.rem(iota((M, NT * 128), 1), 128)
    kk = n // 16
    ii = lax.rem(n, 16)
    place = jnp.where(ii < 8, 8 * kk + ii, 64 + 2 * kk + ii - 8)
    unit = (iota((M, NT * 128), 0) == place) & (ii < MLOC)
    zz[:, NB * 1024 :] = jnp.where(unit, 1.0, 0.0)
    grow = jnp.where(iota((8, NT * 128), 0) == iota((8, NT * 128), 1) // 128, 1.0, 0.0)
    for b in range(NB):
        mask[8 * b : 8 * b + 8, NB * 1024 :] = mm(mk_ref[:, b, :].astype(F32), grow, TN)
    pp[...] = jnp.zeros_like(pp)

    for b in range(NB):
        lanes = slice(b * 1024, b * 1024 + 1024)
        prior = zz[:, lanes]
        accepted = val[0:1, lanes]
        observed = val[1:2, lanes]
        noise = val[2:3, lanes]
        mean = jnp.sum(prior, axis=0, keepdims=True) / M
        dev = prior - mean
        var = jnp.sum(dev * dev, axis=0, keepdims=True) / (M - 1) + epsilon
        den = var + noise
        shift = var / den * (observed - mean)
        factor = jnp.sqrt(noise / den) - 1.0
        inc = accepted * (shift + factor * dev)
        scl = dev / ((M - 1) * var)
        ih, il = split(inc)
        sh, sl = split(scl)
        for q in range(8):
            w = slice(128 * q, 128 * q + 128)
            prod = mm(sh[:, w], ih[:, w], NT_) + mm(sh[:, w], il[:, w], NT_) + mm(sl[:, w], ih[:, w], NT_)
            pp[80 * q : 80 * q + 80, 0:80] = prod
        ph, plo = split(jnp.transpose(pp[...])[:M])
        pt[0:M, :] = ph
        pt[M : 2 * M, :] = plo

        def update(i, _):
            at = pl.ds(pl.multiple_of((b + 1) * 1024 + i * CH, CH), CH)
            v = zz[:, at]
            d = v - jnp.sum(v, axis=0, keepdims=True) * (1.0 / M)
            hi, lo = split(d)
            for q in range(8):
                w = jnp.broadcast_to(mask[8 * b + q : 8 * b + q + 1, at], (16, CH)).astype(BF)
                for g in range(5):
                    rr = slice(80 * q + 16 * g, 80 * q + 16 * g + 16)
                    dh[rr, :] = hi[16 * g : 16 * g + 16] * w
                    dl[rr, :] = lo[16 * g : 16 * g + 16] * w
            both = mm(pt[...], dh[...], NN)
            rest = mm(pt[0:M, :], dl[...], NN)
            zz[:, at] = v + (both[0:M] + (both[M : 2 * M] + rest))
            return 0

        lax.fori_loop(0, (WIDE - (b + 1) * 1024) // CH, update, 0)

    true = iota((M, M), 0)
    tk = true // MLOC
    ti = lax.rem(true, MLOC)
    place = jnp.where(ti < 8, 8 * tk + ti, 64 + 2 * tk + ti - 8)
    perm = jnp.where(iota((M, M), 1) == place, 1.0, 0.0).astype(BF)
    th, tl = split(zz[:, NB * 1024 :])
    tp[0:M, :] = mm(perm, th, NN).astype(BF)
    tp[M : 2 * M, :] = mm(perm, tl, NN).astype(BF)
    sp[...] = jnp.zeros_like(sp)
    for t in range(NT):
        at = slice(TILE * t, TILE * t + TILE)
        for kk in range(NK):
            sp[16 * kk : 16 * kk + MLOC, :] = s_ref[kk, :, at]
        hi, lo = split(sp[...])
        maps = tp[:, 128 * t : 128 * t + 128]
        both = mm(maps, hi, NN)
        rest = mm(maps[0:M], lo, NN)
        out_ref[:, at] = both[0:M] + (both[M : 2 * M] + rest)


def window_call(g, s, mk):
    return pl.pallas_call(
        window_kernel,
        out_shape=jax.ShapeDtypeStruct((M, CELLS), F32),
        in_specs=[vm(), vm(), vm()],
        out_specs=vm(),
        scratch_shapes=[
            pltpu.VMEM((M, WIDE), F32),
            pltpu.VMEM((32, WIDE), F32),
            pltpu.VMEM((8, NB * 1024), F32),
            pltpu.VMEM((640, 128), F32),
            pltpu.VMEM((2 * M, 640), BF),
            pltpu.VMEM((640, CH), BF),
            pltpu.VMEM((640, CH), BF),
            pltpu.VMEM((128, TILE), F32),
            pltpu.VMEM((2 * M, NT * 128), BF),
        ],
        name="window",
    )(g, s, mk)


def local(state, obs_value, obs_var, owner, tile_of, offsets, accept, loc_mask):
    places = jnp.transpose(offsets, (0, 2, 1))
    g, s = exchange_call(
        owner[:, :, 0], tile_of, places, accept, obs_value, obs_var, loc_mask, state
    )
    return window_call(g.reshape(NC, 128, 128), s, loc_mask)


def solution(mesh):
    return jax.shard_map(
        local,
        mesh=mesh,
        in_specs=(
            P("mem", "cols"),
            P(None, "cols"),
            P(None, "cols"),
            P(None, "cols", None),
            P(None, "cols"),
            P(None, "cols", None),
            P(None, "cols"),
            P(("cols", "mem"), None, None),
        ),
        out_specs=P(None, ("cols", "mem")),
        check_vma=False,
    )
```

```python
import jax
import jax.numpy as jnp
from jax import lax
from jax.experimental import pallas as pl
from jax.experimental.pallas import tpu as pltpu
from jax.sharding import PartitionSpec as P

epsilon = 1e-05
MESH = pl.DeviceIdType.MESH
F32 = jnp.float32
BF = jnp.bfloat16
I32 = jnp.int32

NB = 4
NC = 32
NK = 8
MLOC = 10
M = 80
NY = 4
NZ = 8
TILE = 512
NT = 8
CELLS = 4096
RA = 40
RB = 24


def vm():
    return pl.BlockSpec(memory_space=pltpu.VMEM)


def sm():
    return pl.BlockSpec(memory_space=pltpu.SMEM)


def hbm():
    return pl.BlockSpec(memory_space=pl.ANY)


def iota(shape, axis):
    return lax.broadcasted_iota(I32, shape, axis)


def split(v):
    hi = v.astype(BF)
    lo = (v - hi.astype(F32)).astype(BF)
    return hi, lo


def mm(a, b, dims):
    return lax.dot_general(a, b, (dims, ((), ())), preferred_element_type=F32)


NN = ((1,), (0,))
NT_ = ((1,), (1,))
TN = ((0,), (0,))
def send(src, dst, ssem, rsem, dev):
    cp = pltpu.make_async_remote_copy(
        src_ref=src, dst_ref=dst, send_sem=ssem, recv_sem=rsem, device_id=dev, device_id_type=MESH
    )
    cp.start()
    return cp


FAR = sorted(
    ((dy, dz) for dy in range(NY) for dz in range(NZ) if dy + dz > 0),
    key=lambda o: -(min(o[0], NY - o[0]) + min(o[1], NZ - o[1])),
)
FAR_K = (4, 3, 5, 2, 6, 1, 7)
EARLY = (4, 2, 7, 1)
LATE = (5, 3, 6)


def exchange_kernel(
    ow, ti, of, ac, va, vr, lm, st, g_ref, s_ref,
    stv, tiled, fi, fl, mv, mrow, rr, rsm, mks, xs, zrow, rz,
    ls, own, cs, ms, mr, ks, kr, ss, rs, xss, xsr, a1s, a1r, b1s, b1r, a2s, a2r, b2s, b2r,
    pas, par, pbs, pbr, pcs, pcr, pds, pdr, ts, tr,
):
    c = lax.axis_index("cols")
    k = lax.axis_index("mem")
    y = c // NZ
    z = lax.rem(c, NZ)
    core = lax.rem(k, 2)
    quad = lax.rem(k, 4)
    bar = pltpu.get_barrier_semaphore()
    cols = [(dy * NZ + dz, lax.rem(y + dy, NY) * NZ + lax.rem(z + dz, NZ)) for dy, dz in FAR]
    for d, p in cols:
        pl.semaphore_signal(bar, inc=1, device_id=(p, k), device_id_type=MESH)
    for d in FAR_K:
        pl.semaphore_signal(bar, inc=1, device_id=(c, lax.rem(k + d, NK)), device_id_type=MESH)
    load = pltpu.make_async_copy(st, stv, ls)
    load.start()
    mv[...] = jnp.zeros_like(mv)
    tiles = ti[...] * TILE
    cells = [tiles + of[:, p, :] for p in range(4)]
    places = [ow[...], cells[0] + (cells[1] << 15), cells[2] + (cells[3] << 15)]
    fields = [ac[...].astype(F32), va[...], vr[...]]
    for b in range(NB):
        at = slice(32 * b, 32 * b + 32)
        for f in range(3):
            fi[f : f + 1, at] = places[f][b : b + 1, :]
            fl[f : f + 1, at] = fields[f][b : b + 1, :]
        mv[:, 8 * b : 8 * b + 8] = lm[:, b, :].astype(F32)
    r128 = iota((128, 128), 0)
    c128 = iota((128, 128), 1)
    lane32 = iota((NC, 128), 1)
    within = lane32 & 31
    hoti = jnp.where(iota((NC, 128), 0) == fi[0:1, :], 1, 0)
    seen = hoti
    for h in (1, 2, 4, 8, 16):
        seen = seen + jnp.where(within >= h, pltpu.roll(seen, h, 1), 0)
    slots = jnp.zeros((NC, 128), I32)
    for r in range(2):
        for w in range(2):
            v = jnp.where((hoti == 1) & (seen == r + 1), fi[w + 1 : w + 2, :], 0)
            for h in (1, 2, 4, 8, 16):
                v = v + pltpu.roll(v, 128 - h, 1)
            for p, cell in ((2 * w, v & 32767), (2 * w + 1, (v >> 15) & 32767)):
                for f, word in ((p, cell >> 7), (p + 4, cell & 127)):
                    spot = 8 * r + f
                    word = word if spot == 0 else pltpu.roll(word, spot, 1)
                    slots = jnp.where(within == spot, word, slots)
    mrow[...] = slots.reshape(NC, 1, 128)
    hot = hoti.astype(F32)
    rank = jnp.sum((hoti * (seen - 1)).astype(F32), axis=0, keepdims=True)
    load.wait()
    for t in range(NK * CELLS // 128):
        tiled[t] = stv[:, 128 * t : 128 * t + 128]
    pl.semaphore_wait(bar, NC - 1 + NK - 1)

    ask = []
    for d, p in cols:
        ask.append(send(mrow.at[p], rr.at[c], ms.at[d], mr.at[d], (p, k)))
    maps = []
    for d in FAR_K:
        maps.append(send(mv, mks.at[k], ks.at[d], kr.at[d], (c, lax.rem(k + d, NK))))
    rr[c] = mrow[c]
    mks[k] = mv[...]
    def move(d):
        p = lax.rem(k + d, NK)
        part = stv.at[:, pl.ds(pl.multiple_of(p * CELLS, CELLS), CELLS)]
        return send(part, s_ref.at[k], ts.at[d], tr.at[d], (c, p))

    moves = [move(d) for d in EARLY]
    keep = pltpu.make_async_copy(
        stv.at[:, pl.ds(pl.multiple_of(k * CELLS, CELLS), CELLS)], s_ref.at[k], own
    )
    keep.start()
    for cp in maps:
        cp.wait()
    pick = lax.rem(c128, 16) - 10
    chosen = jnp.where((pick >= 0) & (pick < 3) & (r128 == 3 * k + pick), 1.0, 0.0)
    table = mm(mks[...].reshape(64, 128).astype(BF), chosen.astype(BF), NN).astype(BF)
    for cp in ask:
        cp.wait()
    scal = pltpu.make_async_copy(rr, rsm, cs)
    scal.start()
    got = rr[...].reshape(NC, 128)
    extra = jnp.zeros((NC, 128), F32)
    for q in range(8):
        word = 32 * (q // 2) + 8 * (q % 2)
        tile = got[:, word : word + 1] >> 2
        at_tile = jnp.where(iota((NC, 64), 1) == tile, 1.0, 0.0).astype(BF)
        extra = jnp.where(lane32 // 16 == q, mm(at_tile, table, NN), extra)
    scal.wait()
    lane = iota((MLOC, 128), 1)

    def priors(i, accs):
        here = lane == i
        out = []
        for q in range(8):
            v = jnp.zeros((MLOC, 128), F32)
            word = 32 * (q // 2) + 8 * (q % 2)
            for p in range(4):
                hit = lane == rsm[i, 0, word + 4 + p]
                v = v + jnp.where(hit, tiled[rsm[i, 0, word + p]], 0.0)
            out.append(jnp.where(here, jnp.sum(v, axis=1, keepdims=True), accs[q]))
        return tuple(out)

    accs = lax.fori_loop(0, NC, priors, tuple(jnp.zeros((MLOC, 128), F32) for _ in range(8)), unroll=4)
    xs[...] = jnp.zeros_like(xs)
    for q in range(8):
        xs[16 * q : 16 * q + MLOC, :] = accs[q] * 0.25
    zr = jnp.transpose(xs[...])[:NC] + extra
    zrow[...] = zr.reshape(NC, 1, 128)
    back = []
    for d, p in cols:
        back.append(send(zrow.at[p], rz.at[c], ss.at[d], rs.at[d], (p, k)))
    rz[c] = zrow[c]
    for cp in back:
        cp.wait()
    full = lax.dot_general(
        rz[...].reshape(NC, 128), hot, (TN, ((), ())),
        precision=lax.Precision.HIGHEST, preferred_element_type=F32,
    )
    batch = iota((1, 128), 1) // 32
    blk = jnp.zeros((16, 128), F32)
    for q in range(8):
        mine = (batch == q // 2) & (rank == float(q % 2))
        blk = blk + jnp.where(mine, full[16 * q : 16 * q + 16, :], 0.0)
    row16 = iota((16, 128), 0)
    for j in range(3):
        blk = jnp.where(row16 == 13 + j, fl[j : j + 1, :], blk)
    turned = blk
    around = lax.rem(z, 4)
    for j in range(1, 4):
        turned = jnp.where(around == j, pltpu.roll(blk, 32 * j, 1), turned)
    second = turned[8:16]
    placed = second
    for j in range(1, 4):
        placed = jnp.where(quad == j, pltpu.roll(second, 2 * j, 0), placed)
    r0 = pl.multiple_of(16 * k, 16)
    g_ref[y, z, pl.ds(r0, 8), :] = turned[0:8]
    g_ref[y, z, pl.ds(pl.multiple_of(r0 + 8, 8), 8), :] = placed
    block = g_ref.at[y, z, pl.ds(r0, 16), :]
    step = []
    for d in FAR_K:
        step.append(send(block, block, xss.at[d], xsr.at[d], (c, lax.rem(k + d, NK))))
    for cp in step:
        cp.wait()
    moves += [move(d) for d in LATE]
    ra = pl.multiple_of(64 * core, 8)
    rb = pl.multiple_of(64 * core + RA, 8)
    mate = (c, k + 1 - 2 * core)
    a1 = g_ref.at[y, z, pl.ds(ra, RA), :]
    b1 = g_ref.at[y, z, pl.ds(rb, RB), :]
    first_a = []
    first_b = []
    for d in range(1, NZ):
        first_a.append(send(a1, a1, a1s.at[d], a1r.at[d], (y * NZ + lax.rem(z + d, NZ), k)))
    for d in range(1, NY):
        first_b.append(send(b1, b1, b1s.at[d], b1r.at[d], (lax.rem(y + d, NY) * NZ + z, k)))
    for cp in first_b:
        cp.wait()
    b2 = g_ref.at[:, z, pl.ds(rb, RB), :]
    second_b = []
    for d in range(1, NZ):
        second_b.append(send(b2, b2, b2s.at[d], b2r.at[d], (y * NZ + lax.rem(z + d, NZ), k)))
    for cp in first_a:
        cp.wait()
    a2 = g_ref.at[y, :, pl.ds(ra, RA), :]
    second_a = []
    for d in range(1, NY):
        second_a.append(send(a2, a2, a2s.at[d], a2r.at[d], (lax.rem(y + d, NY) * NZ + z, k)))
    pair = []
    for d in range(1, NY):
        piece = g_ref.at[lax.rem(y + d, NY), z, pl.ds(rb, RB), :]
        pair.append(send(piece, piece, pas.at[d], par.at[d], mate))
    for d in range(1, NZ):
        piece = g_ref.at[y, lax.rem(z + d, NZ), pl.ds(ra, RA), :]
        pair.append(send(piece, piece, pbs.at[d], pbr.at[d], mate))
    for d in range(1, NZ):
        second_b[d - 1].wait_recv()
        piece = g_ref.at[:, lax.rem(z + NZ - d, NZ), pl.ds(rb, RB), :]
        pair.append(send(piece, piece, pcs.at[d], pcr.at[d], mate))
    for d in range(1, NY):
        second_a[d - 1].wait_recv()
        piece = g_ref.at[lax.rem(y + NY - d, NY), :, pl.ds(ra, RA), :]
        pair.append(send(piece, piece, pds.at[d], pdr.at[d], mate))
    for cp in second_b + second_a:
        cp.wait_send()
    keep.wait()
    for cp in moves + pair:
        cp.wait()


def exchange_call(ow, ti, of, ac, va, vr, lm, st):
    dma = pltpu.SemaphoreType.DMA
    row = pltpu.VMEM((NC, 1, 128), F32)
    irow = pltpu.VMEM((NC, 1, 128), I32)
    return pl.pallas_call(
        exchange_kernel,
        out_shape=(
            jax.ShapeDtypeStruct((NY, NZ, 128, 128), F32),
            jax.ShapeDtypeStruct((NK, MLOC, CELLS), F32),
        ),
        in_specs=[vm()] * 7 + [hbm()],
        out_specs=(vm(), hbm()),
        scratch_shapes=[
            pltpu.VMEM((MLOC, NK * CELLS), F32),
            pltpu.VMEM((NK * CELLS // 128, MLOC, 128), F32),
            pltpu.VMEM((8, 128), I32),
            pltpu.VMEM((8, 128), F32),
            pltpu.VMEM((8, 128), F32),
            irow, irow,
            pltpu.SMEM((NC, 1, 128), I32),
            pltpu.VMEM((NK, 8, 128), F32),
            pltpu.VMEM((128, 128), F32),
            row, row,
            dma(()), dma(()), dma(()),
            dma((NC,)), dma((NC,)), dma((NK,)), dma((NK,)),
            dma((NC,)), dma((NC,)), dma((NK,)), dma((NK,)),
            dma((NZ,)), dma((NZ,)), dma((NY,)), dma((NY,)),
            dma((NY,)), dma((NY,)), dma((NZ,)), dma((NZ,)),
            dma((NY,)), dma((NY,)), dma((NZ,)), dma((NZ,)),
            dma((NZ,)), dma((NZ,)), dma((NY,)), dma((NY,)),
            dma((NK,)), dma((NK,)),
        ],
        compiler_params=pltpu.CompilerParams(collective_id=0, has_side_effects=True),
        name="exchange",
    )(ow, ti, of, ac, va, vr, lm, st)


WIDE = NB * 1024 + NT * 128
CH = 512


def extra_row(k, x):
    return 16 * k + 8 + (2 * (k % 4) + 2 + x) % 8


def window_kernel(g_hbm, s_hbm, mk_ref, out, zz, mask, val, pp, pt, dh, dl, sp, tp, g_ref, s_ref, out_ref, gsem, ssem, osem):
    gets = [pltpu.make_async_copy(g_hbm.at[pl.ds(4 * q, 4)], g_ref.at[pl.ds(4 * q, 4)], gsem.at[q]) for q in range(8)]
    for cp in gets:
        cp.start()
    state = pltpu.make_async_copy(s_hbm, s_ref, ssem)
    state.start()
    lane_group = iota((128, 128), 1) // 32
    sub = iota((8, 128), 0) // 2

    def assemble(blk, _):
        part = pl.ds(4 * blk, 4)
        pltpu.make_async_copy(g_hbm.at[part], g_ref.at[part], gsem.at[blk]).wait()
        parts = [g_ref[4 * blk + u] for u in range(4)]
        for b in range(NB):
            v = parts[3]
            for u in range(3):
                v = jnp.where(lane_group == (b + u) % 4, parts[u], v)
            lanes = pl.ds(pl.multiple_of(b * 1024 + blk * 128, 128), 128)
            for kk in range(NK):
                zz[8 * kk : 8 * kk + 8, lanes] = v[16 * kk : 16 * kk + 8]
            for h in range(2):
                t = v[16 * (4 * h) + 8 : 16 * (4 * h) + 16]
                for j in range(1, 4):
                    kk = 4 * h + j
                    t = jnp.where(sub == j, v[16 * kk + 8 : 16 * kk + 16], t)
                zz[64 + 8 * h : 72 + 8 * h, lanes] = t
            for e in range(8 * b):
                r = extra_row(e // 3, e % 3)
                mask[e : e + 1, lanes] = v[r : r + 1]
            for j in range(3):
                r = extra_row(0, 3 + j)
                val[j : j + 1, lanes] = v[r : r + 1]
        return 0

    lax.fori_loop(0, 8, assemble, 0)
    n = lax.rem(iota((M, NT * 128), 1), 128)
    kk = n // 16
    ii = lax.rem(n, 16)
    place = jnp.where(ii < 8, 8 * kk + ii, 64 + 2 * kk + ii - 8)
    unit = (iota((M, NT * 128), 0) == place) & (ii < MLOC)
    zz[:, NB * 1024 :] = jnp.where(unit, 1.0, 0.0)
    grow = jnp.where(iota((8, NT * 128), 0) == iota((8, NT * 128), 1) // 128, 1.0, 0.0)
    for b in range(NB):
        mask[8 * b : 8 * b + 8, NB * 1024 :] = mm(mk_ref[:, b, :].astype(F32), grow, TN)
    pp[...] = jnp.zeros_like(pp)

    for b in range(NB):
        lanes = slice(b * 1024, b * 1024 + 1024)
        prior = zz[:, lanes]
        accepted = val[0:1, lanes]
        observed = val[1:2, lanes]
        noise = val[2:3, lanes]
        mean = jnp.sum(prior, axis=0, keepdims=True) / M
        dev = prior - mean
        var = jnp.sum(dev * dev, axis=0, keepdims=True) / (M - 1) + epsilon
        den = var + noise
        shift = var / den * (observed - mean)
        factor = jnp.sqrt(noise / den) - 1.0
        inc = accepted * (shift + factor * dev)
        scl = dev / ((M - 1) * var)
        ih, il = split(inc)
        sh, sl = split(scl)
        for q in range(8):
            w = slice(128 * q, 128 * q + 128)
            prod = mm(sh[:, w], ih[:, w], NT_) + mm(sh[:, w], il[:, w], NT_) + mm(sl[:, w], ih[:, w], NT_)
            pp[80 * q : 80 * q + 80, 0:80] = prod
        ph, plo = split(jnp.transpose(pp[...])[:M])
        pt[0:M, :] = ph
        pt[M : 2 * M, :] = plo

        def update(i, _):
            at = pl.ds(pl.multiple_of((b + 1) * 1024 + i * CH, CH), CH)
            v = zz[:, at]
            d = v - jnp.sum(v, axis=0, keepdims=True) * (1.0 / M)
            hi, lo = split(d)
            for q in range(8):
                w = jnp.broadcast_to(mask[8 * b + q : 8 * b + q + 1, at], (16, CH)).astype(BF)
                for g in range(5):
                    rr = slice(80 * q + 16 * g, 80 * q + 16 * g + 16)
                    dh[rr, :] = hi[16 * g : 16 * g + 16] * w
                    dl[rr, :] = lo[16 * g : 16 * g + 16] * w
            both = mm(pt[...], dh[...], NN)
            rest = mm(pt[0:M, :], dl[...], NN)
            zz[:, at] = v + (both[0:M] + (both[M : 2 * M] + rest))
            return 0

        lax.fori_loop(0, (WIDE - (b + 1) * 1024) // CH, update, 0)

    true = iota((M, M), 0)
    tk = true // MLOC
    ti = lax.rem(true, MLOC)
    place = jnp.where(ti < 8, 8 * tk + ti, 64 + 2 * tk + ti - 8)
    perm = jnp.where(iota((M, M), 1) == place, 1.0, 0.0).astype(BF)
    th, tl = split(zz[:, NB * 1024 :])
    tp[0:M, :] = mm(perm, th, NN).astype(BF)
    tp[M : 2 * M, :] = mm(perm, tl, NN).astype(BF)
    sp[...] = jnp.zeros_like(sp)
    state.wait()
    puts = []
    for t in range(NT):
        at = slice(TILE * t, TILE * t + TILE)
        for kk in range(NK):
            sp[16 * kk : 16 * kk + MLOC, :] = s_ref[kk, :, at]
        hi, lo = split(sp[...])
        maps = tp[:, 128 * t : 128 * t + 128]
        both = mm(maps, hi, NN)
        rest = mm(maps[0:M], lo, NN)
        out_ref[:, at] = both[0:M] + (both[M : 2 * M] + rest)
        puts.append(pltpu.make_async_copy(out_ref.at[:, at], out.at[:, at], osem.at[t]))
        puts[-1].start()
    for cp in puts:
        cp.wait()


def window_call(g, s, mk):
    return pl.pallas_call(
        window_kernel,
        out_shape=jax.ShapeDtypeStruct((M, CELLS), F32),
        in_specs=[hbm(), hbm(), vm()],
        out_specs=hbm(),
        scratch_shapes=[
            pltpu.VMEM((M, WIDE), F32),
            pltpu.VMEM((32, WIDE), F32),
            pltpu.VMEM((8, NB * 1024), F32),
            pltpu.VMEM((640, 128), F32),
            pltpu.VMEM((2 * M, 640), BF),
            pltpu.VMEM((640, CH), BF),
            pltpu.VMEM((640, CH), BF),
            pltpu.VMEM((128, TILE), F32),
            pltpu.VMEM((2 * M, NT * 128), BF),
            pltpu.VMEM((NC, 128, 128), F32),
            pltpu.VMEM((NK, MLOC, CELLS), F32),
            pltpu.VMEM((M, CELLS), F32),
            pltpu.SemaphoreType.DMA((8,)),
            pltpu.SemaphoreType.DMA(()),
            pltpu.SemaphoreType.DMA((NT,)),
        ],
        name="window",
    )(g, s, mk)


def local(state, obs_value, obs_var, owner, tile_of, offsets, accept, loc_mask):
    places = jnp.transpose(offsets, (0, 2, 1))
    g, s = exchange_call(
        owner[:, :, 0], tile_of, places, accept, obs_value, obs_var, loc_mask, state
    )
    return window_call(g.reshape(NC, 128, 128), s, loc_mask)


def solution(mesh):
    return jax.shard_map(
        local,
        mesh=mesh,
        in_specs=(
            P("mem", "cols"),
            P(None, "cols"),
            P(None, "cols"),
            P(None, "cols", None),
            P(None, "cols"),
            P(None, "cols", None),
            P(None, "cols"),
            P(("cols", "mem"), None, None),
        ),
        out_specs=P(None, ("cols", "mem")),
        check_vma=False,
    )
```

```python
import jax
import jax.numpy as jnp
from jax import lax
from jax.experimental import pallas as pl
from jax.experimental.pallas import tpu as pltpu
from jax.sharding import PartitionSpec as P

epsilon = 1e-05
MESH = pl.DeviceIdType.MESH
F32 = jnp.float32
BF = jnp.bfloat16
I32 = jnp.int32

NB = 4
NC = 32
NK = 8
MLOC = 10
M = 80
NY = 4
NZ = 8
TILE = 512
NT = 8
CELLS = 4096
RA = 40
RB = 24


def vm():
    return pl.BlockSpec(memory_space=pltpu.VMEM)


def sm():
    return pl.BlockSpec(memory_space=pltpu.SMEM)


def hbm():
    return pl.BlockSpec(memory_space=pl.ANY)


def iota(shape, axis):
    return lax.broadcasted_iota(I32, shape, axis)


def split(v):
    hi = v.astype(BF)
    lo = (v - hi.astype(F32)).astype(BF)
    return hi, lo


def mm(a, b, dims):
    return lax.dot_general(a, b, (dims, ((), ())), preferred_element_type=F32)


NN = ((1,), (0,))
NT_ = ((1,), (1,))
TN = ((0,), (0,))
def send(src, dst, ssem, rsem, dev):
    cp = pltpu.make_async_remote_copy(
        src_ref=src, dst_ref=dst, send_sem=ssem, recv_sem=rsem, device_id=dev, device_id_type=MESH
    )
    cp.start()
    return cp


FAR = sorted(
    ((dy, dz) for dy in range(NY) for dz in range(NZ) if dy + dz > 0),
    key=lambda o: -(min(o[0], NY - o[0]) + min(o[1], NZ - o[1])),
)
FAR_K = (4, 3, 5, 2, 6, 1, 7)
NEAR_Y = (1, 3, 2)
NEAR_Z = (1, 7, 2, 6, 3, 5, 4)
EARLY = (4, 2, 7, 1)
LATE = (5, 3, 6)


def exchange_kernel(
    ow, ti, of, ac, va, vr, lm, st, g_ref, s_ref,
    stv, tiled, fi, fl, mv, mrow, rr, rsm, mks, xs, zrow, rz,
    ls, own, cs, ms, mr, ks, kr, ss, rs, xss, xsr, a1s, a1r, b1s, b1r, a2s, a2r, b2s, b2r,
    pas, par, ts, tr,
):
    c = lax.axis_index("cols")
    k = lax.axis_index("mem")
    y = c // NZ
    z = lax.rem(c, NZ)
    core = lax.rem(k, 2)
    quad = lax.rem(k, 4)
    bar = pltpu.get_barrier_semaphore()
    cols = [(dy * NZ + dz, lax.rem(y + dy, NY) * NZ + lax.rem(z + dz, NZ)) for dy, dz in FAR]
    for d, p in cols:
        pl.semaphore_signal(bar, inc=1, device_id=(p, k), device_id_type=MESH)
    for d in FAR_K:
        pl.semaphore_signal(bar, inc=1, device_id=(c, lax.rem(k + d, NK)), device_id_type=MESH)
    load = pltpu.make_async_copy(st, stv, ls)
    load.start()
    mv[...] = jnp.zeros_like(mv)
    tiles = ti[...] * TILE
    cells = [tiles + of[:, p, :] for p in range(4)]
    places = [ow[...], cells[0] + (cells[1] << 15), cells[2] + (cells[3] << 15)]
    fields = [ac[...].astype(F32), va[...], vr[...]]
    for b in range(NB):
        at = slice(32 * b, 32 * b + 32)
        for f in range(3):
            fi[f : f + 1, at] = places[f][b : b + 1, :]
            fl[f : f + 1, at] = fields[f][b : b + 1, :]
        mv[:, 8 * b : 8 * b + 8] = lm[:, b, :].astype(F32)
    r128 = iota((128, 128), 0)
    c128 = iota((128, 128), 1)
    lane32 = iota((NC, 128), 1)
    within = lane32 & 31
    hoti = jnp.where(iota((NC, 128), 0) == fi[0:1, :], 1, 0)
    seen = hoti
    for h in (1, 2, 4, 8, 16):
        seen = seen + jnp.where(within >= h, pltpu.roll(seen, h, 1), 0)
    slots = jnp.zeros((NC, 128), I32)
    for r in range(2):
        for w in range(2):
            v = jnp.where((hoti == 1) & (seen == r + 1), fi[w + 1 : w + 2, :], 0)
            for h in (1, 2, 4, 8, 16):
                v = v + pltpu.roll(v, 128 - h, 1)
            for p, cell in ((2 * w, v & 32767), (2 * w + 1, (v >> 15) & 32767)):
                for f, word in ((p, cell >> 7), (p + 4, cell & 127)):
                    spot = 8 * r + f
                    word = word if spot == 0 else pltpu.roll(word, spot, 1)
                    slots = jnp.where(within == spot, word, slots)
    mrow[...] = slots.reshape(NC, 1, 128)
    hot = hoti.astype(F32)
    rank = jnp.sum((hoti * (seen - 1)).astype(F32), axis=0, keepdims=True)
    load.wait()
    for t in range(NK * CELLS // 128):
        tiled[t] = stv[:, 128 * t : 128 * t + 128]
    pl.semaphore_wait(bar, NC - 1 + NK - 1)

    ask = []
    for d, p in cols:
        ask.append(send(mrow.at[p], rr.at[c], ms.at[d], mr.at[d], (p, k)))
    maps = []
    for d in FAR_K:
        maps.append(send(mv, mks.at[k], ks.at[d], kr.at[d], (c, lax.rem(k + d, NK))))
    rr[c] = mrow[c]
    mks[k] = mv[...]
    def move(d):
        p = lax.rem(k + d, NK)
        part = stv.at[:, pl.ds(pl.multiple_of(p * CELLS, CELLS), CELLS)]
        return send(part, s_ref.at[k], ts.at[d], tr.at[d], (c, p))

    moves = [move(d) for d in EARLY]
    keep = pltpu.make_async_copy(
        stv.at[:, pl.ds(pl.multiple_of(k * CELLS, CELLS), CELLS)], s_ref.at[k], own
    )
    keep.start()
    for cp in maps:
        cp.wait()
    pick = lax.rem(c128, 16) - 10
    chosen = jnp.where((pick >= 0) & (pick < 3) & (r128 == 3 * k + pick), 1.0, 0.0)
    table = mm(mks[...].reshape(64, 128).astype(BF), chosen.astype(BF), NN).astype(BF)
    for cp in ask:
        cp.wait()
    scal = pltpu.make_async_copy(rr, rsm, cs)
    scal.start()
    got = rr[...].reshape(NC, 128)
    extra = jnp.zeros((NC, 128), F32)
    for q in range(8):
        word = 32 * (q // 2) + 8 * (q % 2)
        tile = got[:, word : word + 1] >> 2
        at_tile = jnp.where(iota((NC, 64), 1) == tile, 1.0, 0.0).astype(BF)
        extra = jnp.where(lane32 // 16 == q, mm(at_tile, table, NN), extra)
    scal.wait()
    lane = iota((MLOC, 128), 1)

    def priors(i, accs):
        here = lane == i
        out = []
        for q in range(8):
            v = jnp.zeros((MLOC, 128), F32)
            word = 32 * (q // 2) + 8 * (q % 2)
            for p in range(4):
                hit = lane == rsm[i, 0, word + 4 + p]
                v = v + jnp.where(hit, tiled[rsm[i, 0, word + p]], 0.0)
            out.append(jnp.where(here, jnp.sum(v, axis=1, keepdims=True), accs[q]))
        return tuple(out)

    accs = lax.fori_loop(0, NC, priors, tuple(jnp.zeros((MLOC, 128), F32) for _ in range(8)), unroll=True)
    xs[...] = jnp.zeros_like(xs)
    for q in range(8):
        xs[16 * q : 16 * q + MLOC, :] = accs[q] * 0.25
    zr = jnp.transpose(xs[...])[:NC] + extra
    zrow[...] = zr.reshape(NC, 1, 128)
    back = []
    for d, p in cols:
        back.append(send(zrow.at[p], rz.at[c], ss.at[d], rs.at[d], (p, k)))
    rz[c] = zrow[c]
    for cp in back:
        cp.wait()
    full = lax.dot_general(
        rz[...].reshape(NC, 128), hot, (TN, ((), ())),
        precision=lax.Precision.HIGHEST, preferred_element_type=F32,
    )
    batch = iota((1, 128), 1) // 32
    blk = jnp.zeros((16, 128), F32)
    for q in range(8):
        mine = (batch == q // 2) & (rank == float(q % 2))
        blk = blk + jnp.where(mine, full[16 * q : 16 * q + 16, :], 0.0)
    row16 = iota((16, 128), 0)
    for j in range(3):
        blk = jnp.where(row16 == 13 + j, fl[j : j + 1, :], blk)
    turned = blk
    around = lax.rem(z, 4)
    for j in range(1, 4):
        turned = jnp.where(around == j, pltpu.roll(blk, 32 * j, 1), turned)
    second = turned[8:16]
    placed = second
    for j in range(1, 4):
        placed = jnp.where(quad == j, pltpu.roll(second, 2 * j, 0), placed)
    r0 = pl.multiple_of(16 * k, 16)
    g_ref[y, z, pl.ds(r0, 8), :] = turned[0:8]
    g_ref[y, z, pl.ds(pl.multiple_of(r0 + 8, 8), 8), :] = placed
    block = g_ref.at[y, z, pl.ds(r0, 16), :]
    step = []
    for d in FAR_K:
        step.append(send(block, block, xss.at[d], xsr.at[d], (c, lax.rem(k + d, NK))))
    for cp in step:
        cp.wait()
    ra = pl.multiple_of(64 * core, 8)
    rb = pl.multiple_of(64 * core + RA, 8)
    mate = (c, k + 1 - 2 * core)
    y_at = [lax.rem(y + d, NY) for d in range(NY)]
    z_at = [lax.rem(z + d, NZ) for d in range(NZ)]

    def piece_a(dy, dz):
        return g_ref.at[y_at[(-dy) % NY], z_at[(-dz) % NZ], pl.ds(ra, RA), :]

    def piece_b(dy, dz):
        return g_ref.at[y_at[(-dy) % NY], z_at[(-dz) % NZ], pl.ds(rb, RB), :]

    out_a = {}
    out_b = {}
    pair = []

    def along_y(e):
        piece = piece_a(0, e)
        for d in NEAR_Y:
            out_a[d, e] = send(piece, piece, a2s.at[d, e], a2r.at[d, e], (y_at[d] * NZ + z, k))

    def along_z(e):
        piece = piece_b(e, 0)
        for d in NEAR_Z:
            out_b[d, e] = send(piece, piece, b2s.at[d, e], b2r.at[d, e], (y * NZ + z_at[d], k))

    def to_mate(piece, n, dy, dz):
        pair.append(send(piece, piece, pas.at[n, dy, dz], par.at[n, dy, dz], mate))

    own_a = piece_a(0, 0)
    own_b = piece_b(0, 0)
    first_a = {}
    first_b = {}
    for d in NEAR_Z:
        first_a[d] = send(own_a, own_a, a1s.at[d], a1r.at[d], (y * NZ + z_at[d], k))
    for d in NEAR_Y:
        first_b[d] = send(own_b, own_b, b1s.at[d], b1r.at[d], (y_at[d] * NZ + z, k))
    along_y(0)
    along_z(0)
    moves += [move(d) for d in LATE]
    for kind, e in (("b", 1), ("a", 1), ("b", 3), ("a", 7), ("a", 2), ("b", 2), ("a", 6), ("a", 3), ("a", 5), ("a", 4)):
        if kind == "a":
            first_a[e].wait_recv()
            along_y(e)
            to_mate(piece_a(0, e), 0, 0, e)
        else:
            first_b[e].wait_recv()
            along_z(e)
            to_mate(piece_b(e, 0), 1, e, 0)
    order = [(0, d, e) for d in NEAR_Y for e in range(NZ)] + [(1, e, d) for d in NEAR_Z for e in range(NY)]
    order.sort(key=lambda o: (min(o[1], NY - o[1]) + min(o[2], NZ - o[2])))
    for n, dy, dz in order:
        if n == 0:
            out_a[dy, dz].wait_recv()
            to_mate(piece_a(dy, dz), 0, dy, dz)
        else:
            out_b[dz, dy].wait_recv()
            to_mate(piece_b(dy, dz), 1, dy, dz)
    for group in (first_a, first_b, out_a, out_b):
        for cp in group.values():
            cp.wait_send()
    keep.wait()
    for cp in moves + pair:
        cp.wait()


def exchange_call(ow, ti, of, ac, va, vr, lm, st):
    dma = pltpu.SemaphoreType.DMA
    row = pltpu.VMEM((NC, 1, 128), F32)
    irow = pltpu.VMEM((NC, 1, 128), I32)
    return pl.pallas_call(
        exchange_kernel,
        out_shape=(
            jax.ShapeDtypeStruct((NY, NZ, 128, 128), F32),
            jax.ShapeDtypeStruct((NK, MLOC, CELLS), F32),
        ),
        in_specs=[vm()] * 7 + [hbm()],
        out_specs=(vm(), hbm()),
        scratch_shapes=[
            pltpu.VMEM((MLOC, NK * CELLS), F32),
            pltpu.VMEM((NK * CELLS // 128, MLOC, 128), F32),
            pltpu.VMEM((8, 128), I32),
            pltpu.VMEM((8, 128), F32),
            pltpu.VMEM((8, 128), F32),
            irow, irow,
            pltpu.SMEM((NC, 1, 128), I32),
            pltpu.VMEM((NK, 8, 128), F32),
            pltpu.VMEM((128, 128), F32),
            row, row,
            dma(()), dma(()), dma(()),
            dma((NC,)), dma((NC,)), dma((NK,)), dma((NK,)),
            dma((NC,)), dma((NC,)), dma((NK,)), dma((NK,)),
            dma((NZ,)), dma((NZ,)), dma((NY,)), dma((NY,)),
            dma((NY, NZ)), dma((NY, NZ)), dma((NZ, NY)), dma((NZ, NY)),
            dma((2, NY, NZ)), dma((2, NY, NZ)),
            dma((NK,)), dma((NK,)),
        ],
        compiler_params=pltpu.CompilerParams(collective_id=0, has_side_effects=True),
        name="exchange",
    )(ow, ti, of, ac, va, vr, lm, st)


WIDE = NB * 1024 + NT * 128
CH = 512


def extra_row(k, x):
    return 16 * k + 8 + (2 * (k % 4) + 2 + x) % 8


def window_kernel(g_hbm, s_hbm, mk_ref, out, zz, mask, val, pp, pt, dh, dl, sp, tp, g_ref, s_ref, out_ref, gsem, ssem, osem):
    gets = [pltpu.make_async_copy(g_hbm.at[pl.ds(4 * q, 4)], g_ref.at[pl.ds(4 * q, 4)], gsem.at[q]) for q in range(8)]
    for cp in gets:
        cp.start()
    state = pltpu.make_async_copy(s_hbm, s_ref, ssem)
    state.start()
    lane_group = iota((128, 128), 1) // 32
    sub = iota((8, 128), 0) // 2

    def assemble(blk, _):
        part = pl.ds(4 * blk, 4)
        pltpu.make_async_copy(g_hbm.at[part], g_ref.at[part], gsem.at[blk]).wait()
        parts = [g_ref[4 * blk + u] for u in range(4)]
        for b in range(NB):
            v = parts[3]
            for u in range(3):
                v = jnp.where(lane_group == (b + u) % 4, parts[u], v)
            lanes = pl.ds(pl.multiple_of(b * 1024 + blk * 128, 128), 128)
            for kk in range(NK):
                zz[8 * kk : 8 * kk + 8, lanes] = v[16 * kk : 16 * kk + 8]
            for h in range(2):
                t = v[16 * (4 * h) + 8 : 16 * (4 * h) + 16]
                for j in range(1, 4):
                    kk = 4 * h + j
                    t = jnp.where(sub == j, v[16 * kk + 8 : 16 * kk + 16], t)
                zz[64 + 8 * h : 72 + 8 * h, lanes] = t
            for e in range(8 * b):
                r = extra_row(e // 3, e % 3)
                mask[e : e + 1, lanes] = v[r : r + 1]
            for j in range(3):
                r = extra_row(0, 3 + j)
                val[j : j + 1, lanes] = v[r : r + 1]
        return 0

    lax.fori_loop(0, 8, assemble, 0)
    n = lax.rem(iota((M, NT * 128), 1), 128)
    kk = n // 16
    ii = lax.rem(n, 16)
    place = jnp.where(ii < 8, 8 * kk + ii, 64 + 2 * kk + ii - 8)
    unit = (iota((M, NT * 128), 0) == place) & (ii < MLOC)
    zz[:, NB * 1024 :] = jnp.where(unit, 1.0, 0.0)
    grow = jnp.where(iota((8, NT * 128), 0) == iota((8, NT * 128), 1) // 128, 1.0, 0.0)
    for b in range(NB):
        mask[8 * b : 8 * b + 8, NB * 1024 :] = mm(mk_ref[:, b, :].astype(F32), grow, TN)
    pp[...] = jnp.zeros_like(pp)

    for b in range(NB):
        lanes = slice(b * 1024, b * 1024 + 1024)
        prior = zz[:, lanes]
        accepted = val[0:1, lanes]
        observed = val[1:2, lanes]
        noise = val[2:3, lanes]
        mean = jnp.sum(prior, axis=0, keepdims=True) / M
        dev = prior - mean
        var = jnp.sum(dev * dev, axis=0, keepdims=True) / (M - 1) + epsilon
        den = var + noise
        shift = var / den * (observed - mean)
        factor = jnp.sqrt(noise / den) - 1.0
        inc = accepted * (shift + factor * dev)
        scl = dev / ((M - 1) * var)
        ih, il = split(inc)
        sh, sl = split(scl)
        for q in range(8):
            w = slice(128 * q, 128 * q + 128)
            prod = mm(sh[:, w], ih[:, w], NT_) + mm(sh[:, w], il[:, w], NT_) + mm(sl[:, w], ih[:, w], NT_)
            pp[80 * q : 80 * q + 80, 0:80] = prod
        ph, plo = split(jnp.transpose(pp[...])[:M])
        pt[0:M, :] = ph
        pt[M : 2 * M, :] = plo

        def update(i, _):
            at = pl.ds(pl.multiple_of((b + 1) * 1024 + i * CH, CH), CH)
            v = zz[:, at]
            d = v - jnp.sum(v, axis=0, keepdims=True) * (1.0 / M)
            hi, lo = split(d)
            for q in range(8):
                w = jnp.broadcast_to(mask[8 * b + q : 8 * b + q + 1, at], (16, CH)).astype(BF)
                for g in range(5):
                    rr = slice(80 * q + 16 * g, 80 * q + 16 * g + 16)
                    dh[rr, :] = hi[16 * g : 16 * g + 16] * w
                    dl[rr, :] = lo[16 * g : 16 * g + 16] * w
            both = mm(pt[...], dh[...], NN)
            rest = mm(pt[0:M, :], dl[...], NN)
            zz[:, at] = v + (both[0:M] + (both[M : 2 * M] + rest))
            return 0

        lax.fori_loop(0, (WIDE - (b + 1) * 1024) // CH, update, 0)

    true = iota((M, M), 0)
    tk = true // MLOC
    ti = lax.rem(true, MLOC)
    place = jnp.where(ti < 8, 8 * tk + ti, 64 + 2 * tk + ti - 8)
    perm = jnp.where(iota((M, M), 1) == place, 1.0, 0.0).astype(BF)
    th, tl = split(zz[:, NB * 1024 :])
    tp[0:M, :] = mm(perm, th, NN).astype(BF)
    tp[M : 2 * M, :] = mm(perm, tl, NN).astype(BF)
    sp[...] = jnp.zeros_like(sp)
    state.wait()
    puts = []
    for t in range(NT):
        at = slice(TILE * t, TILE * t + TILE)
        for kk in range(NK):
            sp[16 * kk : 16 * kk + MLOC, :] = s_ref[kk, :, at]
        hi, lo = split(sp[...])
        maps = tp[:, 128 * t : 128 * t + 128]
        both = mm(maps, hi, NN)
        rest = mm(maps[0:M], lo, NN)
        out_ref[:, at] = both[0:M] + (both[M : 2 * M] + rest)
        puts.append(pltpu.make_async_copy(out_ref.at[:, at], out.at[:, at], osem.at[t]))
        puts[-1].start()
    for cp in puts:
        cp.wait()


def window_call(g, s, mk):
    return pl.pallas_call(
        window_kernel,
        out_shape=jax.ShapeDtypeStruct((M, CELLS), F32),
        in_specs=[hbm(), hbm(), vm()],
        out_specs=hbm(),
        scratch_shapes=[
            pltpu.VMEM((M, WIDE), F32),
            pltpu.VMEM((32, WIDE), F32),
            pltpu.VMEM((8, NB * 1024), F32),
            pltpu.VMEM((640, 128), F32),
            pltpu.VMEM((2 * M, 640), BF),
            pltpu.VMEM((640, CH), BF),
            pltpu.VMEM((640, CH), BF),
            pltpu.VMEM((128, TILE), F32),
            pltpu.VMEM((2 * M, NT * 128), BF),
            pltpu.VMEM((NC, 128, 128), F32),
            pltpu.VMEM((NK, MLOC, CELLS), F32),
            pltpu.VMEM((M, CELLS), F32),
            pltpu.SemaphoreType.DMA((8,)),
            pltpu.SemaphoreType.DMA(()),
            pltpu.SemaphoreType.DMA((NT,)),
        ],
        name="window",
    )(g, s, mk)


def local(state, obs_value, obs_var, owner, tile_of, offsets, accept, loc_mask):
    places = jnp.transpose(offsets, (0, 2, 1))
    g, s = exchange_call(
        owner[:, :, 0], tile_of, places, accept, obs_value, obs_var, loc_mask, state
    )
    return window_call(g.reshape(NC, 128, 128), s, loc_mask)


def solution(mesh):
    return jax.shard_map(
        local,
        mesh=mesh,
        in_specs=(
            P("mem", "cols"),
            P(None, "cols"),
            P(None, "cols"),
            P(None, "cols", None),
            P(None, "cols"),
            P(None, "cols", None),
            P(None, "cols"),
            P(("cols", "mem"), None, None),
        ),
        out_specs=P(None, ("cols", "mem")),
        check_vma=False,
    )
```

```python
import jax
import jax.numpy as jnp
from jax import lax
from jax.experimental import pallas as pl
from jax.experimental.pallas import tpu as pltpu
from jax.sharding import PartitionSpec as P

epsilon = 1e-05
MESH = pl.DeviceIdType.MESH
F32 = jnp.float32
BF = jnp.bfloat16
I32 = jnp.int32

NB = 4
NC = 32
NK = 8
MLOC = 10
M = 80
NY = 4
NZ = 8
TILE = 512
NT = 8
CELLS = 4096
RA = 48
RB = 16


def vm():
    return pl.BlockSpec(memory_space=pltpu.VMEM)


def sm():
    return pl.BlockSpec(memory_space=pltpu.SMEM)


def hbm():
    return pl.BlockSpec(memory_space=pl.ANY)


def iota(shape, axis):
    return lax.broadcasted_iota(I32, shape, axis)


def split(v):
    hi = v.astype(BF)
    lo = (v - hi.astype(F32)).astype(BF)
    return hi, lo


def mm(a, b, dims):
    return lax.dot_general(a, b, (dims, ((), ())), preferred_element_type=F32)


NN = ((1,), (0,))
NT_ = ((1,), (1,))
TN = ((0,), (0,))
def send(src, dst, ssem, rsem, dev):
    cp = pltpu.make_async_remote_copy(
        src_ref=src, dst_ref=dst, send_sem=ssem, recv_sem=rsem, device_id=dev, device_id_type=MESH
    )
    cp.start()
    return cp


FAR = sorted(
    ((dy, dz) for dy in range(NY) for dz in range(NZ) if dy + dz > 0),
    key=lambda o: -(min(o[0], NY - o[0]) + min(o[1], NZ - o[1])),
)
FAR_K = (4, 3, 5, 2, 6, 1, 7)
NEAR_Y = (1, 3, 2)
NEAR_Z = (1, 7, 2, 6, 3, 5, 4)
EARLY = (4, 2, 7, 1)
LATE = (5, 3, 6)


def exchange_kernel(
    ow, ti, of, ac, va, vr, lm, st, g_ref, s_ref,
    stv, tiled, fi, fl, mv, mrow, rr, rsm, mks, xs, zrow, rz,
    ls, own, cs, ms, mr, ks, kr, ss, rs, xss, xsr, a1s, a1r, b1s, b1r, a2s, a2r, b2s, b2r,
    pas, par, ts, tr,
):
    c = lax.axis_index("cols")
    k = lax.axis_index("mem")
    y = c // NZ
    z = lax.rem(c, NZ)
    core = lax.rem(k, 2)
    quad = lax.rem(k, 4)
    bar = pltpu.get_barrier_semaphore()
    cols = [(dy * NZ + dz, lax.rem(y + dy, NY) * NZ + lax.rem(z + dz, NZ)) for dy, dz in FAR]
    for d, p in cols:
        pl.semaphore_signal(bar, inc=1, device_id=(p, k), device_id_type=MESH)
    for d in FAR_K:
        pl.semaphore_signal(bar, inc=1, device_id=(c, lax.rem(k + d, NK)), device_id_type=MESH)
    load = pltpu.make_async_copy(st, stv, ls)
    load.start()
    mv[...] = jnp.zeros_like(mv)
    tiles = ti[...] * TILE
    cells = [tiles + of[:, p, :] for p in range(4)]
    places = [ow[...], cells[0] + (cells[1] << 15), cells[2] + (cells[3] << 15)]
    fields = [ac[...].astype(F32), va[...], vr[...]]
    for b in range(NB):
        at = slice(32 * b, 32 * b + 32)
        for f in range(3):
            fi[f : f + 1, at] = places[f][b : b + 1, :]
            fl[f : f + 1, at] = fields[f][b : b + 1, :]
        mv[:, 8 * b : 8 * b + 8] = lm[:, b, :].astype(F32)
    r128 = iota((128, 128), 0)
    c128 = iota((128, 128), 1)
    lane32 = iota((NC, 128), 1)
    within = lane32 & 31
    hoti = jnp.where(iota((NC, 128), 0) == fi[0:1, :], 1, 0)
    seen = hoti
    for h in (1, 2, 4, 8, 16):
        seen = seen + jnp.where(within >= h, pltpu.roll(seen, h, 1), 0)
    slots = jnp.zeros((NC, 128), I32)
    for r in range(2):
        for w in range(2):
            v = jnp.where((hoti == 1) & (seen == r + 1), fi[w + 1 : w + 2, :], 0)
            for h in (1, 2, 4, 8, 16):
                v = v + pltpu.roll(v, 128 - h, 1)
            for p, cell in ((2 * w, v & 32767), (2 * w + 1, (v >> 15) & 32767)):
                for f, word in ((p, cell >> 7), (p + 4, cell & 127)):
                    spot = 8 * r + f
                    word = word if spot == 0 else pltpu.roll(word, spot, 1)
                    slots = jnp.where(within == spot, word, slots)
    mrow[...] = slots.reshape(NC, 1, 128)
    hot = hoti.astype(F32)
    rank = jnp.sum((hoti * (seen - 1)).astype(F32), axis=0, keepdims=True)
    load.wait()
    for t in range(NK * CELLS // 128):
        tiled[t] = stv[:, 128 * t : 128 * t + 128]
    pl.semaphore_wait(bar, NC - 1 + NK - 1)

    ask = []
    for d, p in cols:
        ask.append(send(mrow.at[p], rr.at[c], ms.at[d], mr.at[d], (p, k)))
    maps = []
    for d in FAR_K:
        maps.append(send(mv, mks.at[k], ks.at[d], kr.at[d], (c, lax.rem(k + d, NK))))
    rr[c] = mrow[c]
    mks[k] = mv[...]
    def move(d):
        p = lax.rem(k + d, NK)
        part = stv.at[:, pl.ds(pl.multiple_of(p * CELLS, CELLS), CELLS)]
        return send(part, s_ref.at[k], ts.at[d], tr.at[d], (c, p))

    moves = [move(d) for d in EARLY]
    keep = pltpu.make_async_copy(
        stv.at[:, pl.ds(pl.multiple_of(k * CELLS, CELLS), CELLS)], s_ref.at[k], own
    )
    keep.start()
    for cp in maps:
        cp.wait()
    pick = lax.rem(c128, 16) - 10
    chosen = jnp.where((pick >= 0) & (pick < 3) & (r128 == 3 * k + pick), 1.0, 0.0)
    table = mm(mks[...].reshape(64, 128).astype(BF), chosen.astype(BF), NN).astype(BF)
    for cp in ask:
        cp.wait()
    scal = pltpu.make_async_copy(rr, rsm, cs)
    scal.start()
    got = rr[...].reshape(NC, 128)
    extra = jnp.zeros((NC, 128), F32)
    for q in range(8):
        word = 32 * (q // 2) + 8 * (q % 2)
        tile = got[:, word : word + 1] >> 2
        at_tile = jnp.where(iota((NC, 64), 1) == tile, 1.0, 0.0).astype(BF)
        extra = jnp.where(lane32 // 16 == q, mm(at_tile, table, NN), extra)
    scal.wait()
    lane = iota((MLOC, 128), 1)

    def priors(i, accs):
        here = lane == i
        out = []
        for q in range(8):
            v = jnp.zeros((MLOC, 128), F32)
            word = 32 * (q // 2) + 8 * (q % 2)
            for p in range(4):
                hit = lane == rsm[i, 0, word + 4 + p]
                v = v + jnp.where(hit, tiled[rsm[i, 0, word + p]], 0.0)
            out.append(jnp.where(here, jnp.sum(v, axis=1, keepdims=True), accs[q]))
        return tuple(out)

    accs = lax.fori_loop(0, NC, priors, tuple(jnp.zeros((MLOC, 128), F32) for _ in range(8)), unroll=True)
    xs[...] = jnp.zeros_like(xs)
    for q in range(8):
        xs[16 * q : 16 * q + MLOC, :] = accs[q] * 0.25
    zr = jnp.transpose(xs[...])[:NC] + extra
    zrow[...] = zr.reshape(NC, 1, 128)
    back = []
    for d, p in cols:
        back.append(send(zrow.at[p], rz.at[c], ss.at[d], rs.at[d], (p, k)))
    rz[c] = zrow[c]
    for cp in back:
        cp.wait()
    full = lax.dot_general(
        rz[...].reshape(NC, 128), hot, (TN, ((), ())),
        precision=lax.Precision.HIGHEST, preferred_element_type=F32,
    )
    batch = iota((1, 128), 1) // 32
    blk = jnp.zeros((16, 128), F32)
    for q in range(8):
        mine = (batch == q // 2) & (rank == float(q % 2))
        blk = blk + jnp.where(mine, full[16 * q : 16 * q + 16, :], 0.0)
    row16 = iota((16, 128), 0)
    for j in range(3):
        blk = jnp.where(row16 == 13 + j, fl[j : j + 1, :], blk)
    turned = blk
    around = lax.rem(z, 4)
    for j in range(1, 4):
        turned = jnp.where(around == j, pltpu.roll(blk, 32 * j, 1), turned)
    second = turned[8:16]
    placed = second
    for j in range(1, 4):
        placed = jnp.where(quad == j, pltpu.roll(second, 2 * j, 0), placed)
    r0 = pl.multiple_of(16 * k, 16)
    g_ref[y, z, pl.ds(r0, 8), :] = turned[0:8]
    g_ref[y, z, pl.ds(pl.multiple_of(r0 + 8, 8), 8), :] = placed
    block = g_ref.at[y, z, pl.ds(r0, 16), :]
    step = []
    for d in FAR_K:
        step.append(send(block, block, xss.at[d], xsr.at[d], (c, lax.rem(k + d, NK))))
    for cp in step:
        cp.wait()
    ra = pl.multiple_of(64 * core, 8)
    rb = pl.multiple_of(64 * core + RA, 8)
    mate = (c, k + 1 - 2 * core)
    y_at = [lax.rem(y + d, NY) for d in range(NY)]
    z_at = [lax.rem(z + d, NZ) for d in range(NZ)]

    def piece_a(dy, dz):
        return g_ref.at[y_at[(-dy) % NY], z_at[(-dz) % NZ], pl.ds(ra, RA), :]

    def piece_b(dy, dz):
        return g_ref.at[y_at[(-dy) % NY], z_at[(-dz) % NZ], pl.ds(rb, RB), :]

    out_a = {}
    out_b = {}
    pair = []

    def along_y(e):
        piece = piece_a(0, e)
        for d in NEAR_Y:
            out_a[d, e] = send(piece, piece, a2s.at[d, e], a2r.at[d, e], (y_at[d] * NZ + z, k))

    def along_z(e):
        piece = piece_b(e, 0)
        for d in NEAR_Z:
            out_b[d, e] = send(piece, piece, b2s.at[d, e], b2r.at[d, e], (y * NZ + z_at[d], k))

    def to_mate(piece, n, dy, dz):
        pair.append(send(piece, piece, pas.at[n, dy, dz], par.at[n, dy, dz], mate))

    own_a = piece_a(0, 0)
    own_b = piece_b(0, 0)
    first_a = {}
    first_b = {}
    for d in NEAR_Z:
        first_a[d] = send(own_a, own_a, a1s.at[d], a1r.at[d], (y * NZ + z_at[d], k))
    for d in NEAR_Y:
        first_b[d] = send(own_b, own_b, b1s.at[d], b1r.at[d], (y_at[d] * NZ + z, k))
    along_y(0)
    along_z(0)
    moves += [move(d) for d in LATE]
    for kind, e in (("b", 1), ("a", 1), ("b", 3), ("a", 7), ("a", 2), ("b", 2), ("a", 6), ("a", 3), ("a", 5), ("a", 4)):
        if kind == "a":
            first_a[e].wait_recv()
            along_y(e)
            to_mate(piece_a(0, e), 0, 0, e)
        else:
            first_b[e].wait_recv()
            along_z(e)
            to_mate(piece_b(e, 0), 1, e, 0)
    order = [(0, d, e) for d in NEAR_Y for e in range(NZ)] + [(1, e, d) for d in NEAR_Z for e in range(NY)]
    order.sort(key=lambda o: (min(o[1], NY - o[1]) + min(o[2], NZ - o[2])))
    for n, dy, dz in order:
        if n == 0:
            out_a[dy, dz].wait_recv()
            to_mate(piece_a(dy, dz), 0, dy, dz)
        else:
            out_b[dz, dy].wait_recv()
            to_mate(piece_b(dy, dz), 1, dy, dz)
    for group in (first_a, first_b, out_a, out_b):
        for cp in group.values():
            cp.wait_send()
    keep.wait()
    for cp in moves + pair:
        cp.wait()


def exchange_call(ow, ti, of, ac, va, vr, lm, st):
    dma = pltpu.SemaphoreType.DMA
    row = pltpu.VMEM((NC, 1, 128), F32)
    irow = pltpu.VMEM((NC, 1, 128), I32)
    return pl.pallas_call(
        exchange_kernel,
        out_shape=(
            jax.ShapeDtypeStruct((NY, NZ, 128, 128), F32),
            jax.ShapeDtypeStruct((NK, MLOC, CELLS), F32),
        ),
        in_specs=[vm()] * 7 + [hbm()],
        out_specs=(vm(), hbm()),
        scratch_shapes=[
            pltpu.VMEM((MLOC, NK * CELLS), F32),
            pltpu.VMEM((NK * CELLS // 128, MLOC, 128), F32),
            pltpu.VMEM((8, 128), I32),
            pltpu.VMEM((8, 128), F32),
            pltpu.VMEM((8, 128), F32),
            irow, irow,
            pltpu.SMEM((NC, 1, 128), I32),
            pltpu.VMEM((NK, 8, 128), F32),
            pltpu.VMEM((128, 128), F32),
            row, row,
            dma(()), dma(()), dma(()),
            dma((NC,)), dma((NC,)), dma((NK,)), dma((NK,)),
            dma((NC,)), dma((NC,)), dma((NK,)), dma((NK,)),
            dma((NZ,)), dma((NZ,)), dma((NY,)), dma((NY,)),
            dma((NY, NZ)), dma((NY, NZ)), dma((NZ, NY)), dma((NZ, NY)),
            dma((2, NY, NZ)), dma((2, NY, NZ)),
            dma((NK,)), dma((NK,)),
        ],
        compiler_params=pltpu.CompilerParams(collective_id=0, has_side_effects=True),
        name="exchange",
    )(ow, ti, of, ac, va, vr, lm, st)


MAPS = NT * M
WIDE = NB * 1024 + MAPS
CH = 512


def extra_row(k, x):
    return 16 * k + 8 + (2 * (k % 4) + 2 + x) % 8


def window_kernel(g_hbm, s_hbm, mk_ref, out, zz, mask, val, pp, pt, dh, dl, th, tl, sp, tp, g_ref, s_ref, out_ref, gsem, ssem, osem):
    gets = [pltpu.make_async_copy(g_hbm.at[pl.ds(4 * q, 4)], g_ref.at[pl.ds(4 * q, 4)], gsem.at[q]) for q in range(8)]
    for cp in gets:
        cp.start()
    state = pltpu.make_async_copy(s_hbm, s_ref, ssem)
    state.start()
    lane_group = iota((128, 128), 1) // 32
    sub = iota((8, 128), 0) // 2

    def assemble(blk, _):
        part = pl.ds(4 * blk, 4)
        pltpu.make_async_copy(g_hbm.at[part], g_ref.at[part], gsem.at[blk]).wait()
        parts = [g_ref[4 * blk + u] for u in range(4)]
        for b in range(NB):
            v = parts[3]
            for u in range(3):
                v = jnp.where(lane_group == (b + u) % 4, parts[u], v)
            lanes = pl.ds(pl.multiple_of(b * 1024 + blk * 128, 128), 128)
            for kk in range(NK):
                zz[8 * kk : 8 * kk + 8, lanes] = v[16 * kk : 16 * kk + 8]
            for h in range(2):
                t = v[16 * (4 * h) + 8 : 16 * (4 * h) + 16]
                for j in range(1, 4):
                    kk = 4 * h + j
                    t = jnp.where(sub == j, v[16 * kk + 8 : 16 * kk + 16], t)
                zz[64 + 8 * h : 72 + 8 * h, lanes] = t
            for e in range(8 * b):
                r = extra_row(e // 3, e % 3)
                mask[e : e + 1, lanes] = v[r : r + 1]
            for j in range(3):
                r = extra_row(0, 3 + j)
                val[j : j + 1, lanes] = v[r : r + 1]
        return 0

    lax.fori_loop(0, 8, assemble, 0)
    unit = lax.rem(iota((M, MAPS), 1), M) == iota((M, MAPS), 0)
    zz[:, NB * 1024 :] = jnp.where(unit, 1.0, 0.0)
    grow = jnp.where(iota((8, MAPS), 0) == iota((8, MAPS), 1) // M, 1.0, 0.0)
    for b in range(NB):
        mask[8 * b : 8 * b + 8, NB * 1024 :] = mm(mk_ref[:, b, :].astype(F32), grow, TN)
    pp[...] = jnp.zeros_like(pp)

    for b in range(NB):
        lanes = slice(b * 1024, b * 1024 + 1024)
        prior = zz[:, lanes]
        accepted = val[0:1, lanes]
        observed = val[1:2, lanes]
        noise = val[2:3, lanes]
        mean = jnp.sum(prior, axis=0, keepdims=True) / M
        dev = prior - mean
        var = jnp.sum(dev * dev, axis=0, keepdims=True) / (M - 1) + epsilon
        den = var + noise
        shift = var / den * (observed - mean)
        factor = jnp.sqrt(noise / den) - 1.0
        inc = accepted * shift + (accepted * factor) * dev
        scl = dev * (1.0 / ((M - 1) * var))
        ih, il = split(inc)
        sh, sl = split(scl)
        for q in range(8):
            w = slice(128 * q, 128 * q + 128)
            left = jnp.concatenate([sh[:, w], sl[:, w]], axis=1)
            right = jnp.concatenate([ih[:, w], ih[:, w]], axis=1)
            prod = mm(left, right, NT_) + mm(sh[:, w], il[:, w], NT_)
            pp[b % 2, 80 * q : 80 * q + 80, 0:80] = prod
        ph, plo = split(jnp.transpose(pp[b % 2])[:M])
        pt[b, 0:M, :] = ph
        pt[b, M : 2 * M, :] = plo

        def change(at, wide, dh, dl, b=b):
            v = zz[:, at]
            d = v - jnp.sum(v, axis=0, keepdims=True) * (1.0 / M)
            hi, lo = split(d)
            for q in range(8):
                w = jnp.broadcast_to(mask[8 * b + q : 8 * b + q + 1, at], (16, wide)).astype(BF)
                for g in range(5):
                    rr = slice(80 * q + 16 * g, 80 * q + 16 * g + 16)
                    dh[rr, :] = hi[16 * g : 16 * g + 16] * w
                    dl[rr, :] = lo[16 * g : 16 * g + 16] * w
            both = mm(pt[b], dh[...], NN)
            rest = mm(pt[b, 0:M, :], dl[...], NN)
            zz[:, at] = v + (both[0:M] + (both[M : 2 * M] + rest))

        def update(i, _):
            change(pl.ds(pl.multiple_of((b + 1) * 1024 + i * CH, CH), CH), CH, dh, dl)
            return 0

        lax.fori_loop(0, (NB - 1 - b) * 1024 // CH, update, 0)
        change(slice(NB * 1024, WIDE), MAPS, th, tl)

    true = iota((M, M), 0)
    tk = true // MLOC
    ti = lax.rem(true, MLOC)
    place = jnp.where(ti < 8, 8 * tk + ti, 64 + 2 * tk + ti - 8)
    perm = jnp.where(iota((M, M), 1) == place, 1.0, 0.0).astype(BF)
    whole, part = split(zz[:, NB * 1024 :])
    tp[0:M, :] = mm(perm, whole, NN).astype(BF)
    tp[M : 2 * M, :] = mm(perm, part, NN).astype(BF)
    state.wait()
    puts = []
    for t in range(NT):
        at = slice(TILE * t, TILE * t + TILE)
        for kk in range(NK):
            sp[t % 2, 8 * kk : 8 * kk + 8, :] = s_ref[kk, 0:8, at]
            sp[t % 2, 64 + 2 * kk : 66 + 2 * kk, :] = s_ref[kk, 8:10, at]
        hi, lo = split(sp[t % 2])
        maps = tp[:, M * t : M * t + M]
        both = mm(maps, hi, NN)
        rest = mm(maps[0:M], lo, NN)
        out_ref[:, at] = both[0:M] + (both[M : 2 * M] + rest)
        puts.append(pltpu.make_async_copy(out_ref.at[:, at], out.at[:, at], osem.at[t]))
        puts[-1].start()
    for cp in puts:
        cp.wait()


def window_call(g, s, mk):
    return pl.pallas_call(
        window_kernel,
        out_shape=jax.ShapeDtypeStruct((M, CELLS), F32),
        in_specs=[hbm(), hbm(), vm()],
        out_specs=hbm(),
        scratch_shapes=[
            pltpu.VMEM((M, WIDE), F32),
            pltpu.VMEM((32, WIDE), F32),
            pltpu.VMEM((8, NB * 1024), F32),
            pltpu.VMEM((2, 640, 128), F32),
            pltpu.VMEM((NB, 2 * M, 640), BF),
            pltpu.VMEM((640, CH), BF),
            pltpu.VMEM((640, CH), BF),
            pltpu.VMEM((640, MAPS), BF),
            pltpu.VMEM((640, MAPS), BF),
            pltpu.VMEM((2, M, TILE), F32),
            pltpu.VMEM((2 * M, MAPS), BF),
            pltpu.VMEM((NC, 128, 128), F32),
            pltpu.VMEM((NK, MLOC, CELLS), F32),
            pltpu.VMEM((M, CELLS), F32),
            pltpu.SemaphoreType.DMA((8,)),
            pltpu.SemaphoreType.DMA(()),
            pltpu.SemaphoreType.DMA((NT,)),
        ],
        name="window",
    )(g, s, mk)


def local(state, obs_value, obs_var, owner, tile_of, offsets, accept, loc_mask):
    places = jnp.transpose(offsets, (0, 2, 1))
    g, s = exchange_call(
        owner[:, :, 0], tile_of, places, accept, obs_value, obs_var, loc_mask, state
    )
    return window_call(g.reshape(NC, 128, 128), s, loc_mask)


def solution(mesh):
    return jax.shard_map(
        local,
        mesh=mesh,
        in_specs=(
            P("mem", "cols"),
            P(None, "cols"),
            P(None, "cols"),
            P(None, "cols", None),
            P(None, "cols"),
            P(None, "cols", None),
            P(None, "cols"),
            P(("cols", "mem"), None, None),
        ),
        out_specs=P(None, ("cols", "mem")),
        check_vma=False,
    )
```

```python
import jax
import jax.numpy as jnp
from jax import lax
from jax.experimental import pallas as pl
from jax.experimental.pallas import tpu as pltpu
from jax.sharding import PartitionSpec as P

epsilon = 1e-05
MESH = pl.DeviceIdType.MESH
F32 = jnp.float32
BF = jnp.bfloat16
I32 = jnp.int32

NB = 4
NC = 32
NK = 8
MLOC = 10
M = 80
NY = 4
NZ = 8
TILE = 512
NT = 8
CELLS = 4096
RA = 40
RB = 16
HALF = RA + RB
ROWS = 2 * HALF


def vm():
    return pl.BlockSpec(memory_space=pltpu.VMEM)


def sm():
    return pl.BlockSpec(memory_space=pltpu.SMEM)


def hbm():
    return pl.BlockSpec(memory_space=pl.ANY)


def iota(shape, axis):
    return lax.broadcasted_iota(I32, shape, axis)


def split(v):
    hi = v.astype(BF)
    lo = (v - hi.astype(F32)).astype(BF)
    return hi, lo


def mm(a, b, dims):
    return lax.dot_general(a, b, (dims, ((), ())), preferred_element_type=F32)


NN = ((1,), (0,))
NT_ = ((1,), (1,))
TN = ((0,), (0,))
def send(src, dst, ssem, rsem, dev):
    cp = pltpu.make_async_remote_copy(
        src_ref=src, dst_ref=dst, send_sem=ssem, recv_sem=rsem, device_id=dev, device_id_type=MESH
    )
    cp.start()
    return cp


FAR = sorted(
    ((dy, dz) for dy in range(NY) for dz in range(NZ) if dy + dz > 0),
    key=lambda o: -(min(o[0], NY - o[0]) + min(o[1], NZ - o[1])),
)
FAR_K = (4, 3, 5, 2, 6, 1, 7)
NEAR_Y = (1, 3, 2)
NEAR_Z = (1, 7, 2, 6, 3, 5, 4)
EARLY = (4, 2, 7, 1)
LATE = (5, 3, 6)


def exchange_kernel(
    ow, ti, of, ac, va, vr, lm, st, g_ref, s_ref, s2_ref,
    stv, tiled, fi, fl, mv, mrow, rr, rsm, mks, xs, zrow, rz, blocks, tail,
    ls, own, cs, ms, mr, ks, kr, ss, rs, xss, xsr, a1s, a1r, b1s, b1r, a2s, a2r, b2s, b2r,
    pas, par, ts, tr, us, ur, own2,
):
    c = lax.axis_index("cols")
    k = lax.axis_index("mem")
    y = c // NZ
    z = lax.rem(c, NZ)
    core = lax.rem(k, 2)
    bar = pltpu.get_barrier_semaphore()
    cols = [(dy * NZ + dz, lax.rem(y + dy, NY) * NZ + lax.rem(z + dz, NZ)) for dy, dz in FAR]
    for d, p in cols:
        pl.semaphore_signal(bar, inc=1, device_id=(p, k), device_id_type=MESH)
    for d in FAR_K:
        pl.semaphore_signal(bar, inc=1, device_id=(c, lax.rem(k + d, NK)), device_id_type=MESH)
    load = pltpu.make_async_copy(st, stv, ls)
    load.start()
    mv[...] = jnp.zeros_like(mv)
    tiles = ti[...] * TILE
    cells = [tiles + of[:, p, :] for p in range(4)]
    places = [ow[...], cells[0] + (cells[1] << 15), cells[2] + (cells[3] << 15)]
    fields = [ac[...].astype(F32), va[...], vr[...]]
    for b in range(NB):
        at = slice(32 * b, 32 * b + 32)
        for f in range(3):
            fi[f : f + 1, at] = places[f][b : b + 1, :]
            fl[f : f + 1, at] = fields[f][b : b + 1, :]
        mv[:, 8 * b : 8 * b + 8] = lm[:, b, :].astype(F32)
    r128 = iota((128, 128), 0)
    c128 = iota((128, 128), 1)
    lane32 = iota((NC, 128), 1)
    within = lane32 & 31
    hoti = jnp.where(iota((NC, 128), 0) == fi[0:1, :], 1, 0)
    seen = hoti
    for h in (1, 2, 4, 8, 16):
        seen = seen + jnp.where(within >= h, pltpu.roll(seen, h, 1), 0)
    slots = jnp.zeros((NC, 128), I32)
    for r in range(2):
        for w in range(2):
            v = jnp.where((hoti == 1) & (seen == r + 1), fi[w + 1 : w + 2, :], 0)
            for h in (1, 2, 4, 8, 16):
                v = v + pltpu.roll(v, 128 - h, 1)
            for p, cell in ((2 * w, v & 32767), (2 * w + 1, (v >> 15) & 32767)):
                for f, word in ((p, cell >> 7), (p + 4, cell & 127)):
                    spot = 8 * r + f
                    word = word if spot == 0 else pltpu.roll(word, spot, 1)
                    slots = jnp.where(within == spot, word, slots)
    mrow[...] = slots.reshape(NC, 1, 128)
    hot = hoti.astype(F32)
    rank = jnp.sum((hoti * (seen - 1)).astype(F32), axis=0, keepdims=True)
    load.wait()
    for t in range(NK * CELLS // 128):
        tiled[t] = stv[:, 128 * t : 128 * t + 128]
    for p in range(NK):
        for j in range(4):
            at = CELLS * p + 1024 * j
            tail[p, 2 * j : 2 * j + 2, :] = stv[8:10, at : at + 1024]
    pl.semaphore_wait(bar, NC - 1 + NK - 1)

    ask = []
    for d, p in cols:
        ask.append(send(mrow.at[p], rr.at[c], ms.at[d], mr.at[d], (p, k)))
    maps = []
    for d in FAR_K:
        maps.append(send(mv, mks.at[k], ks.at[d], kr.at[d], (c, lax.rem(k + d, NK))))
    rr[c] = mrow[c]
    mks[k] = mv[...]
    def move(d):
        p = lax.rem(k + d, NK)
        part = stv.at[0:8, pl.ds(pl.multiple_of(p * CELLS, CELLS), CELLS)]
        return [
            send(part, s_ref.at[k], ts.at[d], tr.at[d], (c, p)),
            send(tail.at[p], s2_ref.at[k], us.at[d], ur.at[d], (c, p)),
        ]

    moves = [cp for d in EARLY for cp in move(d)]
    keep = pltpu.make_async_copy(
        stv.at[0:8, pl.ds(pl.multiple_of(k * CELLS, CELLS), CELLS)], s_ref.at[k], own
    )
    keep.start()
    keep2 = pltpu.make_async_copy(tail.at[k], s2_ref.at[k], own2)
    keep2.start()
    for cp in maps:
        cp.wait()
    pick = lax.rem(c128, 16) - 10
    chosen = jnp.where((pick >= 0) & (pick < 3) & (r128 == 3 * k + pick), 1.0, 0.0)
    table = mm(mks[...].reshape(64, 128).astype(BF), chosen.astype(BF), NN).astype(BF)
    for cp in ask:
        cp.wait()
    scal = pltpu.make_async_copy(rr, rsm, cs)
    scal.start()
    got = rr[...].reshape(NC, 128)
    extra = jnp.zeros((NC, 128), F32)
    for q in range(8):
        word = 32 * (q // 2) + 8 * (q % 2)
        tile = got[:, word : word + 1] >> 2
        at_tile = jnp.where(iota((NC, 64), 1) == tile, 1.0, 0.0).astype(BF)
        extra = jnp.where(lane32 // 16 == q, mm(at_tile, table, NN), extra)
    scal.wait()
    lane = iota((MLOC, 128), 1)

    def priors(i, accs):
        here = lane == i
        out = []
        for q in range(8):
            v = jnp.zeros((MLOC, 128), F32)
            word = 32 * (q // 2) + 8 * (q % 2)
            for p in range(4):
                hit = lane == rsm[i, 0, word + 4 + p]
                v = v + jnp.where(hit, tiled[rsm[i, 0, word + p]], 0.0)
            out.append(jnp.where(here, jnp.sum(v, axis=1, keepdims=True), accs[q]))
        return tuple(out)

    accs = lax.fori_loop(0, NC, priors, tuple(jnp.zeros((MLOC, 128), F32) for _ in range(8)), unroll=True)
    xs[...] = jnp.zeros_like(xs)
    for q in range(8):
        xs[16 * q : 16 * q + MLOC, :] = accs[q] * 0.25
    zr = jnp.transpose(xs[...])[:NC] + extra
    zrow[...] = zr.reshape(NC, 1, 128)
    back = []
    for d, p in cols:
        back.append(send(zrow.at[p], rz.at[c], ss.at[d], rs.at[d], (p, k)))
    rz[c] = zrow[c]
    for cp in back:
        cp.wait()
    full = lax.dot_general(
        rz[...].reshape(NC, 128), hot, (TN, ((), ())),
        precision=lax.Precision.HIGHEST, preferred_element_type=F32,
    )
    batch = iota((1, 128), 1) // 32
    blk = jnp.zeros((16, 128), F32)
    for q in range(8):
        mine = (batch == q // 2) & (rank == float(q % 2))
        blk = blk + jnp.where(mine, full[16 * q : 16 * q + 16, :], 0.0)
    row16 = iota((16, 128), 0)
    for j in range(3):
        blk = jnp.where(row16 == 13 + j, fl[j : j + 1, :], blk)
    turned = blk
    around = lax.rem(z, 4)
    for j in range(1, 4):
        turned = jnp.where(around == j, pltpu.roll(blk, 32 * j, 1), turned)
    blocks[k] = turned
    block = blocks.at[k]
    step = []
    for d in FAR_K:
        step.append(send(block, block, xss.at[d], xsr.at[d], (c, lax.rem(k + d, NK))))
    for cp in step:
        cp.wait()
    sub8 = iota((8, 128), 0)
    for h in range(2):
        tails = [blocks[4 * h + u, 8:16, :] for u in range(4)]
        for u in range(4):
            g_ref[y, z, HALF * h + 8 * u : HALF * h + 8 * u + 8, :] = blocks[4 * h + u, 0:8, :]
        last = tails[0]
        for u in range(1, 4):
            last = jnp.where(sub8 // 2 == u, pltpu.roll(tails[u], 2 * u, 0), last)
        g_ref[y, z, HALF * h + 32 : HALF * h + 40, :] = last
        low = jnp.where(sub8 < 3, pltpu.roll(tails[0], 6, 0), pltpu.roll(tails[1], 1, 0))
        low = jnp.where(sub8 >= 6, pltpu.roll(tails[0], 1, 0), low)
        high = jnp.where(sub8 < 3, pltpu.roll(tails[2], 6, 0), pltpu.roll(tails[3], 1, 0))
        high = jnp.where(sub8 >= 6, pltpu.roll(tails[2], 7, 0), high)
        g_ref[y, z, HALF * h + 40 : HALF * h + 48, :] = low
        g_ref[y, z, HALF * h + 48 : HALF * h + 56, :] = high
    ra = pl.multiple_of(HALF * core, 8)
    rb = pl.multiple_of(HALF * core + RA, 8)
    mate = (c, k + 1 - 2 * core)
    y_at = [lax.rem(y + d, NY) for d in range(NY)]
    z_at = [lax.rem(z + d, NZ) for d in range(NZ)]

    def piece_a(dy, dz):
        return g_ref.at[y_at[(-dy) % NY], z_at[(-dz) % NZ], pl.ds(ra, RA), :]

    def piece_b(dy, dz):
        return g_ref.at[y_at[(-dy) % NY], z_at[(-dz) % NZ], pl.ds(rb, RB), :]

    out_a = {}
    out_b = {}
    pair = []

    def along_y(e):
        piece = piece_a(0, e)
        for d in NEAR_Y:
            out_a[d, e] = send(piece, piece, a2s.at[d, e], a2r.at[d, e], (y_at[d] * NZ + z, k))

    def along_z(e):
        piece = piece_b(e, 0)
        for d in NEAR_Z:
            out_b[d, e] = send(piece, piece, b2s.at[d, e], b2r.at[d, e], (y * NZ + z_at[d], k))

    def to_mate(piece, n, dy, dz):
        pair.append(send(piece, piece, pas.at[n, dy, dz], par.at[n, dy, dz], mate))

    own_a = piece_a(0, 0)
    own_b = piece_b(0, 0)
    first_a = {}
    first_b = {}
    for d in NEAR_Z:
        first_a[d] = send(own_a, own_a, a1s.at[d], a1r.at[d], (y * NZ + z_at[d], k))
    for d in NEAR_Y:
        first_b[d] = send(own_b, own_b, b1s.at[d], b1r.at[d], (y_at[d] * NZ + z, k))
    along_y(0)
    along_z(0)
    moves += [cp for d in LATE for cp in move(d)]
    for kind, e in (("b", 1), ("a", 1), ("b", 3), ("a", 7), ("a", 2), ("b", 2), ("a", 6), ("a", 3), ("a", 5), ("a", 4)):
        if kind == "a":
            first_a[e].wait_recv()
            along_y(e)
            to_mate(piece_a(0, e), 0, 0, e)
        else:
            first_b[e].wait_recv()
            along_z(e)
            to_mate(piece_b(e, 0), 1, e, 0)
    order = [(0, d, e) for d in NEAR_Y for e in range(NZ)] + [(1, e, d) for d in NEAR_Z for e in range(NY)]
    order.sort(key=lambda o: (min(o[1], NY - o[1]) + min(o[2], NZ - o[2])))
    for n, dy, dz in order:
        if n == 0:
            out_a[dy, dz].wait_recv()
            to_mate(piece_a(dy, dz), 0, dy, dz)
        else:
            out_b[dz, dy].wait_recv()
            to_mate(piece_b(dy, dz), 1, dy, dz)
    for group in (first_a, first_b, out_a, out_b):
        for cp in group.values():
            cp.wait_send()
    keep.wait()
    keep2.wait()
    for cp in moves + pair:
        cp.wait()


def exchange_call(ow, ti, of, ac, va, vr, lm, st):
    dma = pltpu.SemaphoreType.DMA
    row = pltpu.VMEM((NC, 1, 128), F32)
    irow = pltpu.VMEM((NC, 1, 128), I32)
    return pl.pallas_call(
        exchange_kernel,
        out_shape=(
            jax.ShapeDtypeStruct((NY, NZ, ROWS, 128), F32),
            jax.ShapeDtypeStruct((NK, 8, CELLS), F32),
            jax.ShapeDtypeStruct((NK, 8, 1024), F32),
        ),
        in_specs=[vm()] * 7 + [hbm()],
        out_specs=(vm(), hbm(), hbm()),
        scratch_shapes=[
            pltpu.VMEM((MLOC, NK * CELLS), F32),
            pltpu.VMEM((NK * CELLS // 128, MLOC, 128), F32),
            pltpu.VMEM((8, 128), I32),
            pltpu.VMEM((8, 128), F32),
            pltpu.VMEM((8, 128), F32),
            irow, irow,
            pltpu.SMEM((NC, 1, 128), I32),
            pltpu.VMEM((NK, 8, 128), F32),
            pltpu.VMEM((128, 128), F32),
            row, row,
            pltpu.VMEM((NK, 16, 128), F32),
            pltpu.VMEM((NK, 8, 1024), F32),
            dma(()), dma(()), dma(()),
            dma((NC,)), dma((NC,)), dma((NK,)), dma((NK,)),
            dma((NC,)), dma((NC,)), dma((NK,)), dma((NK,)),
            dma((NZ,)), dma((NZ,)), dma((NY,)), dma((NY,)),
            dma((NY, NZ)), dma((NY, NZ)), dma((NZ, NY)), dma((NZ, NY)),
            dma((2, NY, NZ)), dma((2, NY, NZ)),
            dma((NK,)), dma((NK,)), dma((NK,)), dma((NK,)), dma(()),
        ],
        compiler_params=pltpu.CompilerParams(collective_id=0, has_side_effects=True),
        name="exchange",
    )(ow, ti, of, ac, va, vr, lm, st)


MAPS = NT * M
WIDE = NB * 1024 + MAPS
CH = 512


def mask_row(e):
    k, x = divmod(e, 3)
    return HALF * (k // 4) + 40 + 8 * (k % 4 // 2) + 3 * (k % 2) + x


VALUE_ROWS = (46, 47, 54)


def window_kernel(g_hbm, s_hbm, s2_hbm, mk_ref, out, zz, mask, val, pp, pt, dh, dl, th, tl, sp, tp, g_ref, s_ref, s2_ref, out_ref, gsem, ssem, ssem2, osem):
    gets = [pltpu.make_async_copy(g_hbm.at[pl.ds(4 * q, 4)], g_ref.at[pl.ds(4 * q, 4)], gsem.at[q]) for q in range(8)]
    for cp in gets:
        cp.start()
    state = pltpu.make_async_copy(s_hbm, s_ref, ssem)
    state.start()
    ends = pltpu.make_async_copy(s2_hbm, s2_ref, ssem2)
    ends.start()
    lane_group = iota((ROWS, 128), 1) // 32

    def assemble(blk, _):
        part = pl.ds(4 * blk, 4)
        pltpu.make_async_copy(g_hbm.at[part], g_ref.at[part], gsem.at[blk]).wait()
        parts = [g_ref[4 * blk + u] for u in range(4)]
        for b in range(NB):
            v = parts[3]
            for u in range(3):
                v = jnp.where(lane_group == (b + u) % 4, parts[u], v)
            lanes = pl.ds(pl.multiple_of(b * 1024 + blk * 128, 128), 128)
            for h in range(2):
                zz[32 * h : 32 * h + 32, lanes] = v[HALF * h : HALF * h + 32]
                zz[64 + 8 * h : 72 + 8 * h, lanes] = v[HALF * h + 32 : HALF * h + 40]
            for e in range(8 * b):
                r = mask_row(e)
                mask[e : e + 1, lanes] = v[r : r + 1]
            for j, r in enumerate(VALUE_ROWS):
                val[j : j + 1, lanes] = v[r : r + 1]
        return 0

    lax.fori_loop(0, 8, assemble, 0)
    unit = lax.rem(iota((M, MAPS), 1), M) == iota((M, MAPS), 0)
    zz[:, NB * 1024 :] = jnp.where(unit, 1.0, 0.0)
    grow = jnp.where(iota((8, MAPS), 0) == iota((8, MAPS), 1) // M, 1.0, 0.0)
    for b in range(NB):
        mask[8 * b : 8 * b + 8, NB * 1024 :] = mm(mk_ref[:, b, :].astype(F32), grow, TN)
    pp[...] = jnp.zeros_like(pp)

    for b in range(NB):
        lanes = slice(b * 1024, b * 1024 + 1024)
        prior = zz[:, lanes]
        accepted = val[0:1, lanes]
        observed = val[1:2, lanes]
        noise = val[2:3, lanes]
        mean = jnp.sum(prior, axis=0, keepdims=True) / M
        dev = prior - mean
        var = jnp.sum(dev * dev, axis=0, keepdims=True) / (M - 1) + epsilon
        den = var + noise
        shift = var / den * (observed - mean)
        factor = jnp.sqrt(noise / den) - 1.0
        inc = accepted * shift + (accepted * factor) * dev
        scl = dev * (1.0 / ((M - 1) * var))
        ih, il = split(inc)
        sh, sl = split(scl)
        for q in range(8):
            w = slice(128 * q, 128 * q + 128)
            left = jnp.concatenate([sh[:, w], sl[:, w]], axis=1)
            right = jnp.concatenate([ih[:, w], ih[:, w]], axis=1)
            prod = mm(left, right, NT_) + mm(sh[:, w], il[:, w], NT_)
            pp[b % 2, 80 * q : 80 * q + 80, 0:80] = prod
        ph, plo = split(jnp.transpose(pp[b % 2])[:M])
        pt[b, 0:M, :] = ph
        pt[b, M : 2 * M, :] = plo

        def change(at, wide, dh, dl, b=b):
            v = zz[:, at]
            d = v - jnp.sum(v, axis=0, keepdims=True) * (1.0 / M)
            hi, lo = split(d)
            for q in range(8):
                w = jnp.broadcast_to(mask[8 * b + q : 8 * b + q + 1, at], (16, wide)).astype(BF)
                for g in range(5):
                    rr = slice(80 * q + 16 * g, 80 * q + 16 * g + 16)
                    dh[rr, :] = hi[16 * g : 16 * g + 16] * w
                    dl[rr, :] = lo[16 * g : 16 * g + 16] * w
            both = mm(pt[b], dh[...], NN)
            rest = mm(pt[b, 0:M, :], dl[...], NN)
            zz[:, at] = v + (both[0:M] + (both[M : 2 * M] + rest))

        def update(i, _):
            change(pl.ds(pl.multiple_of((b + 1) * 1024 + i * CH, CH), CH), CH, dh, dl)
            return 0

        lax.fori_loop(0, (NB - 1 - b) * 1024 // CH, update, 0)
        change(slice(NB * 1024, WIDE), MAPS, th, tl)

    true = iota((M, M), 0)
    tk = true // MLOC
    ti = lax.rem(true, MLOC)
    place = jnp.where(ti < 8, 8 * tk + ti, 64 + 2 * tk + ti - 8)
    perm = jnp.where(iota((M, M), 1) == place, 1.0, 0.0).astype(BF)
    whole, part = split(zz[:, NB * 1024 :])
    tp[0:M, :] = mm(perm, whole, NN).astype(BF)
    tp[M : 2 * M, :] = mm(perm, part, NN).astype(BF)
    state.wait()
    ends.wait()
    puts = []
    for t in range(NT):
        at = slice(TILE * t, TILE * t + TILE)
        for kk in range(NK):
            sp[t % 2, 8 * kk : 8 * kk + 8, :] = s_ref[kk, :, at]
            sp[t % 2, 64 + 2 * kk : 66 + 2 * kk, :] = s2_ref[
                kk, 2 * (t // 2) : 2 * (t // 2) + 2, TILE * (t % 2) : TILE * (t % 2) + TILE
            ]
        hi, lo = split(sp[t % 2])
        maps = tp[:, M * t : M * t + M]
        both = mm(maps, hi, NN)
        rest = mm(maps[0:M], lo, NN)
        out_ref[:, at] = both[0:M] + (both[M : 2 * M] + rest)
        puts.append(pltpu.make_async_copy(out_ref.at[:, at], out.at[:, at], osem.at[t]))
        puts[-1].start()
    for cp in puts:
        cp.wait()


def window_call(g, s, s2, mk):
    return pl.pallas_call(
        window_kernel,
        out_shape=jax.ShapeDtypeStruct((M, CELLS), F32),
        in_specs=[hbm(), hbm(), hbm(), vm()],
        out_specs=hbm(),
        scratch_shapes=[
            pltpu.VMEM((M, WIDE), F32),
            pltpu.VMEM((32, WIDE), F32),
            pltpu.VMEM((8, NB * 1024), F32),
            pltpu.VMEM((2, 640, 128), F32),
            pltpu.VMEM((NB, 2 * M, 640), BF),
            pltpu.VMEM((640, CH), BF),
            pltpu.VMEM((640, CH), BF),
            pltpu.VMEM((640, MAPS), BF),
            pltpu.VMEM((640, MAPS), BF),
            pltpu.VMEM((2, M, TILE), F32),
            pltpu.VMEM((2 * M, MAPS), BF),
            pltpu.VMEM((NC, ROWS, 128), F32),
            pltpu.VMEM((NK, 8, CELLS), F32),
            pltpu.VMEM((NK, 8, 1024), F32),
            pltpu.VMEM((M, CELLS), F32),
            pltpu.SemaphoreType.DMA((8,)),
            pltpu.SemaphoreType.DMA(()),
            pltpu.SemaphoreType.DMA(()),
            pltpu.SemaphoreType.DMA((NT,)),
        ],
        name="window",
    )(g, s, s2, mk)


def local(state, obs_value, obs_var, owner, tile_of, offsets, accept, loc_mask):
    places = jnp.transpose(offsets, (0, 2, 1))
    g, s, s2 = exchange_call(
        owner[:, :, 0], tile_of, places, accept, obs_value, obs_var, loc_mask, state
    )
    return window_call(g.reshape(NC, ROWS, 128), s, s2, loc_mask)


def solution(mesh):
    return jax.shard_map(
        local,
        mesh=mesh,
        in_specs=(
            P("mem", "cols"),
            P(None, "cols"),
            P(None, "cols"),
            P(None, "cols", None),
            P(None, "cols"),
            P(None, "cols", None),
            P(None, "cols"),
            P(("cols", "mem"), None, None),
        ),
        out_specs=P(None, ("cols", "mem")),
        check_vma=False,
    )
```

```python
import jax
import jax.numpy as jnp
from jax import lax
from jax.experimental import pallas as pl
from jax.experimental.pallas import tpu as pltpu
from jax.sharding import PartitionSpec as P

epsilon = 1e-05
MESH = pl.DeviceIdType.MESH
F32 = jnp.float32
BF = jnp.bfloat16
I32 = jnp.int32

NB = 4
NC = 32
NK = 8
MLOC = 10
M = 80
NY = 4
NZ = 8
TILE = 512
NT = 8
CELLS = 4096
RA = 40
RB = 16
HALF = RA + RB
ROWS = 2 * HALF


def vm():
    return pl.BlockSpec(memory_space=pltpu.VMEM)


def sm():
    return pl.BlockSpec(memory_space=pltpu.SMEM)


def hbm():
    return pl.BlockSpec(memory_space=pl.ANY)


def iota(shape, axis):
    return lax.broadcasted_iota(I32, shape, axis)


def split(v):
    hi = v.astype(BF)
    lo = (v - hi.astype(F32)).astype(BF)
    return hi, lo


def mm(a, b, dims):
    return lax.dot_general(a, b, (dims, ((), ())), preferred_element_type=F32)


NN = ((1,), (0,))
NT_ = ((1,), (1,))
TN = ((0,), (0,))
def send(src, dst, ssem, rsem, dev):
    cp = pltpu.make_async_remote_copy(
        src_ref=src, dst_ref=dst, send_sem=ssem, recv_sem=rsem, device_id=dev, device_id_type=MESH
    )
    cp.start()
    return cp


FAR = sorted(
    ((dy, dz) for dy in range(NY) for dz in range(NZ) if dy + dz > 0),
    key=lambda o: -(min(o[0], NY - o[0]) + min(o[1], NZ - o[1])),
)
FAR_K = (4, 3, 5, 2, 6, 1, 7)
NEAR_Y = (1, 3, 2)
NEAR_Z = (1, 7, 2, 6, 3, 5, 4)
EARLY = (4, 2, 7, 1)
LATE = (5, 3, 6)


def exchange_kernel(
    ow, ti, of, ac, va, vr, lm, st, g_ref, s_ref, s2_ref,
    stv, tiled, fi, fl, mv, mrow, rr, rsm, mks, xs, zrow, rz, blocks, tail,
    ls, own, cs, ms, mr, ks, kr, ss, rs, xss, xsr, a1s, a1r, b1s, b1r, a2s, a2r, b2s, b2r,
    pas, par, ts, tr, us, ur, own2,
):
    c = lax.axis_index("cols")
    k = lax.axis_index("mem")
    y = c // NZ
    z = lax.rem(c, NZ)
    core = lax.rem(k, 2)
    bar = pltpu.get_barrier_semaphore()
    cols = [(dy * NZ + dz, lax.rem(y + dy, NY) * NZ + lax.rem(z + dz, NZ)) for dy, dz in FAR]
    for d, p in cols:
        pl.semaphore_signal(bar, inc=1, device_id=(p, k), device_id_type=MESH)
    for d in FAR_K:
        pl.semaphore_signal(bar, inc=1, device_id=(c, lax.rem(k + d, NK)), device_id_type=MESH)
    load = pltpu.make_async_copy(st, stv, ls)
    load.start()
    mv[...] = jnp.zeros_like(mv)
    tiles = ti[...] * TILE
    cells = [tiles + of[:, p, :] for p in range(4)]
    places = [ow[...], cells[0] + (cells[1] << 15), cells[2] + (cells[3] << 15)]
    fields = [ac[...].astype(F32), va[...], vr[...]]
    for b in range(NB):
        at = slice(32 * b, 32 * b + 32)
        for f in range(3):
            fi[f : f + 1, at] = places[f][b : b + 1, :]
            fl[f : f + 1, at] = fields[f][b : b + 1, :]
        mv[:, 8 * b : 8 * b + 8] = lm[:, b, :].astype(F32)
    r128 = iota((128, 128), 0)
    c128 = iota((128, 128), 1)
    lane32 = iota((NC, 128), 1)
    within = lane32 & 31
    hoti = jnp.where(iota((NC, 128), 0) == fi[0:1, :], 1, 0)
    seen = hoti
    for h in (1, 2, 4, 8, 16):
        seen = seen + jnp.where(within >= h, pltpu.roll(seen, h, 1), 0)
    slots = jnp.zeros((NC, 128), I32)
    for r in range(2):
        for w in range(2):
            v = jnp.where((hoti == 1) & (seen == r + 1), fi[w + 1 : w + 2, :], 0)
            for h in (1, 2, 4, 8, 16):
                v = v + pltpu.roll(v, 128 - h, 1)
            for p, cell in ((2 * w, v & 32767), (2 * w + 1, (v >> 15) & 32767)):
                for f, word in ((p, cell >> 7), (p + 4, cell & 127)):
                    spot = 8 * r + f
                    word = word if spot == 0 else pltpu.roll(word, spot, 1)
                    slots = jnp.where(within == spot, word, slots)
    mrow[...] = slots.reshape(NC, 1, 128)
    hot = hoti.astype(F32)
    rank = jnp.sum((hoti * (seen - 1)).astype(F32), axis=0, keepdims=True)
    load.wait()
    for t in range(NK * CELLS // 128):
        tiled[t] = stv[:, 128 * t : 128 * t + 128]
    for p in range(NK):
        for j in range(4):
            at = CELLS * p + 1024 * j
            tail[p, 2 * j : 2 * j + 2, :] = stv[8:10, at : at + 1024]
    pl.semaphore_wait(bar, NC - 1 + NK - 1)

    ask = []
    for d, p in cols:
        ask.append(send(mrow.at[p], rr.at[c], ms.at[d], mr.at[d], (p, k)))
    maps = []
    for d in FAR_K:
        maps.append(send(mv, mks.at[k], ks.at[d], kr.at[d], (c, lax.rem(k + d, NK))))
    rr[c] = mrow[c]
    mks[k] = mv[...]
    def move(d):
        p = lax.rem(k + d, NK)
        part = stv.at[0:8, pl.ds(pl.multiple_of(p * CELLS, CELLS), CELLS)]
        return [
            send(part, s_ref.at[k], ts.at[d], tr.at[d], (c, p)),
            send(tail.at[p], s2_ref.at[k], us.at[d], ur.at[d], (c, p)),
        ]

    moves = [cp for d in EARLY for cp in move(d)]
    keep = pltpu.make_async_copy(
        stv.at[0:8, pl.ds(pl.multiple_of(k * CELLS, CELLS), CELLS)], s_ref.at[k], own
    )
    keep.start()
    keep2 = pltpu.make_async_copy(tail.at[k], s2_ref.at[k], own2)
    keep2.start()
    for cp in maps:
        cp.wait()
    pick = lax.rem(c128, 16) - 10
    chosen = jnp.where((pick >= 0) & (pick < 3) & (r128 == 3 * k + pick), 1.0, 0.0)
    table = mm(mks[...].reshape(64, 128).astype(BF), chosen.astype(BF), NN).astype(BF)
    for cp in ask:
        cp.wait()
    scal = pltpu.make_async_copy(rr, rsm, cs)
    scal.start()
    got = rr[...].reshape(NC, 128)
    extra = jnp.zeros((NC, 128), F32)
    for q in range(8):
        word = 32 * (q // 2) + 8 * (q % 2)
        tile = got[:, word : word + 1] >> 2
        at_tile = jnp.where(iota((NC, 64), 1) == tile, 1.0, 0.0).astype(BF)
        extra = jnp.where(lane32 // 16 == q, mm(at_tile, table, NN), extra)
    scal.wait()
    lane = iota((MLOC, 128), 1)

    def priors(i, accs):
        here = lane == i
        out = []
        for q in range(8):
            v = jnp.zeros((MLOC, 128), F32)
            word = 32 * (q // 2) + 8 * (q % 2)
            for p in range(4):
                hit = lane == rsm[i, 0, word + 4 + p]
                v = v + jnp.where(hit, tiled[rsm[i, 0, word + p]], 0.0)
            out.append(jnp.where(here, jnp.sum(v, axis=1, keepdims=True), accs[q]))
        return tuple(out)

    accs = lax.fori_loop(0, NC, priors, tuple(jnp.zeros((MLOC, 128), F32) for _ in range(8)), unroll=True)
    xs[...] = jnp.zeros_like(xs)
    for q in range(8):
        xs[16 * q : 16 * q + MLOC, :] = accs[q] * 0.25
    zr = jnp.transpose(xs[...])[:NC] + extra
    zrow[...] = zr.reshape(NC, 1, 128)
    back = []
    for d, p in cols:
        back.append(send(zrow.at[p], rz.at[c], ss.at[d], rs.at[d], (p, k)))
    rz[c] = zrow[c]
    for cp in back:
        cp.wait()
    full = lax.dot_general(
        rz[...].reshape(NC, 128), hot, (TN, ((), ())),
        precision=lax.Precision.HIGHEST, preferred_element_type=F32,
    )
    batch = iota((1, 128), 1) // 32
    blk = jnp.zeros((16, 128), F32)
    for q in range(8):
        mine = (batch == q // 2) & (rank == float(q % 2))
        blk = blk + jnp.where(mine, full[16 * q : 16 * q + 16, :], 0.0)
    row16 = iota((16, 128), 0)
    for j in range(3):
        blk = jnp.where(row16 == 13 + j, fl[j : j + 1, :], blk)
    turned = blk
    around = lax.rem(z, 4)
    for j in range(1, 4):
        turned = jnp.where(around == j, pltpu.roll(blk, 32 * j, 1), turned)
    blocks[k] = turned
    block = blocks.at[k]
    step = []
    for d in FAR_K:
        step.append(send(block, block, xss.at[d], xsr.at[d], (c, lax.rem(k + d, NK))))
    for cp in step:
        cp.wait()
    sub8 = iota((8, 128), 0)
    for h in range(2):
        tails = [blocks[4 * h + u, 8:16, :] for u in range(4)]
        for u in range(4):
            g_ref[y, z, HALF * h + 8 * u : HALF * h + 8 * u + 8, :] = blocks[4 * h + u, 0:8, :]
        last = tails[0]
        for u in range(1, 4):
            last = jnp.where(sub8 // 2 == u, pltpu.roll(tails[u], 2 * u, 0), last)
        g_ref[y, z, HALF * h + 32 : HALF * h + 40, :] = last
        low = jnp.where(sub8 < 3, pltpu.roll(tails[0], 6, 0), pltpu.roll(tails[1], 1, 0))
        low = jnp.where(sub8 >= 6, pltpu.roll(tails[0], 1, 0), low)
        high = jnp.where(sub8 < 3, pltpu.roll(tails[2], 6, 0), pltpu.roll(tails[3], 1, 0))
        high = jnp.where(sub8 >= 6, pltpu.roll(tails[2], 7, 0), high)
        g_ref[y, z, HALF * h + 40 : HALF * h + 48, :] = low
        g_ref[y, z, HALF * h + 48 : HALF * h + 56, :] = high
    ra = pl.multiple_of(HALF * core, 8)
    rb = pl.multiple_of(HALF * core + RA, 8)
    mate = (c, k + 1 - 2 * core)
    y_at = [lax.rem(y + d, NY) for d in range(NY)]
    z_at = [lax.rem(z + d, NZ) for d in range(NZ)]

    def piece_a(dy, dz):
        return g_ref.at[y_at[(-dy) % NY], z_at[(-dz) % NZ], pl.ds(ra, RA), :]

    def piece_b(dy, dz):
        return g_ref.at[y_at[(-dy) % NY], z_at[(-dz) % NZ], pl.ds(rb, RB), :]

    out_a = {}
    out_b = {}
    pair = []

    def along_y(e):
        piece = piece_a(0, e)
        for d in NEAR_Y:
            out_a[d, e] = send(piece, piece, a2s.at[d, e], a2r.at[d, e], (y_at[d] * NZ + z, k))

    def along_z(e):
        piece = piece_b(e, 0)
        for d in NEAR_Z:
            out_b[d, e] = send(piece, piece, b2s.at[d, e], b2r.at[d, e], (y * NZ + z_at[d], k))

    def to_mate(piece, n, dy, dz):
        pair.append(send(piece, piece, pas.at[n, dy, dz], par.at[n, dy, dz], mate))

    own_a = piece_a(0, 0)
    own_b = piece_b(0, 0)
    first_a = {}
    first_b = {}
    for d in NEAR_Z:
        first_a[d] = send(own_a, own_a, a1s.at[d], a1r.at[d], (y * NZ + z_at[d], k))
    for d in NEAR_Y:
        first_b[d] = send(own_b, own_b, b1s.at[d], b1r.at[d], (y_at[d] * NZ + z, k))
    along_y(0)
    along_z(0)
    moves += [cp for d in LATE for cp in move(d)]
    for kind, e in (("b", 1), ("a", 1), ("b", 3), ("a", 7), ("a", 2), ("b", 2), ("a", 6), ("a", 3), ("a", 5), ("a", 4)):
        if kind == "a":
            first_a[e].wait_recv()
            along_y(e)
            to_mate(piece_a(0, e), 0, 0, e)
        else:
            first_b[e].wait_recv()
            along_z(e)
            to_mate(piece_b(e, 0), 1, e, 0)
    order = [(0, d, e) for d in NEAR_Y for e in range(NZ)] + [(1, e, d) for d in NEAR_Z for e in range(NY)]
    order.sort(key=lambda o: (min(o[1], NY - o[1]) + min(o[2], NZ - o[2])))
    for n, dy, dz in order:
        if n == 0:
            out_a[dy, dz].wait_recv()
            to_mate(piece_a(dy, dz), 0, dy, dz)
        else:
            out_b[dz, dy].wait_recv()
            to_mate(piece_b(dy, dz), 1, dy, dz)
    for group in (first_a, first_b, out_a, out_b):
        for cp in group.values():
            cp.wait_send()
    keep.wait()
    keep2.wait()
    for cp in moves + pair:
        cp.wait()


def exchange_call(ow, ti, of, ac, va, vr, lm, st):
    dma = pltpu.SemaphoreType.DMA
    row = pltpu.VMEM((NC, 1, 128), F32)
    irow = pltpu.VMEM((NC, 1, 128), I32)
    return pl.pallas_call(
        exchange_kernel,
        out_shape=(
            jax.ShapeDtypeStruct((NY, NZ, ROWS, 128), F32),
            jax.ShapeDtypeStruct((NK, 8, CELLS), F32),
            jax.ShapeDtypeStruct((NK, 8, 1024), F32),
        ),
        in_specs=[vm()] * 7 + [pl.BlockSpec(memory_space=pltpu.HBM)],
        out_specs=(vm(), hbm(), hbm()),
        scratch_shapes=[
            pltpu.VMEM((MLOC, NK * CELLS), F32),
            pltpu.VMEM((NK * CELLS // 128, MLOC, 128), F32),
            pltpu.VMEM((8, 128), I32),
            pltpu.VMEM((8, 128), F32),
            pltpu.VMEM((8, 128), F32),
            irow, irow,
            pltpu.SMEM((NC, 1, 128), I32),
            pltpu.VMEM((NK, 8, 128), F32),
            pltpu.VMEM((128, 128), F32),
            row, row,
            pltpu.VMEM((NK, 16, 128), F32),
            pltpu.VMEM((NK, 8, 1024), F32),
            dma(()), dma(()), dma(()),
            dma((NC,)), dma((NC,)), dma((NK,)), dma((NK,)),
            dma((NC,)), dma((NC,)), dma((NK,)), dma((NK,)),
            dma((NZ,)), dma((NZ,)), dma((NY,)), dma((NY,)),
            dma((NY, NZ)), dma((NY, NZ)), dma((NZ, NY)), dma((NZ, NY)),
            dma((2, NY, NZ)), dma((2, NY, NZ)),
            dma((NK,)), dma((NK,)), dma((NK,)), dma((NK,)), dma(()),
        ],
        compiler_params=pltpu.CompilerParams(collective_id=0, has_side_effects=True, vmem_limit_bytes=52_000_000),
        name="exchange",
    )(ow, ti, of, ac, va, vr, lm, st)


MAPS = NT * M
WIDE = NB * 1024 + MAPS
CH = 512


def mask_row(e):
    k, x = divmod(e, 3)
    return HALF * (k // 4) + 40 + 8 * (k % 4 // 2) + 3 * (k % 2) + x


VALUE_ROWS = (46, 47, 54)


def window_kernel(g_ref, s_ref, s2_ref, mk_ref, out, zz, mask, val, pp, pt, dh, dl, th, tl, sp, tp, out_ref, osem):
    lane_group = iota((ROWS, 128), 1) // 32

    def assemble(blk, _):
        parts = [g_ref[4 * blk + u] for u in range(4)]
        for b in range(NB):
            v = parts[3]
            for u in range(3):
                v = jnp.where(lane_group == (b + u) % 4, parts[u], v)
            lanes = pl.ds(pl.multiple_of(b * 1024 + blk * 128, 128), 128)
            for h in range(2):
                zz[32 * h : 32 * h + 32, lanes] = v[HALF * h : HALF * h + 32]
                zz[64 + 8 * h : 72 + 8 * h, lanes] = v[HALF * h + 32 : HALF * h + 40]
            for e in range(8 * b):
                r = mask_row(e)
                mask[e : e + 1, lanes] = v[r : r + 1]
            for j, r in enumerate(VALUE_ROWS):
                val[j : j + 1, lanes] = v[r : r + 1]
        return 0

    lax.fori_loop(0, 8, assemble, 0)
    unit = lax.rem(iota((M, MAPS), 1), M) == iota((M, MAPS), 0)
    zz[:, NB * 1024 :] = jnp.where(unit, 1.0, 0.0)
    grow = jnp.where(iota((8, MAPS), 0) == iota((8, MAPS), 1) // M, 1.0, 0.0)
    for b in range(NB):
        mask[8 * b : 8 * b + 8, NB * 1024 :] = mm(mk_ref[:, b, :].astype(F32), grow, TN)
    pp[...] = jnp.zeros_like(pp)

    for b in range(NB):
        lanes = slice(b * 1024, b * 1024 + 1024)
        prior = zz[:, lanes]
        accepted = val[0:1, lanes]
        observed = val[1:2, lanes]
        noise = val[2:3, lanes]
        mean = jnp.sum(prior, axis=0, keepdims=True) / M
        dev = prior - mean
        var = jnp.sum(dev * dev, axis=0, keepdims=True) / (M - 1) + epsilon
        den = var + noise
        shift = var / den * (observed - mean)
        factor = jnp.sqrt(noise / den) - 1.0
        inc = accepted * shift + (accepted * factor) * dev
        scl = dev * (1.0 / ((M - 1) * var))
        ih, il = split(inc)
        sh, sl = split(scl)
        for q in range(8):
            w = slice(128 * q, 128 * q + 128)
            left = jnp.concatenate([sh[:, w], sl[:, w]], axis=1)
            right = jnp.concatenate([ih[:, w], ih[:, w]], axis=1)
            prod = mm(left, right, NT_) + mm(sh[:, w], il[:, w], NT_)
            pp[b % 2, 80 * q : 80 * q + 80, 0:80] = prod
        ph, plo = split(jnp.transpose(pp[b % 2])[:M])
        pt[b, 0:M, :] = ph
        pt[b, M : 2 * M, :] = plo

        def change(at, wide, dh, dl, b=b):
            v = zz[:, at]
            d = v - jnp.sum(v, axis=0, keepdims=True) * (1.0 / M)
            hi, lo = split(d)
            for q in range(8):
                w = jnp.broadcast_to(mask[8 * b + q : 8 * b + q + 1, at], (16, wide)).astype(BF)
                for g in range(5):
                    rr = slice(80 * q + 16 * g, 80 * q + 16 * g + 16)
                    dh[rr, :] = hi[16 * g : 16 * g + 16] * w
                    dl[rr, :] = lo[16 * g : 16 * g + 16] * w
            both = mm(pt[b], dh[...], NN)
            rest = mm(pt[b, 0:M, :], dl[...], NN)
            zz[:, at] = v + (both[0:M] + (both[M : 2 * M] + rest))

        def update(i, _):
            change(pl.ds(pl.multiple_of((b + 1) * 1024 + i * CH, CH), CH), CH, dh, dl)
            return 0

        lax.fori_loop(0, (NB - 1 - b) * 1024 // CH, update, 0)
        change(slice(NB * 1024, WIDE), MAPS, th, tl)

    true = iota((M, M), 0)
    tk = true // MLOC
    ti = lax.rem(true, MLOC)
    place = jnp.where(ti < 8, 8 * tk + ti, 64 + 2 * tk + ti - 8)
    perm = jnp.where(iota((M, M), 1) == place, 1.0, 0.0).astype(BF)
    whole, part = split(zz[:, NB * 1024 :])
    tp[0:M, :] = mm(perm, whole, NN).astype(BF)
    tp[M : 2 * M, :] = mm(perm, part, NN).astype(BF)
    puts = []
    for t in range(NT):
        at = slice(TILE * t, TILE * t + TILE)
        for kk in range(NK):
            sp[t % 2, 8 * kk : 8 * kk + 8, :] = s_ref[kk, :, at]
            sp[t % 2, 64 + 2 * kk : 66 + 2 * kk, :] = s2_ref[
                kk, 2 * (t // 2) : 2 * (t // 2) + 2, TILE * (t % 2) : TILE * (t % 2) + TILE
            ]
        hi, lo = split(sp[t % 2])
        maps = tp[:, M * t : M * t + M]
        both = mm(maps, hi, NN)
        rest = mm(maps[0:M], lo, NN)
        out_ref[:, at] = both[0:M] + (both[M : 2 * M] + rest)
        puts.append(pltpu.make_async_copy(out_ref.at[:, at], out.at[:, at], osem.at[t]))
        puts[-1].start()
    for cp in puts:
        cp.wait()


def window_call(g, s, s2, mk):
    return pl.pallas_call(
        window_kernel,
        out_shape=jax.ShapeDtypeStruct((M, CELLS), F32),
        in_specs=[vm()] * 4,
        out_specs=hbm(),
        scratch_shapes=[
            pltpu.VMEM((M, WIDE), F32),
            pltpu.VMEM((32, WIDE), F32),
            pltpu.VMEM((8, NB * 1024), F32),
            pltpu.VMEM((2, 640, 128), F32),
            pltpu.VMEM((NB, 2 * M, 640), BF),
            pltpu.VMEM((640, CH), BF),
            pltpu.VMEM((640, CH), BF),
            pltpu.VMEM((640, MAPS), BF),
            pltpu.VMEM((640, MAPS), BF),
            pltpu.VMEM((2, M, TILE), F32),
            pltpu.VMEM((2 * M, MAPS), BF),
            pltpu.VMEM((M, CELLS), F32),
            pltpu.SemaphoreType.DMA((NT,)),
        ],
        compiler_params=pltpu.CompilerParams(vmem_limit_bytes=24 << 20),
        name="window",
    )(g, s, s2, mk)


def local(state, obs_value, obs_var, owner, tile_of, offsets, accept, loc_mask):
    places = jnp.transpose(offsets, (0, 2, 1))
    g, s, s2 = exchange_call(
        owner[:, :, 0], tile_of, places, accept, obs_value, obs_var, loc_mask, state
    )
    return window_call(g.reshape(NC, ROWS, 128), s, s2, loc_mask)


def solution(mesh):
    return jax.shard_map(
        local,
        mesh=mesh,
        in_specs=(
            P("mem", "cols"),
            P(None, "cols"),
            P(None, "cols"),
            P(None, "cols", None),
            P(None, "cols"),
            P(None, "cols", None),
            P(None, "cols"),
            P(("cols", "mem"), None, None),
        ),
        out_specs=P(None, ("cols", "mem")),
        check_vma=False,
    )
```

```python
import jax
import jax.numpy as jnp
from jax import lax
from jax.experimental import pallas as pl
from jax.experimental.pallas import tpu as pltpu
from jax.sharding import PartitionSpec as P

epsilon = 1e-05
MESH = pl.DeviceIdType.MESH
F32 = jnp.float32
BF = jnp.bfloat16
I32 = jnp.int32

NB = 4
NC = 32
NK = 8
MLOC = 10
M = 80
NY = 4
NZ = 8
TILE = 512
NT = 8
CELLS = 4096
RA = 40
RB = 16
HALF = RA + RB
ROWS = 2 * HALF


def vm():
    return pl.BlockSpec(memory_space=pltpu.VMEM)


def sm():
    return pl.BlockSpec(memory_space=pltpu.SMEM)


def hbm():
    return pl.BlockSpec(memory_space=pl.ANY)


def iota(shape, axis):
    return lax.broadcasted_iota(I32, shape, axis)


def split(v):
    hi = v.astype(BF)
    lo = (v - hi.astype(F32)).astype(BF)
    return hi, lo


def mm(a, b, dims):
    return lax.dot_general(a, b, (dims, ((), ())), preferred_element_type=F32)


NN = ((1,), (0,))
NT_ = ((1,), (1,))
TN = ((0,), (0,))
def send(src, dst, ssem, rsem, dev):
    cp = pltpu.make_async_remote_copy(
        src_ref=src, dst_ref=dst, send_sem=ssem, recv_sem=rsem, device_id=dev, device_id_type=MESH
    )
    cp.start()
    return cp


FAR = sorted(
    ((dy, dz) for dy in range(NY) for dz in range(NZ) if dy + dz > 0),
    key=lambda o: -(min(o[0], NY - o[0]) + min(o[1], NZ - o[1])),
)
FAR_K = (4, 3, 5, 2, 6, 1, 7)
NEAR_Y = (1, 3, 2)
NEAR_Z = (1, 7, 2, 6, 3, 5, 4)
EARLY = (4, 2, 7, 1)
LATE = (5, 3, 6)


def exchange_kernel(
    ow_in, ti_in, of_in, ac_in, va_in, vr_in, lm_in, st, g_ref, s_ref, s2_ref,
    ow, ti, of, ac, va, vr, lm, ins,
    stv, tiled, fi, fl, mv, mrow, rr, rsm, mks, xs, zrow, rz, blocks, tail,
    ls, own, cs, ms, mr, ks, kr, ss, rs, xss, xsr, a1s, a1r, b1s, b1r, a2s, a2r, b2s, b2r,
    pas, par, ts, tr, us, ur, own2,
):
    c = lax.axis_index("cols")
    k = lax.axis_index("mem")
    y = c // NZ
    z = lax.rem(c, NZ)
    core = lax.rem(k, 2)
    bar = pltpu.get_barrier_semaphore()
    cols = [(dy * NZ + dz, lax.rem(y + dy, NY) * NZ + lax.rem(z + dz, NZ)) for dy, dz in FAR]
    for d, p in cols:
        pl.semaphore_signal(bar, inc=1, device_id=(p, k), device_id_type=MESH)
    for d in FAR_K:
        pl.semaphore_signal(bar, inc=1, device_id=(c, lax.rem(k + d, NK)), device_id_type=MESH)
    small = [
        pltpu.make_async_copy(src, dst, ins.at[n])
        for n, (src, dst) in enumerate(
            ((ow_in, ow), (ti_in, ti), (of_in, of), (ac_in, ac), (va_in, va), (vr_in, vr), (lm_in, lm))
        )
    ]
    for cp in small:
        cp.start()
    load = pltpu.make_async_copy(st, stv, ls)
    load.start()
    for cp in small:
        cp.wait()
    mv[...] = jnp.zeros_like(mv)
    tiles = ti[...] * TILE
    cells = [tiles + of[:, p, :] for p in range(4)]
    places = [ow[...], cells[0] + (cells[1] << 15), cells[2] + (cells[3] << 15)]
    fields = [ac[...].astype(F32), va[...], vr[...]]
    for b in range(NB):
        at = slice(32 * b, 32 * b + 32)
        for f in range(3):
            fi[f : f + 1, at] = places[f][b : b + 1, :]
            fl[f : f + 1, at] = fields[f][b : b + 1, :]
        mv[:, 8 * b : 8 * b + 8] = lm[:, b, :].astype(F32)
    r128 = iota((128, 128), 0)
    c128 = iota((128, 128), 1)
    lane32 = iota((NC, 128), 1)
    within = lane32 & 31
    hoti = jnp.where(iota((NC, 128), 0) == fi[0:1, :], 1, 0)
    seen = hoti
    for h in (1, 2, 4, 8, 16):
        seen = seen + jnp.where(within >= h, pltpu.roll(seen, h, 1), 0)
    slots = jnp.zeros((NC, 128), I32)
    for r in range(2):
        for w in range(2):
            v = jnp.where((hoti == 1) & (seen == r + 1), fi[w + 1 : w + 2, :], 0)
            for h in (1, 2, 4, 8, 16):
                v = v + pltpu.roll(v, 128 - h, 1)
            for p, cell in ((2 * w, v & 32767), (2 * w + 1, (v >> 15) & 32767)):
                for f, word in ((p, cell >> 7), (p + 4, cell & 127)):
                    spot = 8 * r + f
                    word = word if spot == 0 else pltpu.roll(word, spot, 1)
                    slots = jnp.where(within == spot, word, slots)
    mrow[...] = slots.reshape(NC, 1, 128)
    hot = hoti.astype(F32)
    rank = jnp.sum((hoti * (seen - 1)).astype(F32), axis=0, keepdims=True)
    load.wait()
    for t in range(NK * CELLS // 128):
        tiled[t] = stv[:, 128 * t : 128 * t + 128]
    for p in range(NK):
        for j in range(4):
            at = CELLS * p + 1024 * j
            tail[p, 2 * j : 2 * j + 2, :] = stv[8:10, at : at + 1024]
    pl.semaphore_wait(bar, NC - 1 + NK - 1)

    ask = []
    for d, p in cols:
        ask.append(send(mrow.at[p], rr.at[c], ms.at[d], mr.at[d], (p, k)))
    maps = []
    for d in FAR_K:
        maps.append(send(mv, mks.at[k], ks.at[d], kr.at[d], (c, lax.rem(k + d, NK))))
    rr[c] = mrow[c]
    mks[k] = mv[...]
    def move(d):
        p = lax.rem(k + d, NK)
        part = stv.at[0:8, pl.ds(pl.multiple_of(p * CELLS, CELLS), CELLS)]
        return [
            send(part, s_ref.at[k], ts.at[d], tr.at[d], (c, p)),
            send(tail.at[p], s2_ref.at[k], us.at[d], ur.at[d], (c, p)),
        ]

    moves = [cp for d in EARLY for cp in move(d)]
    keep = pltpu.make_async_copy(
        stv.at[0:8, pl.ds(pl.multiple_of(k * CELLS, CELLS), CELLS)], s_ref.at[k], own
    )
    keep.start()
    keep2 = pltpu.make_async_copy(tail.at[k], s2_ref.at[k], own2)
    keep2.start()
    for cp in maps:
        cp.wait()
    pick = lax.rem(c128, 16) - 10
    chosen = jnp.where((pick >= 0) & (pick < 3) & (r128 == 3 * k + pick), 1.0, 0.0)
    table = mm(mks[...].reshape(64, 128).astype(BF), chosen.astype(BF), NN).astype(BF)
    for cp in ask:
        cp.wait()
    scal = pltpu.make_async_copy(rr, rsm, cs)
    scal.start()
    got = rr[...].reshape(NC, 128)
    extra = jnp.zeros((NC, 128), F32)
    for q in range(8):
        word = 32 * (q // 2) + 8 * (q % 2)
        tile = got[:, word : word + 1] >> 2
        at_tile = jnp.where(iota((NC, 64), 1) == tile, 1.0, 0.0).astype(BF)
        extra = jnp.where(lane32 // 16 == q, mm(at_tile, table, NN), extra)
    scal.wait()
    lane = iota((MLOC, 128), 1)

    def priors(i, accs):
        here = lane == i
        out = []
        for q in range(8):
            v = jnp.zeros((MLOC, 128), F32)
            word = 32 * (q // 2) + 8 * (q % 2)
            for p in range(4):
                hit = lane == rsm[i, 0, word + 4 + p]
                v = v + jnp.where(hit, tiled[rsm[i, 0, word + p]], 0.0)
            out.append(jnp.where(here, jnp.sum(v, axis=1, keepdims=True), accs[q]))
        return tuple(out)

    accs = lax.fori_loop(0, NC, priors, tuple(jnp.zeros((MLOC, 128), F32) for _ in range(8)), unroll=True)
    xs[...] = jnp.zeros_like(xs)
    for q in range(8):
        xs[16 * q : 16 * q + MLOC, :] = accs[q] * 0.25
    zr = jnp.transpose(xs[...])[:NC] + extra
    zrow[...] = zr.reshape(NC, 1, 128)
    back = []
    for d, p in cols:
        back.append(send(zrow.at[p], rz.at[c], ss.at[d], rs.at[d], (p, k)))
    rz[c] = zrow[c]
    for cp in back:
        cp.wait()
    full = lax.dot_general(
        rz[...].reshape(NC, 128), hot, (TN, ((), ())),
        precision=lax.Precision.HIGHEST, preferred_element_type=F32,
    )
    batch = iota((1, 128), 1) // 32
    blk = jnp.zeros((16, 128), F32)
    for q in range(8):
        mine = (batch == q // 2) & (rank == float(q % 2))
        blk = blk + jnp.where(mine, full[16 * q : 16 * q + 16, :], 0.0)
    row16 = iota((16, 128), 0)
    for j in range(3):
        blk = jnp.where(row16 == 13 + j, fl[j : j + 1, :], blk)
    turned = blk
    around = lax.rem(z, 4)
    for j in range(1, 4):
        turned = jnp.where(around == j, pltpu.roll(blk, 32 * j, 1), turned)
    blocks[k] = turned
    block = blocks.at[k]
    step = []
    for d in FAR_K:
        step.append(send(block, block, xss.at[d], xsr.at[d], (c, lax.rem(k + d, NK))))
    for cp in step:
        cp.wait()
    sub8 = iota((8, 128), 0)
    for h in range(2):
        tails = [blocks[4 * h + u, 8:16, :] for u in range(4)]
        for u in range(4):
            g_ref[y, z, HALF * h + 8 * u : HALF * h + 8 * u + 8, :] = blocks[4 * h + u, 0:8, :]
        last = tails[0]
        for u in range(1, 4):
            last = jnp.where(sub8 // 2 == u, pltpu.roll(tails[u], 2 * u, 0), last)
        g_ref[y, z, HALF * h + 32 : HALF * h + 40, :] = last
        low = jnp.where(sub8 < 3, pltpu.roll(tails[0], 6, 0), pltpu.roll(tails[1], 1, 0))
        low = jnp.where(sub8 >= 6, pltpu.roll(tails[0], 1, 0), low)
        high = jnp.where(sub8 < 3, pltpu.roll(tails[2], 6, 0), pltpu.roll(tails[3], 1, 0))
        high = jnp.where(sub8 >= 6, pltpu.roll(tails[2], 7, 0), high)
        g_ref[y, z, HALF * h + 40 : HALF * h + 48, :] = low
        g_ref[y, z, HALF * h + 48 : HALF * h + 56, :] = high
    ra = pl.multiple_of(HALF * core, 8)
    rb = pl.multiple_of(HALF * core + RA, 8)
    mate = (c, k + 1 - 2 * core)
    y_at = [lax.rem(y + d, NY) for d in range(NY)]
    z_at = [lax.rem(z + d, NZ) for d in range(NZ)]

    def piece_a(dy, dz):
        return g_ref.at[y_at[(-dy) % NY], z_at[(-dz) % NZ], pl.ds(ra, RA), :]

    def piece_b(dy, dz):
        return g_ref.at[y_at[(-dy) % NY], z_at[(-dz) % NZ], pl.ds(rb, RB), :]

    out_a = {}
    out_b = {}
    pair = []

    def along_y(e):
        piece = piece_a(0, e)
        for d in NEAR_Y:
            out_a[d, e] = send(piece, piece, a2s.at[d, e], a2r.at[d, e], (y_at[d] * NZ + z, k))

    def along_z(e):
        piece = piece_b(e, 0)
        for d in NEAR_Z:
            out_b[d, e] = send(piece, piece, b2s.at[d, e], b2r.at[d, e], (y * NZ + z_at[d], k))

    def to_mate(piece, n, dy, dz):
        pair.append(send(piece, piece, pas.at[n, dy, dz], par.at[n, dy, dz], mate))

    own_a = piece_a(0, 0)
    own_b = piece_b(0, 0)
    first_a = {}
    first_b = {}
    for d in NEAR_Z:
        first_a[d] = send(own_a, own_a, a1s.at[d], a1r.at[d], (y * NZ + z_at[d], k))
    for d in NEAR_Y:
        first_b[d] = send(own_b, own_b, b1s.at[d], b1r.at[d], (y_at[d] * NZ + z, k))
    along_y(0)
    along_z(0)
    moves += [cp for d in LATE for cp in move(d)]
    for kind, e in (("b", 1), ("a", 1), ("b", 3), ("a", 7), ("a", 2), ("b", 2), ("a", 6), ("a", 3), ("a", 5), ("a", 4)):
        if kind == "a":
            first_a[e].wait_recv()
            along_y(e)
            to_mate(piece_a(0, e), 0, 0, e)
        else:
            first_b[e].wait_recv()
            along_z(e)
            to_mate(piece_b(e, 0), 1, e, 0)
    order = [(0, d, e) for d in NEAR_Y for e in range(NZ)] + [(1, e, d) for d in NEAR_Z for e in range(NY)]
    order.sort(key=lambda o: (min(o[1], NY - o[1]) + min(o[2], NZ - o[2])))
    for n, dy, dz in order:
        if n == 0:
            out_a[dy, dz].wait_recv()
            to_mate(piece_a(dy, dz), 0, dy, dz)
        else:
            out_b[dz, dy].wait_recv()
            to_mate(piece_b(dy, dz), 1, dy, dz)
    for group in (first_a, first_b, out_a, out_b):
        for cp in group.values():
            cp.wait_send()
    keep.wait()
    keep2.wait()
    for cp in moves + pair:
        cp.wait()


def exchange_call(ow, ti, of, ac, va, vr, lm, st):
    dma = pltpu.SemaphoreType.DMA
    row = pltpu.VMEM((NC, 1, 128), F32)
    irow = pltpu.VMEM((NC, 1, 128), I32)
    return pl.pallas_call(
        exchange_kernel,
        out_shape=(
            jax.ShapeDtypeStruct((NY, NZ, ROWS, 128), F32),
            jax.ShapeDtypeStruct((NK, 8, CELLS), F32),
            jax.ShapeDtypeStruct((NK, 8, 1024), F32),
        ),
        in_specs=[pl.BlockSpec(memory_space=pltpu.HBM)] * 8,
        out_specs=(vm(), hbm(), hbm()),
        scratch_shapes=[
            pltpu.VMEM((NB, 32), I32),
            pltpu.VMEM((NB, 32), I32),
            pltpu.VMEM((NB, 4, 32), I32),
            pltpu.VMEM((NB, 32), I32),
            pltpu.VMEM((NB, 32), F32),
            pltpu.VMEM((NB, 32), F32),
            pltpu.VMEM((NT, NB, 8), I32),
            dma((7,)),
            pltpu.VMEM((MLOC, NK * CELLS), F32),
            pltpu.VMEM((NK * CELLS // 128, MLOC, 128), F32),
            pltpu.VMEM((8, 128), I32),
            pltpu.VMEM((8, 128), F32),
            pltpu.VMEM((8, 128), F32),
            irow, irow,
            pltpu.SMEM((NC, 1, 128), I32),
            pltpu.VMEM((NK, 8, 128), F32),
            pltpu.VMEM((128, 128), F32),
            row, row,
            pltpu.VMEM((NK, 16, 128), F32),
            pltpu.VMEM((NK, 8, 1024), F32),
            dma(()), dma(()), dma(()),
            dma((NC,)), dma((NC,)), dma((NK,)), dma((NK,)),
            dma((NC,)), dma((NC,)), dma((NK,)), dma((NK,)),
            dma((NZ,)), dma((NZ,)), dma((NY,)), dma((NY,)),
            dma((NY, NZ)), dma((NY, NZ)), dma((NZ, NY)), dma((NZ, NY)),
            dma((2, NY, NZ)), dma((2, NY, NZ)),
            dma((NK,)), dma((NK,)), dma((NK,)), dma((NK,)), dma(()),
        ],
        compiler_params=pltpu.CompilerParams(collective_id=0, has_side_effects=True, vmem_limit_bytes=52_000_000),
        name="exchange",
    )(ow, ti, of, ac, va, vr, lm, st)


MAPS = NT * M
WIDE = NB * 1024 + MAPS
CH = 512


def mask_row(e):
    k, x = divmod(e, 3)
    return HALF * (k // 4) + 40 + 8 * (k % 4 // 2) + 3 * (k % 2) + x


VALUE_ROWS = (46, 47, 54)


def window_kernel(g_ref, s_ref, s2_ref, mk_ref, out, zz, mask, val, pp, pt, dh, dl, th, tl, sp, tp, out_ref, osem):
    lane_group = iota((ROWS, 128), 1) // 32

    def assemble(blk, _):
        parts = [g_ref[4 * blk + u] for u in range(4)]
        for b in range(NB):
            v = parts[3]
            for u in range(3):
                v = jnp.where(lane_group == (b + u) % 4, parts[u], v)
            lanes = pl.ds(pl.multiple_of(b * 1024 + blk * 128, 128), 128)
            for h in range(2):
                zz[32 * h : 32 * h + 32, lanes] = v[HALF * h : HALF * h + 32]
                zz[64 + 8 * h : 72 + 8 * h, lanes] = v[HALF * h + 32 : HALF * h + 40]
            for e in range(8 * b):
                r = mask_row(e)
                mask[e : e + 1, lanes] = v[r : r + 1]
            for j, r in enumerate(VALUE_ROWS):
                val[j : j + 1, lanes] = v[r : r + 1]
        return 0

    lax.fori_loop(0, 8, assemble, 0)
    unit = lax.rem(iota((M, MAPS), 1), M) == iota((M, MAPS), 0)
    zz[:, NB * 1024 :] = jnp.where(unit, 1.0, 0.0)
    grow = jnp.where(iota((8, MAPS), 0) == iota((8, MAPS), 1) // M, 1.0, 0.0)
    for b in range(NB):
        mask[8 * b : 8 * b + 8, NB * 1024 :] = mm(mk_ref[:, b, :].astype(F32), grow, TN)
    pp[...] = jnp.zeros_like(pp)

    for b in range(NB):
        lanes = slice(b * 1024, b * 1024 + 1024)
        prior = zz[:, lanes]
        accepted = val[0:1, lanes]
        observed = val[1:2, lanes]
        noise = val[2:3, lanes]
        mean = jnp.sum(prior, axis=0, keepdims=True) / M
        dev = prior - mean
        var = jnp.sum(dev * dev, axis=0, keepdims=True) / (M - 1) + epsilon
        den = var + noise
        shift = var / den * (observed - mean)
        factor = jnp.sqrt(noise / den) - 1.0
        inc = accepted * shift + (accepted * factor) * dev
        scl = dev * (1.0 / ((M - 1) * var))
        ih, il = split(inc)
        sh, sl = split(scl)
        for q in range(8):
            w = slice(128 * q, 128 * q + 128)
            left = jnp.concatenate([sh[:, w], sl[:, w]], axis=1)
            right = jnp.concatenate([ih[:, w], ih[:, w]], axis=1)
            prod = mm(left, right, NT_) + mm(sh[:, w], il[:, w], NT_)
            pp[b % 2, 80 * q : 80 * q + 80, 0:80] = prod
        ph, plo = split(jnp.transpose(pp[b % 2])[:M])
        pt[b, 0:M, :] = ph
        pt[b, M : 2 * M, :] = plo

        def change(at, wide, dh, dl, b=b):
            v = zz[:, at]
            d = v - jnp.sum(v, axis=0, keepdims=True) * (1.0 / M)
            hi, lo = split(d)
            for q in range(8):
                w = jnp.broadcast_to(mask[8 * b + q : 8 * b + q + 1, at], (16, wide)).astype(BF)
                for g in range(5):
                    rr = slice(80 * q + 16 * g, 80 * q + 16 * g + 16)
                    dh[rr, :] = hi[16 * g : 16 * g + 16] * w
                    dl[rr, :] = lo[16 * g : 16 * g + 16] * w
            both = mm(pt[b], dh[...], NN)
            rest = mm(pt[b, 0:M, :], dl[...], NN)
            zz[:, at] = v + (both[0:M] + (both[M : 2 * M] + rest))

        def update(i, _):
            change(pl.ds(pl.multiple_of((b + 1) * 1024 + i * CH, CH), CH), CH, dh, dl)
            return 0

        lax.fori_loop(0, (NB - 1 - b) * 1024 // CH, update, 0)
        change(slice(NB * 1024, WIDE), MAPS, th, tl)

    true = iota((M, M), 0)
    tk = true // MLOC
    ti = lax.rem(true, MLOC)
    place = jnp.where(ti < 8, 8 * tk + ti, 64 + 2 * tk + ti - 8)
    perm = jnp.where(iota((M, M), 1) == place, 1.0, 0.0).astype(BF)
    whole, part = split(zz[:, NB * 1024 :])
    tp[0:M, :] = mm(perm, whole, NN).astype(BF)
    tp[M : 2 * M, :] = mm(perm, part, NN).astype(BF)
    puts = []
    for t in range(NT):
        at = slice(TILE * t, TILE * t + TILE)
        for kk in range(NK):
            sp[t % 2, 8 * kk : 8 * kk + 8, :] = s_ref[kk, :, at]
            sp[t % 2, 64 + 2 * kk : 66 + 2 * kk, :] = s2_ref[
                kk, 2 * (t // 2) : 2 * (t // 2) + 2, TILE * (t % 2) : TILE * (t % 2) + TILE
            ]
        hi, lo = split(sp[t % 2])
        maps = tp[:, M * t : M * t + M]
        both = mm(maps, hi, NN)
        rest = mm(maps[0:M], lo, NN)
        out_ref[:, at] = both[0:M] + (both[M : 2 * M] + rest)
        puts.append(pltpu.make_async_copy(out_ref.at[:, at], out.at[:, at], osem.at[t]))
        puts[-1].start()
    for cp in puts:
        cp.wait()


def window_call(g, s, s2, mk):
    return pl.pallas_call(
        window_kernel,
        out_shape=jax.ShapeDtypeStruct((M, CELLS), F32),
        in_specs=[vm()] * 4,
        out_specs=hbm(),
        scratch_shapes=[
            pltpu.VMEM((M, WIDE), F32),
            pltpu.VMEM((32, WIDE), F32),
            pltpu.VMEM((8, NB * 1024), F32),
            pltpu.VMEM((2, 640, 128), F32),
            pltpu.VMEM((NB, 2 * M, 640), BF),
            pltpu.VMEM((640, CH), BF),
            pltpu.VMEM((640, CH), BF),
            pltpu.VMEM((640, MAPS), BF),
            pltpu.VMEM((640, MAPS), BF),
            pltpu.VMEM((2, M, TILE), F32),
            pltpu.VMEM((2 * M, MAPS), BF),
            pltpu.VMEM((M, CELLS), F32),
            pltpu.SemaphoreType.DMA((NT,)),
        ],
        compiler_params=pltpu.CompilerParams(vmem_limit_bytes=24 << 20),
        name="window",
    )(g, s, s2, mk)


def local(state, obs_value, obs_var, owner, tile_of, offsets, accept, loc_mask):
    places = jnp.transpose(offsets, (0, 2, 1))
    given = (owner[:, :, 0], tile_of, places, accept, obs_value, obs_var, loc_mask, state)
    g, s, s2 = exchange_call(*(pltpu.with_memory_space_constraint(x, pltpu.HBM) for x in given))
    return window_call(g.reshape(NC, ROWS, 128), s, s2, loc_mask)


def solution(mesh):
    return jax.shard_map(
        local,
        mesh=mesh,
        in_specs=(
            P("mem", "cols"),
            P(None, "cols"),
            P(None, "cols"),
            P(None, "cols", None),
            P(None, "cols"),
            P(None, "cols", None),
            P(None, "cols"),
            P(("cols", "mem"), None, None),
        ),
        out_specs=P(None, ("cols", "mem")),
        check_vma=False,
    )
```

```python
import jax
import jax.numpy as jnp
from jax import lax
from jax.experimental import pallas as pl
from jax.experimental.pallas import tpu as pltpu
from jax.sharding import PartitionSpec as P

epsilon = 1e-05
MESH = pl.DeviceIdType.MESH
F32 = jnp.float32
BF = jnp.bfloat16
I32 = jnp.int32

NB = 4
NC = 32
NK = 8
MLOC = 10
M = 80
NY = 4
NZ = 8
TILE = 512
NT = 8
CELLS = 4096
RA = 40
RB = 16
HALF = RA + RB
ROWS = 2 * HALF


def vm():
    return pl.BlockSpec(memory_space=pltpu.VMEM)


def sm():
    return pl.BlockSpec(memory_space=pltpu.SMEM)


def hbm():
    return pl.BlockSpec(memory_space=pl.ANY)


def iota(shape, axis):
    return lax.broadcasted_iota(I32, shape, axis)


def split(v):
    hi = v.astype(BF)
    lo = (v - hi.astype(F32)).astype(BF)
    return hi, lo


def mm(a, b, dims):
    return lax.dot_general(a, b, (dims, ((), ())), preferred_element_type=F32)


NN = ((1,), (0,))
NT_ = ((1,), (1,))
TN = ((0,), (0,))
def send(src, dst, ssem, rsem, dev):
    cp = pltpu.make_async_remote_copy(
        src_ref=src, dst_ref=dst, send_sem=ssem, recv_sem=rsem, device_id=dev, device_id_type=MESH
    )
    cp.start()
    return cp


FAR = sorted(
    ((dy, dz) for dy in range(NY) for dz in range(NZ) if dy + dz > 0),
    key=lambda o: -(min(o[0], NY - o[0]) + min(o[1], NZ - o[1])),
)
FAR_K = (4, 3, 5, 2, 6, 1, 7)
NEAR_Y = (1, 3, 2)
NEAR_Z = (1, 7, 2, 6, 3, 5, 4)
EARLY = (4, 2, 7, 1)
LATE = (5, 3, 6)


def exchange_kernel(
    ow_in, ti_in, of_in, ac_in, va_in, vr_in, lm_in, st, g_ref, s_ref, s2_ref,
    ow, ti, of, ac, va, vr, lm, ins,
    stv, tiled, fi, fl, mv, mrow, rr, rsm, mks, xs, zrow, rz, blocks, tail,
    ls, own, cs, ms, mr, ks, kr, ss, rs, xss, xsr, a1s, a1r, b1s, b1r, a2s, a2r, b2s, b2r,
    pas, par, ts, tr, us, ur, own2,
):
    c = lax.axis_index("cols")
    k = lax.axis_index("mem")
    y = c // NZ
    z = lax.rem(c, NZ)
    core = lax.rem(k, 2)
    bar = pltpu.get_barrier_semaphore()
    cols = [(dy * NZ + dz, lax.rem(y + dy, NY) * NZ + lax.rem(z + dz, NZ)) for dy, dz in FAR]
    for d, p in cols:
        pl.semaphore_signal(bar, inc=1, device_id=(p, k), device_id_type=MESH)
    for d in FAR_K:
        pl.semaphore_signal(bar, inc=1, device_id=(c, lax.rem(k + d, NK)), device_id_type=MESH)
    small = [
        pltpu.make_async_copy(src, dst, ins.at[n])
        for n, (src, dst) in enumerate(
            ((ow_in, ow), (ti_in, ti), (of_in, of), (ac_in, ac), (va_in, va), (vr_in, vr), (lm_in, lm))
        )
    ]
    for cp in small:
        cp.start()
    load = pltpu.make_async_copy(st, stv, ls)
    load.start()
    for cp in small:
        cp.wait()
    mv[...] = jnp.zeros_like(mv)
    tiles = ti[...] * TILE
    cells = [tiles + of[:, p, :] for p in range(4)]
    places = [ow[...], cells[0] + (cells[1] << 15), cells[2] + (cells[3] << 15)]
    fields = [ac[...].astype(F32), va[...], vr[...]]
    for b in range(NB):
        at = slice(32 * b, 32 * b + 32)
        for f in range(3):
            fi[f : f + 1, at] = places[f][b : b + 1, :]
            fl[f : f + 1, at] = fields[f][b : b + 1, :]
        mv[:, 8 * b : 8 * b + 8] = lm[:, b, :].astype(F32)
    r128 = iota((128, 128), 0)
    c128 = iota((128, 128), 1)
    lane32 = iota((NC, 128), 1)
    within = lane32 & 31
    hoti = jnp.where(iota((NC, 128), 0) == fi[0:1, :], 1, 0)
    seen = hoti
    for h in (1, 2, 4, 8, 16):
        seen = seen + jnp.where(within >= h, pltpu.roll(seen, h, 1), 0)
    slots = jnp.zeros((NC, 128), I32)
    for r in range(2):
        for w in range(2):
            v = jnp.where((hoti == 1) & (seen == r + 1), fi[w + 1 : w + 2, :], 0)
            for h in (1, 2, 4, 8, 16):
                v = v + pltpu.roll(v, 128 - h, 1)
            for p, cell in ((2 * w, v & 32767), (2 * w + 1, (v >> 15) & 32767)):
                for f, word in ((p, cell >> 7), (p + 4, cell & 127)):
                    spot = 8 * r + f
                    word = word if spot == 0 else pltpu.roll(word, spot, 1)
                    slots = jnp.where(within == spot, word, slots)
    mrow[...] = slots.reshape(NC, 1, 128)
    hot = hoti.astype(F32)
    rank = jnp.sum((hoti * (seen - 1)).astype(F32), axis=0, keepdims=True)
    load.wait()
    for t in range(NK * CELLS // 128):
        tiled[t] = stv[:, 128 * t : 128 * t + 128]
    for p in range(NK):
        for j in range(4):
            at = CELLS * p + 1024 * j
            tail[p, 2 * j : 2 * j + 2, :] = stv[8:10, at : at + 1024]
    pl.semaphore_wait(bar, NC - 1 + NK - 1)

    ask = []
    for d, p in cols:
        ask.append(send(mrow.at[p], rr.at[c], ms.at[d], mr.at[d], (p, k)))
    maps = []
    for d in FAR_K:
        maps.append(send(mv, mks.at[k], ks.at[d], kr.at[d], (c, lax.rem(k + d, NK))))
    rr[c] = mrow[c]
    mks[k] = mv[...]
    def move(d):
        p = lax.rem(k + d, NK)
        part = stv.at[0:8, pl.ds(pl.multiple_of(p * CELLS, CELLS), CELLS)]
        return [
            send(part, s_ref.at[k], ts.at[d], tr.at[d], (c, p)),
            send(tail.at[p], s2_ref.at[k], us.at[d], ur.at[d], (c, p)),
        ]

    moves = [cp for d in EARLY for cp in move(d)]
    keep = pltpu.make_async_copy(
        stv.at[0:8, pl.ds(pl.multiple_of(k * CELLS, CELLS), CELLS)], s_ref.at[k], own
    )
    keep.start()
    keep2 = pltpu.make_async_copy(tail.at[k], s2_ref.at[k], own2)
    keep2.start()
    for cp in maps:
        cp.wait()
    pick = lax.rem(c128, 16) - 10
    chosen = jnp.where((pick >= 0) & (pick < 3) & (r128 == 3 * k + pick), 1.0, 0.0)
    table = mm(mks[...].reshape(64, 128).astype(BF), chosen.astype(BF), NN).astype(BF)
    for cp in ask:
        cp.wait()
    scal = pltpu.make_async_copy(rr, rsm, cs)
    scal.start()
    got = rr[...].reshape(NC, 128)
    extra = jnp.zeros((NC, 128), F32)
    for q in range(8):
        word = 32 * (q // 2) + 8 * (q % 2)
        tile = got[:, word : word + 1] >> 2
        at_tile = jnp.where(iota((NC, 64), 1) == tile, 1.0, 0.0).astype(BF)
        extra = jnp.where(lane32 // 16 == q, mm(at_tile, table, NN), extra)
    scal.wait()
    lane = iota((MLOC, 128), 1)

    def priors(i, accs):
        here = lane == i
        out = []
        for q in range(8):
            v = jnp.zeros((MLOC, 128), F32)
            word = 32 * (q // 2) + 8 * (q % 2)
            for p in range(4):
                hit = lane == rsm[i, 0, word + 4 + p]
                v = v + jnp.where(hit, tiled[rsm[i, 0, word + p]], 0.0)
            out.append(jnp.where(here, jnp.sum(v, axis=1, keepdims=True), accs[q]))
        return tuple(out)

    accs = lax.fori_loop(0, NC, priors, tuple(jnp.zeros((MLOC, 128), F32) for _ in range(8)), unroll=True)
    xs[...] = jnp.zeros_like(xs)
    for q in range(8):
        xs[16 * q : 16 * q + MLOC, :] = accs[q] * 0.25
    zr = jnp.transpose(xs[...])[:NC] + extra
    zrow[...] = zr.reshape(NC, 1, 128)
    back = []
    for d, p in cols:
        back.append(send(zrow.at[p], rz.at[c], ss.at[d], rs.at[d], (p, k)))
    rz[c] = zrow[c]
    for cp in back:
        cp.wait()
    full = lax.dot_general(
        rz[...].reshape(NC, 128), hot, (TN, ((), ())),
        precision=lax.Precision.HIGHEST, preferred_element_type=F32,
    )
    batch = iota((1, 128), 1) // 32
    blk = jnp.zeros((16, 128), F32)
    for q in range(8):
        mine = (batch == q // 2) & (rank == float(q % 2))
        blk = blk + jnp.where(mine, full[16 * q : 16 * q + 16, :], 0.0)
    row16 = iota((16, 128), 0)
    for j in range(3):
        blk = jnp.where(row16 == 13 + j, fl[j : j + 1, :], blk)
    turned = blk
    around = lax.rem(z, 4)
    for j in range(1, 4):
        turned = jnp.where(around == j, pltpu.roll(blk, 32 * j, 1), turned)
    blocks[k] = turned
    block = blocks.at[k]
    step = []
    for d in FAR_K:
        step.append(send(block, block, xss.at[d], xsr.at[d], (c, lax.rem(k + d, NK))))
    for cp in step:
        cp.wait()
    sub8 = iota((8, 128), 0)
    for h in range(2):
        tails = [blocks[4 * h + u, 8:16, :] for u in range(4)]
        for u in range(4):
            g_ref[y, z, HALF * h + 8 * u : HALF * h + 8 * u + 8, :] = blocks[4 * h + u, 0:8, :]
        last = tails[0]
        for u in range(1, 4):
            last = jnp.where(sub8 // 2 == u, pltpu.roll(tails[u], 2 * u, 0), last)
        g_ref[y, z, HALF * h + 32 : HALF * h + 40, :] = last
        low = jnp.where(sub8 < 3, pltpu.roll(tails[0], 6, 0), pltpu.roll(tails[1], 1, 0))
        low = jnp.where(sub8 >= 6, pltpu.roll(tails[0], 1, 0), low)
        high = jnp.where(sub8 < 3, pltpu.roll(tails[2], 6, 0), pltpu.roll(tails[3], 1, 0))
        high = jnp.where(sub8 >= 6, pltpu.roll(tails[2], 7, 0), high)
        g_ref[y, z, HALF * h + 40 : HALF * h + 48, :] = low
        g_ref[y, z, HALF * h + 48 : HALF * h + 56, :] = high
    ra = pl.multiple_of(HALF * core, 8)
    rb = pl.multiple_of(HALF * core + RA, 8)
    mate = (c, k + 1 - 2 * core)
    y_at = [lax.rem(y + d, NY) for d in range(NY)]
    z_at = [lax.rem(z + d, NZ) for d in range(NZ)]

    def piece_a(dy, dz):
        return g_ref.at[y_at[(-dy) % NY], z_at[(-dz) % NZ], pl.ds(ra, RA), :]

    def piece_b(dy, dz):
        return g_ref.at[y_at[(-dy) % NY], z_at[(-dz) % NZ], pl.ds(rb, RB), :]

    out_a = {}
    out_b = {}
    pair = []

    def along_y(e):
        piece = piece_a(0, e)
        for d in NEAR_Y:
            out_a[d, e] = send(piece, piece, a2s.at[d, e], a2r.at[d, e], (y_at[d] * NZ + z, k))

    def along_z(e):
        piece = piece_b(e, 0)
        for d in NEAR_Z:
            out_b[d, e] = send(piece, piece, b2s.at[d, e], b2r.at[d, e], (y * NZ + z_at[d], k))

    def to_mate(piece, n, dy, dz):
        pair.append(send(piece, piece, pas.at[n, dy, dz], par.at[n, dy, dz], mate))

    own_a = piece_a(0, 0)
    own_b = piece_b(0, 0)
    first_a = {}
    first_b = {}
    for d in NEAR_Z:
        first_a[d] = send(own_a, own_a, a1s.at[d], a1r.at[d], (y * NZ + z_at[d], k))
    for d in NEAR_Y:
        first_b[d] = send(own_b, own_b, b1s.at[d], b1r.at[d], (y_at[d] * NZ + z, k))
    along_y(0)
    along_z(0)
    moves += [cp for d in LATE for cp in move(d)]
    for kind, e in (("b", 1), ("a", 1), ("b", 3), ("a", 7), ("a", 2), ("b", 2), ("a", 6), ("a", 3), ("a", 5), ("a", 4)):
        if kind == "a":
            first_a[e].wait_recv()
            along_y(e)
            to_mate(piece_a(0, e), 0, 0, e)
        else:
            first_b[e].wait_recv()
            along_z(e)
            to_mate(piece_b(e, 0), 1, e, 0)
    order = [(0, d, e) for d in NEAR_Y for e in range(NZ)] + [(1, e, d) for d in NEAR_Z for e in range(NY)]
    order.sort(key=lambda o: (min(o[1], NY - o[1]) + min(o[2], NZ - o[2])))
    for n, dy, dz in order:
        if n == 0:
            out_a[dy, dz].wait_recv()
            to_mate(piece_a(dy, dz), 0, dy, dz)
        else:
            out_b[dz, dy].wait_recv()
            to_mate(piece_b(dy, dz), 1, dy, dz)
    for group in (first_a, first_b, out_a, out_b):
        for cp in group.values():
            cp.wait_send()
    keep.wait()
    keep2.wait()
    for cp in moves + pair:
        cp.wait()


def exchange_call(ow, ti, of, ac, va, vr, lm, st):
    dma = pltpu.SemaphoreType.DMA
    row = pltpu.VMEM((NC, 1, 128), F32)
    irow = pltpu.VMEM((NC, 1, 128), I32)
    return pl.pallas_call(
        exchange_kernel,
        out_shape=(
            jax.ShapeDtypeStruct((NY, NZ, ROWS, 128), F32),
            jax.ShapeDtypeStruct((NK, 8, CELLS), F32),
            jax.ShapeDtypeStruct((NK, 8, 1024), F32),
        ),
        in_specs=[pl.BlockSpec(memory_space=pltpu.HBM)] * 8,
        out_specs=(vm(), hbm(), hbm()),
        scratch_shapes=[
            pltpu.VMEM((NB, 32), I32),
            pltpu.VMEM((NB, 32), I32),
            pltpu.VMEM((NB, 4, 32), I32),
            pltpu.VMEM((NB, 32), I32),
            pltpu.VMEM((NB, 32), F32),
            pltpu.VMEM((NB, 32), F32),
            pltpu.VMEM((NT, NB, 8), I32),
            dma((7,)),
            pltpu.VMEM((MLOC, NK * CELLS), F32),
            pltpu.VMEM((NK * CELLS // 128, MLOC, 128), F32),
            pltpu.VMEM((8, 128), I32),
            pltpu.VMEM((8, 128), F32),
            pltpu.VMEM((8, 128), F32),
            irow, irow,
            pltpu.SMEM((NC, 1, 128), I32),
            pltpu.VMEM((NK, 8, 128), F32),
            pltpu.VMEM((128, 128), F32),
            row, row,
            pltpu.VMEM((NK, 16, 128), F32),
            pltpu.VMEM((NK, 8, 1024), F32),
            dma(()), dma(()), dma(()),
            dma((NC,)), dma((NC,)), dma((NK,)), dma((NK,)),
            dma((NC,)), dma((NC,)), dma((NK,)), dma((NK,)),
            dma((NZ,)), dma((NZ,)), dma((NY,)), dma((NY,)),
            dma((NY, NZ)), dma((NY, NZ)), dma((NZ, NY)), dma((NZ, NY)),
            dma((2, NY, NZ)), dma((2, NY, NZ)),
            dma((NK,)), dma((NK,)), dma((NK,)), dma((NK,)), dma(()),
        ],
        compiler_params=pltpu.CompilerParams(collective_id=0, has_side_effects=True, vmem_limit_bytes=52_000_000),
        name="exchange",
    )(ow, ti, of, ac, va, vr, lm, st)


MAPS = NT * M
WIDE = NB * 1024 + MAPS
CH = 1024


def mask_row(e):
    k, x = divmod(e, 3)
    return HALF * (k // 4) + 40 + 8 * (k % 4 // 2) + 3 * (k % 2) + x


VALUE_ROWS = (46, 47, 54)


def window_kernel(g_ref, s_ref, s2_ref, mk_ref, out, zz, mask, val, pp, pt, dh, dl, th, tl, sp, tp, out_ref, osem):
    lane_group = iota((ROWS, 128), 1) // 32

    def assemble(blk, _):
        parts = [g_ref[4 * blk + u] for u in range(4)]
        for b in range(NB):
            v = parts[3]
            for u in range(3):
                v = jnp.where(lane_group == (b + u) % 4, parts[u], v)
            lanes = pl.ds(pl.multiple_of(b * 1024 + blk * 128, 128), 128)
            for h in range(2):
                zz[32 * h : 32 * h + 32, lanes] = v[HALF * h : HALF * h + 32]
                zz[64 + 8 * h : 72 + 8 * h, lanes] = v[HALF * h + 32 : HALF * h + 40]
            for e in range(8 * b):
                r = mask_row(e)
                mask[e : e + 1, lanes] = v[r : r + 1]
            for j, r in enumerate(VALUE_ROWS):
                val[j : j + 1, lanes] = v[r : r + 1]
        return 0

    lax.fori_loop(0, 8, assemble, 0)
    unit = lax.rem(iota((M, MAPS), 1), M) == iota((M, MAPS), 0)
    zz[:, NB * 1024 :] = jnp.where(unit, 1.0, 0.0)
    grow = jnp.where(iota((8, MAPS), 0) == iota((8, MAPS), 1) // M, 1.0, 0.0)
    for b in range(NB):
        mask[8 * b : 8 * b + 8, NB * 1024 :] = mm(mk_ref[:, b, :].astype(F32), grow, TN)

    for b in range(NB):
        lanes = slice(b * 1024, b * 1024 + 1024)
        prior = zz[:, lanes]
        accepted = val[0:1, lanes]
        observed = val[1:2, lanes]
        noise = val[2:3, lanes]
        mean = jnp.sum(prior, axis=0, keepdims=True) / M
        dev = prior - mean
        var = jnp.sum(dev * dev, axis=0, keepdims=True) / (M - 1) + epsilon
        den = var + noise
        shift = var / den * (observed - mean)
        factor = jnp.sqrt(noise / den) - 1.0
        inc = accepted * shift + (accepted * factor) * dev
        scl = dev * (1.0 / ((M - 1) * var))
        ih, il = split(inc)
        sh, sl = split(scl)
        for q in range(8):
            w = slice(128 * q, 128 * q + 128)
            left = jnp.concatenate([ih[:, w], il[:, w]], axis=1)
            right = jnp.concatenate([sh[:, w], sh[:, w]], axis=1)
            prod = mm(left, right, NT_) + mm(ih[:, w], sl[:, w], NT_)
            pp[b % 2, :, 80 * q : 80 * q + 80] = prod
        ph, plo = split(pp[b % 2])
        pt[b, 0:M, :] = ph
        pt[b, M : 2 * M, :] = plo

        def change(at, wide, dh, dl, b=b):
            v = zz[:, at]
            d = v - jnp.sum(v, axis=0, keepdims=True) * (1.0 / M)
            hi, lo = split(d)
            for q in range(8):
                w = jnp.broadcast_to(mask[8 * b + q : 8 * b + q + 1, at], (16, wide)).astype(BF)
                for g in range(5):
                    rr = slice(80 * q + 16 * g, 80 * q + 16 * g + 16)
                    dh[rr, :] = hi[16 * g : 16 * g + 16] * w
                    dl[rr, :] = lo[16 * g : 16 * g + 16] * w
            both = mm(pt[b], dh[...], NN)
            rest = mm(pt[b, 0:M, :], dl[...], NN)
            zz[:, at] = v + (both[0:M] + (both[M : 2 * M] + rest))

        def update(i, _):
            change(pl.ds(pl.multiple_of((b + 1) * 1024 + i * CH, CH), CH), CH, dh, dl)
            return 0

        lax.fori_loop(0, (NB - 1 - b) * 1024 // CH, update, 0)
        change(slice(NB * 1024, WIDE), MAPS, th, tl)

    true = iota((M, M), 0)
    tk = true // MLOC
    ti = lax.rem(true, MLOC)
    place = jnp.where(ti < 8, 8 * tk + ti, 64 + 2 * tk + ti - 8)
    perm = jnp.where(iota((M, M), 1) == place, 1.0, 0.0).astype(BF)
    whole, part = split(zz[:, NB * 1024 :])
    tp[0:M, :] = mm(perm, whole, NN).astype(BF)
    tp[M : 2 * M, :] = mm(perm, part, NN).astype(BF)
    puts = []
    for t in range(NT):
        at = slice(TILE * t, TILE * t + TILE)
        for kk in range(NK):
            sp[t % 2, 8 * kk : 8 * kk + 8, :] = s_ref[kk, :, at]
            sp[t % 2, 64 + 2 * kk : 66 + 2 * kk, :] = s2_ref[
                kk, 2 * (t // 2) : 2 * (t // 2) + 2, TILE * (t % 2) : TILE * (t % 2) + TILE
            ]
        hi, lo = split(sp[t % 2])
        maps = tp[:, M * t : M * t + M]
        both = mm(maps, hi, NN)
        rest = mm(maps[0:M], lo, NN)
        out_ref[:, at] = both[0:M] + (both[M : 2 * M] + rest)
        puts.append(pltpu.make_async_copy(out_ref.at[:, at], out.at[:, at], osem.at[t]))
        puts[-1].start()
    for cp in puts:
        cp.wait()


def window_call(g, s, s2, mk):
    return pl.pallas_call(
        window_kernel,
        out_shape=jax.ShapeDtypeStruct((M, CELLS), F32),
        in_specs=[vm()] * 4,
        out_specs=hbm(),
        scratch_shapes=[
            pltpu.VMEM((M, WIDE), F32),
            pltpu.VMEM((32, WIDE), F32),
            pltpu.VMEM((8, NB * 1024), F32),
            pltpu.VMEM((2, M, 640), F32),
            pltpu.VMEM((NB, 2 * M, 640), BF),
            pltpu.VMEM((640, CH), BF),
            pltpu.VMEM((640, CH), BF),
            pltpu.VMEM((640, MAPS), BF),
            pltpu.VMEM((640, MAPS), BF),
            pltpu.VMEM((2, M, TILE), F32),
            pltpu.VMEM((2 * M, MAPS), BF),
            pltpu.VMEM((M, CELLS), F32),
            pltpu.SemaphoreType.DMA((NT,)),
        ],
        compiler_params=pltpu.CompilerParams(vmem_limit_bytes=24 << 20),
        name="window",
    )(g, s, s2, mk)


def local(state, obs_value, obs_var, owner, tile_of, offsets, accept, loc_mask):
    places = jnp.transpose(offsets, (0, 2, 1))
    given = (owner[:, :, 0], tile_of, places, accept, obs_value, obs_var, loc_mask, state)
    g, s, s2 = exchange_call(*(pltpu.with_memory_space_constraint(x, pltpu.HBM) for x in given))
    return window_call(g.reshape(NC, ROWS, 128), s, s2, loc_mask)


def solution(mesh):
    return jax.shard_map(
        local,
        mesh=mesh,
        in_specs=(
            P("mem", "cols"),
            P(None, "cols"),
            P(None, "cols"),
            P(None, "cols", None),
            P(None, "cols"),
            P(None, "cols", None),
            P(None, "cols"),
            P(("cols", "mem"), None, None),
        ),
        out_specs=P(None, ("cols", "mem")),
        check_vma=False,
    )
```

```python
import jax
import jax.numpy as jnp
from jax import lax
from jax.experimental import pallas as pl
from jax.experimental.pallas import tpu as pltpu
from jax.sharding import PartitionSpec as P

epsilon = 1e-05
MESH = pl.DeviceIdType.MESH
F32 = jnp.float32
BF = jnp.bfloat16
I32 = jnp.int32

NB = 4
NC = 32
NK = 8
MLOC = 10
M = 80
NY = 4
NZ = 8
TILE = 512
NT = 8
CELLS = 4096
RA = 40
RB = 16
HALF = RA + RB
ROWS = 2 * HALF


def vm():
    return pl.BlockSpec(memory_space=pltpu.VMEM)


def sm():
    return pl.BlockSpec(memory_space=pltpu.SMEM)


def hbm():
    return pl.BlockSpec(memory_space=pl.ANY)


def iota(shape, axis):
    return lax.broadcasted_iota(I32, shape, axis)


def split(v):
    hi = v.astype(BF)
    lo = (v - hi.astype(F32)).astype(BF)
    return hi, lo


def mm(a, b, dims):
    return lax.dot_general(a, b, (dims, ((), ())), preferred_element_type=F32)


NN = ((1,), (0,))
NT_ = ((1,), (1,))
TN = ((0,), (0,))
def send(src, dst, ssem, rsem, dev):
    cp = pltpu.make_async_remote_copy(
        src_ref=src, dst_ref=dst, send_sem=ssem, recv_sem=rsem, device_id=dev, device_id_type=MESH
    )
    cp.start()
    return cp


FAR = sorted(
    ((dy, dz) for dy in range(NY) for dz in range(NZ) if dy + dz > 0),
    key=lambda o: -(min(o[0], NY - o[0]) + min(o[1], NZ - o[1])),
)
FAR_K = (4, 3, 5, 2, 6, 1, 7)
NEAR_Y = (1, 3, 2)
NEAR_Z = (1, 7, 2, 6, 3, 5, 4)
EARLY = (4, 2, 7, 1)
LATE = (5, 3, 6)


def exchange_kernel(
    ow_in, ti_in, of_in, ac_in, va_in, vr_in, lm_in, st, g_ref, s_ref, s2_ref,
    ow, ti, of, ac, va, vr, lm, ins,
    stv, tiled, fi, fl, mv, mrow, rr, rsm, mks, xs, zrow, rz, blocks, tail,
    ls, own, cs, ms, mr, ks, kr, ss, rs, xss, xsr, a1s, a1r, b1s, b1r, a2s, a2r, b2s, b2r,
    pas, par, ts, tr, us, ur, own2,
):
    c = lax.axis_index("cols")
    k = lax.axis_index("mem")
    y = c // NZ
    z = lax.rem(c, NZ)
    core = lax.rem(k, 2)
    bar = pltpu.get_barrier_semaphore()
    cols = [(dy * NZ + dz, lax.rem(y + dy, NY) * NZ + lax.rem(z + dz, NZ)) for dy, dz in FAR]
    for d, p in cols:
        pl.semaphore_signal(bar, inc=1, device_id=(p, k), device_id_type=MESH)
    for d in FAR_K:
        pl.semaphore_signal(bar, inc=1, device_id=(c, lax.rem(k + d, NK)), device_id_type=MESH)
    small = [
        pltpu.make_async_copy(src, dst, ins.at[n])
        for n, (src, dst) in enumerate(
            ((ow_in, ow), (ti_in, ti), (of_in, of), (ac_in, ac), (va_in, va), (vr_in, vr), (lm_in, lm))
        )
    ]
    for cp in small:
        cp.start()
    load = pltpu.make_async_copy(st, stv, ls)
    load.start()
    for cp in small:
        cp.wait()
    mv[...] = jnp.zeros_like(mv)
    tiles = ti[...] * TILE
    cells = [tiles + of[:, p, :] for p in range(4)]
    places = [ow[...], cells[0] + (cells[1] << 15), cells[2] + (cells[3] << 15)]
    fields = [ac[...].astype(F32), va[...], vr[...]]
    for b in range(NB):
        at = slice(32 * b, 32 * b + 32)
        for f in range(3):
            fi[f : f + 1, at] = places[f][b : b + 1, :]
            fl[f : f + 1, at] = fields[f][b : b + 1, :]
        mv[:, 8 * b : 8 * b + 8] = lm[:, b, :].astype(F32)
    r128 = iota((128, 128), 0)
    c128 = iota((128, 128), 1)
    lane32 = iota((NC, 128), 1)
    within = lane32 & 31
    hoti = jnp.where(iota((NC, 128), 0) == fi[0:1, :], 1, 0)
    seen = hoti
    for h in (1, 2, 4, 8, 16):
        seen = seen + jnp.where(within >= h, pltpu.roll(seen, h, 1), 0)
    slots = jnp.zeros((NC, 128), I32)
    for r in range(2):
        for w in range(2):
            v = jnp.where((hoti == 1) & (seen == r + 1), fi[w + 1 : w + 2, :], 0)
            for h in (1, 2, 4, 8, 16):
                v = v + pltpu.roll(v, 128 - h, 1)
            for p, cell in ((2 * w, v & 32767), (2 * w + 1, (v >> 15) & 32767)):
                for f, word in ((p, cell >> 7), (p + 4, cell & 127)):
                    spot = 8 * r + f
                    word = word if spot == 0 else pltpu.roll(word, spot, 1)
                    slots = jnp.where(within == spot, word, slots)
    mrow[...] = slots.reshape(NC, 1, 128)
    hot = hoti.astype(F32)
    rank = jnp.sum((hoti * (seen - 1)).astype(F32), axis=0, keepdims=True)
    load.wait()
    for p in range(NK):
        for j in range(4):
            at = CELLS * p + 1024 * j
            tail[p, 2 * j : 2 * j + 2, :] = stv[8:10, at : at + 1024]
    pl.semaphore_wait(bar, NC - 1 + NK - 1)

    ask = []
    for d, p in cols:
        ask.append(send(mrow.at[p], rr.at[c], ms.at[d], mr.at[d], (p, k)))
    maps = []
    for d in FAR_K:
        maps.append(send(mv, mks.at[k], ks.at[d], kr.at[d], (c, lax.rem(k + d, NK))))
    rr[c] = mrow[c]
    mks[k] = mv[...]
    def move(d):
        p = lax.rem(k + d, NK)
        part = stv.at[0:8, pl.ds(pl.multiple_of(p * CELLS, CELLS), CELLS)]
        return [
            send(part, s_ref.at[k], ts.at[d], tr.at[d], (c, p)),
            send(tail.at[p], s2_ref.at[k], us.at[d], ur.at[d], (c, p)),
        ]

    moves = [cp for d in EARLY for cp in move(d)]
    keep = pltpu.make_async_copy(
        stv.at[0:8, pl.ds(pl.multiple_of(k * CELLS, CELLS), CELLS)], s_ref.at[k], own
    )
    keep.start()
    keep2 = pltpu.make_async_copy(tail.at[k], s2_ref.at[k], own2)
    keep2.start()
    for t in range(NK * CELLS // 128):
        tiled[t] = stv[:, 128 * t : 128 * t + 128]
    for cp in maps:
        cp.wait()
    pick = lax.rem(c128, 16) - 10
    chosen = jnp.where((pick >= 0) & (pick < 3) & (r128 == 3 * k + pick), 1.0, 0.0)
    table = mm(mks[...].reshape(64, 128).astype(BF), chosen.astype(BF), NN).astype(BF)
    for cp in ask:
        cp.wait()
    scal = pltpu.make_async_copy(rr, rsm, cs)
    scal.start()
    got = rr[...].reshape(NC, 128)
    extra = jnp.zeros((NC, 128), F32)
    for q in range(8):
        word = 32 * (q // 2) + 8 * (q % 2)
        tile = got[:, word : word + 1] >> 2
        at_tile = jnp.where(iota((NC, 64), 1) == tile, 1.0, 0.0).astype(BF)
        extra = jnp.where(lane32 // 16 == q, mm(at_tile, table, NN), extra)
    scal.wait()
    lane = iota((MLOC, 128), 1)

    def priors(i, accs):
        here = lane == i
        out = []
        for q in range(8):
            v = jnp.zeros((MLOC, 128), F32)
            word = 32 * (q // 2) + 8 * (q % 2)
            for p in range(4):
                hit = lane == rsm[i, 0, word + 4 + p]
                v = v + jnp.where(hit, tiled[rsm[i, 0, word + p]], 0.0)
            out.append(jnp.where(here, jnp.sum(v, axis=1, keepdims=True), accs[q]))
        return tuple(out)

    accs = lax.fori_loop(0, NC, priors, tuple(jnp.zeros((MLOC, 128), F32) for _ in range(8)), unroll=True)
    xs[...] = jnp.zeros_like(xs)
    for q in range(8):
        xs[16 * q : 16 * q + MLOC, :] = accs[q] * 0.25
    zr = jnp.transpose(xs[...])[:NC] + extra
    zrow[...] = zr.reshape(NC, 1, 128)
    back = []
    for d, p in cols:
        back.append(send(zrow.at[p], rz.at[c], ss.at[d], rs.at[d], (p, k)))
    rz[c] = zrow[c]
    for cp in back:
        cp.wait()
    full = lax.dot_general(
        rz[...].reshape(NC, 128), hot, (TN, ((), ())),
        precision=lax.Precision.HIGHEST, preferred_element_type=F32,
    )
    batch = iota((1, 128), 1) // 32
    blk = jnp.zeros((16, 128), F32)
    for q in range(8):
        mine = (batch == q // 2) & (rank == float(q % 2))
        blk = blk + jnp.where(mine, full[16 * q : 16 * q + 16, :], 0.0)
    row16 = iota((16, 128), 0)
    for j in range(3):
        blk = jnp.where(row16 == 13 + j, fl[j : j + 1, :], blk)
    turned = blk
    around = lax.rem(z, 4)
    for j in range(1, 4):
        turned = jnp.where(around == j, pltpu.roll(blk, 32 * j, 1), turned)
    blocks[k] = turned
    block = blocks.at[k]
    step = []
    for d in FAR_K:
        step.append(send(block, block, xss.at[d], xsr.at[d], (c, lax.rem(k + d, NK))))
    for cp in step:
        cp.wait()
    sub8 = iota((8, 128), 0)
    for h in range(2):
        tails = [blocks[4 * h + u, 8:16, :] for u in range(4)]
        for u in range(4):
            g_ref[y, z, HALF * h + 8 * u : HALF * h + 8 * u + 8, :] = blocks[4 * h + u, 0:8, :]
        last = tails[0]
        for u in range(1, 4):
            last = jnp.where(sub8 // 2 == u, pltpu.roll(tails[u], 2 * u, 0), last)
        g_ref[y, z, HALF * h + 32 : HALF * h + 40, :] = last
        low = jnp.where(sub8 < 3, pltpu.roll(tails[0], 6, 0), pltpu.roll(tails[1], 1, 0))
        low = jnp.where(sub8 >= 6, pltpu.roll(tails[0], 1, 0), low)
        high = jnp.where(sub8 < 3, pltpu.roll(tails[2], 6, 0), pltpu.roll(tails[3], 1, 0))
        high = jnp.where(sub8 >= 6, pltpu.roll(tails[2], 7, 0), high)
        g_ref[y, z, HALF * h + 40 : HALF * h + 48, :] = low
        g_ref[y, z, HALF * h + 48 : HALF * h + 56, :] = high
    ra = pl.multiple_of(HALF * core, 8)
    rb = pl.multiple_of(HALF * core + RA, 8)
    mate = (c, k + 1 - 2 * core)
    y_at = [lax.rem(y + d, NY) for d in range(NY)]
    z_at = [lax.rem(z + d, NZ) for d in range(NZ)]

    def piece_a(dy, dz):
        return g_ref.at[y_at[(-dy) % NY], z_at[(-dz) % NZ], pl.ds(ra, RA), :]

    def piece_b(dy, dz):
        return g_ref.at[y_at[(-dy) % NY], z_at[(-dz) % NZ], pl.ds(rb, RB), :]

    out_a = {}
    out_b = {}
    pair = []

    def along_y(e):
        piece = piece_a(0, e)
        for d in NEAR_Y:
            out_a[d, e] = send(piece, piece, a2s.at[d, e], a2r.at[d, e], (y_at[d] * NZ + z, k))

    def along_z(e):
        piece = piece_b(e, 0)
        for d in NEAR_Z:
            out_b[d, e] = send(piece, piece, b2s.at[d, e], b2r.at[d, e], (y * NZ + z_at[d], k))

    def to_mate(piece, n, dy, dz):
        pair.append(send(piece, piece, pas.at[n, dy, dz], par.at[n, dy, dz], mate))

    own_a = piece_a(0, 0)
    own_b = piece_b(0, 0)
    first_a = {}
    first_b = {}
    for d in NEAR_Z:
        first_a[d] = send(own_a, own_a, a1s.at[d], a1r.at[d], (y * NZ + z_at[d], k))
    for d in NEAR_Y:
        first_b[d] = send(own_b, own_b, b1s.at[d], b1r.at[d], (y_at[d] * NZ + z, k))
    along_y(0)
    along_z(0)
    moves += [cp for d in LATE for cp in move(d)]
    for kind, e in (("b", 1), ("a", 1), ("b", 3), ("a", 7), ("a", 2), ("b", 2), ("a", 6), ("a", 3), ("a", 5), ("a", 4)):
        if kind == "a":
            first_a[e].wait_recv()
            along_y(e)
            to_mate(piece_a(0, e), 0, 0, e)
        else:
            first_b[e].wait_recv()
            along_z(e)
            to_mate(piece_b(e, 0), 1, e, 0)
    order = [(0, d, e) for d in NEAR_Y for e in range(NZ)] + [(1, e, d) for d in NEAR_Z for e in range(NY)]
    order.sort(key=lambda o: (min(o[1], NY - o[1]) + min(o[2], NZ - o[2])))
    for n, dy, dz in order:
        if n == 0:
            out_a[dy, dz].wait_recv()
            to_mate(piece_a(dy, dz), 0, dy, dz)
        else:
            out_b[dz, dy].wait_recv()
            to_mate(piece_b(dy, dz), 1, dy, dz)
    for group in (first_a, first_b, out_a, out_b):
        for cp in group.values():
            cp.wait_send()
    keep.wait()
    keep2.wait()
    for cp in moves + pair:
        cp.wait()


def exchange_call(ow, ti, of, ac, va, vr, lm, st):
    dma = pltpu.SemaphoreType.DMA
    row = pltpu.VMEM((NC, 1, 128), F32)
    irow = pltpu.VMEM((NC, 1, 128), I32)
    return pl.pallas_call(
        exchange_kernel,
        out_shape=(
            jax.ShapeDtypeStruct((NY, NZ, ROWS, 128), F32),
            jax.ShapeDtypeStruct((NK, 8, CELLS), F32),
            jax.ShapeDtypeStruct((NK, 8, 1024), F32),
        ),
        in_specs=[pl.BlockSpec(memory_space=pltpu.HBM)] * 8,
        out_specs=(vm(), hbm(), hbm()),
        scratch_shapes=[
            pltpu.VMEM((NB, 32), I32),
            pltpu.VMEM((NB, 32), I32),
            pltpu.VMEM((NB, 4, 32), I32),
            pltpu.VMEM((NB, 32), I32),
            pltpu.VMEM((NB, 32), F32),
            pltpu.VMEM((NB, 32), F32),
            pltpu.VMEM((NT, NB, 8), I32),
            dma((7,)),
            pltpu.VMEM((MLOC, NK * CELLS), F32),
            pltpu.VMEM((NK * CELLS // 128, MLOC, 128), F32),
            pltpu.VMEM((8, 128), I32),
            pltpu.VMEM((8, 128), F32),
            pltpu.VMEM((8, 128), F32),
            irow, irow,
            pltpu.SMEM((NC, 1, 128), I32),
            pltpu.VMEM((NK, 8, 128), F32),
            pltpu.VMEM((128, 128), F32),
            row, row,
            pltpu.VMEM((NK, 16, 128), F32),
            pltpu.VMEM((NK, 8, 1024), F32),
            dma(()), dma(()), dma(()),
            dma((NC,)), dma((NC,)), dma((NK,)), dma((NK,)),
            dma((NC,)), dma((NC,)), dma((NK,)), dma((NK,)),
            dma((NZ,)), dma((NZ,)), dma((NY,)), dma((NY,)),
            dma((NY, NZ)), dma((NY, NZ)), dma((NZ, NY)), dma((NZ, NY)),
            dma((2, NY, NZ)), dma((2, NY, NZ)),
            dma((NK,)), dma((NK,)), dma((NK,)), dma((NK,)), dma(()),
        ],
        compiler_params=pltpu.CompilerParams(collective_id=0, has_side_effects=True, vmem_limit_bytes=52_000_000),
        name="exchange",
    )(ow, ti, of, ac, va, vr, lm, st)


MAPS = NT * M
WIDE = NB * 1024 + MAPS
CH = 1024


def mask_row(e):
    k, x = divmod(e, 3)
    return HALF * (k // 4) + 40 + 8 * (k % 4 // 2) + 3 * (k % 2) + x


VALUE_ROWS = (46, 47, 54)


def window_kernel(g_ref, s_ref, s2_ref, mk_ref, out, zz, mask, val, pp, pt, dh, dl, th, tl, sp, tp, out_ref, osem):
    lane_group = iota((ROWS, 128), 1) // 32

    def assemble(blk, _):
        parts = [g_ref[4 * blk + u] for u in range(4)]
        for b in range(NB):
            v = parts[3]
            for u in range(3):
                v = jnp.where(lane_group == (b + u) % 4, parts[u], v)
            lanes = pl.ds(pl.multiple_of(b * 1024 + blk * 128, 128), 128)
            for h in range(2):
                zz[32 * h : 32 * h + 32, lanes] = v[HALF * h : HALF * h + 32]
                zz[64 + 8 * h : 72 + 8 * h, lanes] = v[HALF * h + 32 : HALF * h + 40]
            for e in range(8 * b):
                r = mask_row(e)
                mask[e : e + 1, lanes] = v[r : r + 1]
            for j, r in enumerate(VALUE_ROWS):
                val[j : j + 1, lanes] = v[r : r + 1]
        return 0

    lax.fori_loop(0, 8, assemble, 0)
    unit = lax.rem(iota((M, MAPS), 1), M) == iota((M, MAPS), 0)
    zz[:, NB * 1024 :] = jnp.where(unit, 1.0, 0.0)
    grow = jnp.where(iota((8, MAPS), 0) == iota((8, MAPS), 1) // M, 1.0, 0.0)
    for b in range(NB):
        mask[8 * b : 8 * b + 8, NB * 1024 :] = mm(mk_ref[:, b, :].astype(F32), grow, TN)

    for b in range(NB):
        lanes = slice(b * 1024, b * 1024 + 1024)
        prior = zz[:, lanes]
        accepted = val[0:1, lanes]
        observed = val[1:2, lanes]
        noise = val[2:3, lanes]
        mean = jnp.sum(prior, axis=0, keepdims=True) / M
        dev = prior - mean
        var = jnp.sum(dev * dev, axis=0, keepdims=True) / (M - 1) + epsilon
        den = var + noise
        shift = var / den * (observed - mean)
        factor = jnp.sqrt(noise / den) - 1.0
        inc = accepted * shift + (accepted * factor) * dev
        scl = dev * (1.0 / ((M - 1) * var))
        ih, il = split(inc)
        sh, sl = split(scl)
        for q in range(8):
            w = slice(128 * q, 128 * q + 128)
            left = jnp.concatenate([ih[:, w], il[:, w]], axis=1)
            right = jnp.concatenate([sh[:, w], sh[:, w]], axis=1)
            prod = mm(left, right, NT_) + mm(ih[:, w], sl[:, w], NT_)
            pp[b % 2, :, 80 * q : 80 * q + 80] = prod
        ph, plo = split(pp[b % 2])
        pt[b, 0:M, :] = ph
        pt[b, M : 2 * M, :] = plo

        def change(at, wide, dh, dl, b=b):
            v = zz[:, at]
            d = v - jnp.sum(v, axis=0, keepdims=True) * (1.0 / M)
            hi, lo = split(d)
            for q in range(8):
                w = jnp.broadcast_to(mask[8 * b + q : 8 * b + q + 1, at], (16, wide)).astype(BF)
                for g in range(5):
                    rr = slice(80 * q + 16 * g, 80 * q + 16 * g + 16)
                    dh[rr, :] = hi[16 * g : 16 * g + 16] * w
                    dl[rr, :] = lo[16 * g : 16 * g + 16] * w
            both = mm(pt[b], dh[...], NN)
            rest = mm(pt[b, 0:M, :], dl[...], NN)
            zz[:, at] = v + (both[0:M] + (both[M : 2 * M] + rest))

        def update(i, _):
            change(pl.ds(pl.multiple_of((b + 1) * 1024 + i * CH, CH), CH), CH, dh, dl)
            return 0

        lax.fori_loop(0, (NB - 1 - b) * 1024 // CH, update, 0, unroll=True)
        change(slice(NB * 1024, WIDE), MAPS, th, tl)

    true = iota((M, M), 0)
    tk = true // MLOC
    ti = lax.rem(true, MLOC)
    place = jnp.where(ti < 8, 8 * tk + ti, 64 + 2 * tk + ti - 8)
    perm = jnp.where(iota((M, M), 1) == place, 1.0, 0.0).astype(BF)
    whole, part = split(zz[:, NB * 1024 :])
    tp[0:M, :] = mm(perm, whole, NN).astype(BF)
    tp[M : 2 * M, :] = mm(perm, part, NN).astype(BF)
    puts = []
    for t in range(NT):
        at = slice(TILE * t, TILE * t + TILE)
        for kk in range(NK):
            sp[t % 2, 8 * kk : 8 * kk + 8, :] = s_ref[kk, :, at]
            sp[t % 2, 64 + 2 * kk : 66 + 2 * kk, :] = s2_ref[
                kk, 2 * (t // 2) : 2 * (t // 2) + 2, TILE * (t % 2) : TILE * (t % 2) + TILE
            ]
        hi, lo = split(sp[t % 2])
        maps = tp[:, M * t : M * t + M]
        both = mm(maps, hi, NN)
        rest = mm(maps[0:M], lo, NN)
        out_ref[:, at] = both[0:M] + (both[M : 2 * M] + rest)
        puts.append(pltpu.make_async_copy(out_ref.at[:, at], out.at[:, at], osem.at[t]))
        puts[-1].start()
    for cp in puts:
        cp.wait()


def window_call(g, s, s2, mk):
    return pl.pallas_call(
        window_kernel,
        out_shape=jax.ShapeDtypeStruct((M, CELLS), F32),
        in_specs=[vm()] * 4,
        out_specs=hbm(),
        scratch_shapes=[
            pltpu.VMEM((M, WIDE), F32),
            pltpu.VMEM((32, WIDE), F32),
            pltpu.VMEM((8, NB * 1024), F32),
            pltpu.VMEM((2, M, 640), F32),
            pltpu.VMEM((NB, 2 * M, 640), BF),
            pltpu.VMEM((640, CH), BF),
            pltpu.VMEM((640, CH), BF),
            pltpu.VMEM((640, MAPS), BF),
            pltpu.VMEM((640, MAPS), BF),
            pltpu.VMEM((2, M, TILE), F32),
            pltpu.VMEM((2 * M, MAPS), BF),
            pltpu.VMEM((M, CELLS), F32),
            pltpu.SemaphoreType.DMA((NT,)),
        ],
        compiler_params=pltpu.CompilerParams(vmem_limit_bytes=24 << 20),
        name="window",
    )(g, s, s2, mk)


def local(state, obs_value, obs_var, owner, tile_of, offsets, accept, loc_mask):
    places = jnp.transpose(offsets, (0, 2, 1))
    given = (owner[:, :, 0], tile_of, places, accept, obs_value, obs_var, loc_mask, state)
    g, s, s2 = exchange_call(*(pltpu.with_memory_space_constraint(x, pltpu.HBM) for x in given))
    return window_call(g.reshape(NC, ROWS, 128), s, s2, loc_mask)


def solution(mesh):
    return jax.shard_map(
        local,
        mesh=mesh,
        in_specs=(
            P("mem", "cols"),
            P(None, "cols"),
            P(None, "cols"),
            P(None, "cols", None),
            P(None, "cols"),
            P(None, "cols", None),
            P(None, "cols"),
            P(("cols", "mem"), None, None),
        ),
        out_specs=P(None, ("cols", "mem")),
        check_vma=False,
    )
```
